256 devices in a mesh: ctx: 64 (over x, y_hi, z), ch: 4 (over y_lo, core).
Axes of the slice: x: 4, y: 4 (y_hi: 2, y_lo: 2; y = y_hi * 2 + y_lo), z: 8, core: 2. Of those that a mesh axis runs over, the one named last changes fastest.
Arguments:
- inputs: bfloat16 [32, 16, 8192], P(None, 'ch', 'ctx'), may hold values from -0.0390625 to 0.0390625
- short_filter: float32 [3, 32, 16], P(None, None, 'ch'), may hold values from -3.5 to 3.5
- long_filter: bfloat16 [32, 8192], P(None, 'ctx'), may hold values from -0.15625 to 0.15625
- grad_out: bfloat16 [32, 16, 8192], P(None, 'ch', 'ctx'), may hold values from -6 to 6
Outputs:
- grad_in: bfloat16 [32, 16, 8192], P(None, 'ch', 'ctx')
- grad_long: float32 [32, 8192], P(None, 'ctx')
- grad_short: float32 [3, 32, 16], P(None, None, 'ch')
The draws below stay inside these ranges and needn't reach their ends.
All inputs are finite; a program needn't handle non-finite values.
Results may differ from the reference program's by a relative error of at most 0.0031.
Values may be sent and summed in bfloat16 or wider, within the bound.
A program may use at most 128 MiB of HBM per device.

```python
import jax
import jax.numpy as jnp

FG = 32
GS = 16
KS = 3
TOKENS = 8192


def block_levels(rng, shape, pieces, least, top_value):
    level = 1.0
    for axis_at, blocks in pieces:
        heights = jax.random.uniform(jax.random.fold_in(jax.random.fold_in(rng, 6), axis_at), (blocks,), jnp.float32, least / len(pieces), top_value / len(pieces))
        level = level * jnp.repeat(jnp.exp(heights), shape[axis_at] // blocks).reshape((-1,) + (1,) * (len(shape) - 1 - axis_at))
    return level


def centred(stream_key, dims, deviation, most, pieces=(), kind=jnp.bfloat16):
    array = deviation * jax.random.normal(stream_key, dims, jnp.float32)
    if pieces:
        array = array * block_levels(stream_key, dims, pieces, -0.22, 0.18)
    return jnp.clip(array, -most, most).astype(kind)


def setup_inputs(seed: int = 0) -> dict:
    streams_of = jax.random.split(jax.random.key(seed), 5)
    return {
        "inputs": centred(streams_of[0], (FG, GS, TOKENS), ((GS * TOKENS) ** -0.5), 0.0390625, ((1, 4), (2, 64))),
        "short_filter": centred(streams_of[1], (KS, FG, GS), KS ** -0.5, 3.5, ((2, 4),), jnp.float32),
        "long_filter": centred(streams_of[2], (FG, TOKENS), (TOKENS ** -0.5), 0.15625, ((1, 64),)),
        "grad_out": centred(streams_of[3], (FG, GS, TOKENS), 1.0, 6.0, ((1, 4), (2, 64))),
    }


def shifted(values, lag):
    padded = jnp.pad(values, ((0, 0), (0, 0), (lag, 0)))
    return padded[:, :, :TOKENS]


def reference(inputs, short_filter, long_filter, grad_out):
    xf = inputs.astype(jnp.float32)
    hidden = sum(short_filter[offset][:, :, None] * shifted(xf, offset) for offset in range(KS))
    hidden = hidden.astype(jnp.bfloat16)
    length = 2 * TOKENS
    spec_grad = jnp.fft.rfft(grad_out.astype(jnp.float32), n=length, axis=-1)
    spec_filter = jnp.fft.rfft(long_filter.astype(jnp.float32), n=length, axis=-1)
    grad_hidden = jnp.fft.irfft(jnp.conj(spec_filter)[:, None, :] * spec_grad, n=length, axis=-1)[:, :, :TOKENS]
    spec_hidden = jnp.fft.rfft(hidden.astype(jnp.float32), n=length, axis=-1)
    grad_long = jnp.fft.irfft(jnp.sum(spec_grad * jnp.conj(spec_hidden), axis=1), n=length, axis=-1)[:, :TOKENS]
    grad_pad = jnp.pad(grad_hidden, ((0, 0), (0, 0), (0, KS)))
    grad_in = sum(short_filter[offset][:, :, None] * grad_pad[:, :, offset:offset + TOKENS] for offset in range(KS))
    grad_short = jnp.stack([jnp.sum(grad_hidden * shifted(xf, offset), axis=2) for offset in range(KS)])
    return grad_in.astype(jnp.bfloat16), grad_long.astype(jnp.float32), grad_short.astype(jnp.float32)
```

```python
import jax
import jax.numpy as jnp
from jax import lax
from jax.sharding import PartitionSpec as P


def delayed(values, by, length):
    return jnp.pad(values, ((0, 0), (by, 0)))[:, :length]


def toeplitz_blocks(sources, block_len):
    count, total_len = sources.shape
    block_count = total_len // block_len
    blocks = sources.reshape(count, block_count, block_len)
    padded = jnp.pad(blocks, ((0, 0), (1, 1), (0, 0)))
    pairs = jnp.concatenate([padded[:, :-1], padded[:, 1:]], axis=2)
    shape = (2 * block_len, block_len, block_len)
    at = lax.broadcasted_iota(jnp.int32, shape, 0)
    col = lax.broadcasted_iota(jnp.int32, shape, 1)
    row = lax.broadcasted_iota(jnp.int32, shape, 2)
    one_hot = (at == block_len + col - row).astype(sources.dtype).reshape(2 * block_len, -1)
    kernel = jnp.dot(
        pairs.reshape(-1, 2 * block_len), one_hot, preferred_element_type=sources.dtype
    )
    return kernel.reshape(count, block_count + 1, block_len, block_len)


def correlate(lhs, kernel, block_count):
    return lax.conv_general_dilated(
        lhs,
        kernel,
        window_strides=(1,),
        padding=((0, block_count),),
        dimension_numbers=("NWC", "WIO", "NWC"),
        preferred_element_type=jnp.float32,
    )


def per_device(inputs, short_filter, long_filter, grad_out):
    tap_count = short_filter.shape[0]
    filter_count, chan_count, shard_len = inputs.shape
    ctx_count = lax.axis_size("ctx")
    my_index = lax.axis_index("ctx")
    total_len = shard_len * ctx_count
    per_dev = filter_count * chan_count // ctx_count
    per_filter = chan_count // per_dev
    block_len = 128
    block_count = total_len // block_len

    send = jnp.concatenate(
        [
            grad_out.reshape(ctx_count, per_dev, shard_len),
            inputs.reshape(ctx_count, per_dev, shard_len),
            jnp.repeat(long_filter, per_filter, axis=0)[:, None, :],
        ],
        axis=1,
    )
    recv = lax.all_to_all(send, "ctx", 0, 0, tiled=True)
    seqs = recv.transpose(1, 0, 2).reshape(2 * per_dev + 1, total_len)
    grad_seq = seqs[:per_dev]
    in_seq = seqs[per_dev : 2 * per_dev].astype(jnp.float32)
    filt_seq = seqs[2 * per_dev :]
    taps = short_filter.reshape(tap_count, ctx_count, per_dev)
    taps = lax.dynamic_index_in_dim(taps, my_index, axis=1, keepdims=False)

    hidden = sum(
        (taps[offset][:, None] * delayed(in_seq, offset, total_len) for offset in range(tap_count))
    )
    hidden = hidden.astype(jnp.bfloat16)

    kernels = toeplitz_blocks(jnp.concatenate([filt_seq, hidden], axis=0), block_len)
    grad_blocks = grad_seq.reshape(per_dev, block_count, block_len)
    grad_hidden = correlate(grad_blocks, kernels[0], block_count).reshape(per_dev, total_len)
    merged = grad_blocks.transpose(1, 0, 2).reshape(1, block_count, per_dev * block_len)
    hidden_kernel = kernels[1:].transpose(1, 0, 2, 3).reshape(
        block_count + 1, per_dev * block_len, block_len
    )
    grad_long = correlate(merged, hidden_kernel, block_count).reshape(total_len)

    padded_grad = jnp.pad(grad_hidden, ((0, 0), (0, tap_count - 1)))
    grad_in = sum(
        (
            taps[offset][:, None] * padded_grad[:, offset : offset + total_len]
            for offset in range(tap_count)
        )
    )
    grad_in = grad_in.astype(jnp.bfloat16)
    grad_short = jnp.stack(
        [
            jnp.sum(grad_hidden * delayed(in_seq, offset, total_len), axis=1)
            for offset in range(tap_count)
        ]
    )

    short_row = jnp.pad(
        grad_short.reshape(1, tap_count * per_dev),
        ((0, 0), (0, shard_len - tap_count * per_dev)),
    )
    back = jnp.concatenate(
        [
            grad_in.astype(jnp.float32).reshape(per_dev, ctx_count, shard_len).transpose(1, 0, 2),
            grad_long.reshape(ctx_count, 1, shard_len),
            jnp.broadcast_to(short_row[None], (ctx_count, 1, shard_len)),
        ],
        axis=1,
    )
    got = lax.all_to_all(back, "ctx", 0, 0, tiled=True)
    grad_in_out = got[:, :per_dev].reshape(filter_count, chan_count, shard_len)
    grad_in_out = grad_in_out.astype(jnp.bfloat16)
    long_part = got[:, per_dev].reshape(filter_count, per_filter, shard_len).sum(axis=1)
    grad_long_out = lax.psum(long_part, "ch")
    short_all = got[:, per_dev + 1, : tap_count * per_dev].reshape(ctx_count, tap_count, per_dev)
    grad_short_out = short_all.transpose(1, 0, 2).reshape(tap_count, filter_count, chan_count)
    return (grad_in_out, grad_long_out, grad_short_out)


def solution(mesh):
    in_specs = (P(None, "ch", "ctx"), P(None, None, "ch"), P(None, "ctx"), P(None, "ch", "ctx"))
    out_specs = (P(None, "ch", "ctx"), P(None, "ctx"), P(None, None, "ch"))
    return jax.shard_map(
        per_device, mesh=mesh, in_specs=in_specs, out_specs=out_specs, check_vma=False
    )
```

```python
import jax
import jax.numpy as jnp
from jax import lax
from jax.sharding import PartitionSpec as P


def delayed(values, by, length):
    return jnp.pad(values, ((0, 0), (by, 0)))[:, :length]


def toeplitz_blocks(sources, block_len):
    count, total_len = sources.shape
    block_count = total_len // block_len
    blocks = sources.reshape(count, block_count, block_len)
    padded = jnp.pad(blocks, ((0, 0), (1, 1), (0, 0)))
    pairs = jnp.concatenate([padded[:, :-1], padded[:, 1:]], axis=2)
    shape = (2 * block_len, block_len, block_len)
    at = lax.broadcasted_iota(jnp.int32, shape, 0)
    col = lax.broadcasted_iota(jnp.int32, shape, 1)
    row = lax.broadcasted_iota(jnp.int32, shape, 2)
    one_hot = (at == block_len + col - row).astype(sources.dtype).reshape(2 * block_len, -1)
    kernel = jnp.dot(
        pairs.reshape(-1, 2 * block_len), one_hot, preferred_element_type=sources.dtype
    )
    return kernel.reshape(count, block_count + 1, block_len, block_len)


def per_device(inputs, short_filter, long_filter, grad_out):
    tap_count = short_filter.shape[0]
    filter_count, chan_count, shard_len = inputs.shape
    ctx_count = lax.axis_size("ctx")
    my_index = lax.axis_index("ctx")
    total_len = shard_len * ctx_count
    per_dev = filter_count * chan_count // ctx_count
    per_filter = chan_count // per_dev
    block_len = 128
    block_count = total_len // block_len

    send = jnp.concatenate(
        [
            grad_out.reshape(ctx_count, per_dev, shard_len),
            inputs.reshape(ctx_count, per_dev, shard_len),
            jnp.repeat(long_filter, per_filter, axis=0)[:, None, :],
        ],
        axis=1,
    )
    recv = lax.all_to_all(send, "ctx", 0, 0, tiled=True)
    seqs = recv.transpose(1, 0, 2).reshape(2 * per_dev + 1, total_len)
    grad_seq = seqs[:per_dev]
    in_seq = seqs[per_dev : 2 * per_dev].astype(jnp.float32)
    filt_seq = seqs[2 * per_dev :]
    taps = short_filter.reshape(tap_count, ctx_count, per_dev)
    taps = lax.dynamic_index_in_dim(taps, my_index, axis=1, keepdims=False)

    hidden = sum(
        (taps[offset][:, None] * delayed(in_seq, offset, total_len) for offset in range(tap_count))
    )
    hidden = hidden.astype(jnp.bfloat16)

    kernels = toeplitz_blocks(jnp.concatenate([filt_seq, hidden], axis=0), block_len)
    grad_blocks = jnp.pad(
        grad_seq.reshape(per_dev, block_count, block_len).transpose(1, 0, 2),
        ((0, block_count), (0, 0), (0, 0)),
    )
    hankel = jnp.stack(
        [grad_blocks[lag : lag + block_count] for lag in range(block_count + 1)], axis=2
    )
    window = (block_count + 1) * block_len
    grad_long = jnp.dot(
        hankel.reshape(block_count, per_dev * window),
        kernels[1:].reshape(per_dev * window, block_len),
        preferred_element_type=jnp.float32,
    )
    got_long = lax.all_to_all(
        grad_long.reshape(ctx_count, 1, shard_len), "ctx", 0, 0, tiled=True
    )
    long_part = got_long.reshape(filter_count, per_filter, shard_len).sum(axis=1)
    grad_long_out = lax.psum(long_part, "ch")

    grad_hidden = jnp.dot(
        hankel.reshape(block_count * per_dev, window),
        kernels[0].reshape(window, block_len),
        preferred_element_type=jnp.float32,
    )
    grad_hidden = grad_hidden.reshape(block_count, per_dev, block_len).transpose(1, 0, 2)
    grad_hidden = grad_hidden.reshape(per_dev, total_len)

    padded_grad = jnp.pad(grad_hidden, ((0, 0), (0, tap_count - 1)))
    grad_in = sum(
        (
            taps[offset][:, None] * padded_grad[:, offset : offset + total_len]
            for offset in range(tap_count)
        )
    )
    grad_in = grad_in.astype(jnp.bfloat16)
    grad_short = jnp.stack(
        [
            jnp.sum(grad_hidden * delayed(in_seq, offset, total_len), axis=1)
            for offset in range(tap_count)
        ]
    )

    short_row = jnp.pad(
        grad_short.reshape(1, tap_count * per_dev),
        ((0, 0), (0, shard_len - tap_count * per_dev)),
    )
    back = jnp.concatenate(
        [
            grad_in.astype(jnp.float32).reshape(per_dev, ctx_count, shard_len).transpose(1, 0, 2),
            jnp.broadcast_to(short_row[None], (ctx_count, 1, shard_len)),
        ],
        axis=1,
    )
    got = lax.all_to_all(back, "ctx", 0, 0, tiled=True)
    grad_in_out = got[:, :per_dev].reshape(filter_count, chan_count, shard_len)
    grad_in_out = grad_in_out.astype(jnp.bfloat16)
    short_all = got[:, per_dev, : tap_count * per_dev].reshape(ctx_count, tap_count, per_dev)
    grad_short_out = short_all.transpose(1, 0, 2).reshape(tap_count, filter_count, chan_count)
    return (grad_in_out, grad_long_out, grad_short_out)


def solution(mesh):
    in_specs = (P(None, "ch", "ctx"), P(None, None, "ch"), P(None, "ctx"), P(None, "ch", "ctx"))
    out_specs = (P(None, "ch", "ctx"), P(None, "ctx"), P(None, None, "ch"))
    return jax.shard_map(
        per_device, mesh=mesh, in_specs=in_specs, out_specs=out_specs, check_vma=False
    )
```

```python
import jax
import jax.numpy as jnp
from jax import lax
from jax.experimental import pallas as pl
from jax.experimental.pallas import tpu as pltpu
from jax.sharding import PartitionSpec as P


def delayed(values, by, length):
    return jnp.pad(values, ((0, 0), (by, 0)))[:, :length]


def conv_kernel(grad_ref, rev_ref, hidden_ref, long_ref, hankel, toeplitz):
    chans, _, block_len = grad_ref.shape
    block_count = hidden_ref.shape[1]
    sources, lags, _ = rev_ref.shape

    def fill_hankel(lag, carry):
        col = pl.multiple_of(lag * block_len, block_len)
        for g in range(chans):
            hankel[g, :, pl.ds(col, block_len)] = grad_ref[g, pl.ds(lag, block_count), :].astype(
                hankel.dtype
            )
        return carry

    lax.fori_loop(0, lags, fill_hankel, 0)

    def fill_toeplitz(lag, carry):
        row = pl.multiple_of(lag * block_len, block_len)
        for s in range(sources):
            line = rev_ref[s, pl.ds(lag, 1), :]
            tiled = jnp.broadcast_to(line, (block_len, 2 * block_len))
            skewed = pltpu.roll(tiled, block_len + 1, 1, stride=1, stride_axis=0)
            toeplitz[s, pl.ds(row, block_len), :] = skewed[:, :block_len].astype(toeplitz.dtype)
        return carry

    lax.fori_loop(0, lags, fill_toeplitz, 0)

    for g in range(chans):
        hidden_ref[g] = jnp.dot(hankel[g], toeplitz[0], preferred_element_type=jnp.float32)
    acc = jnp.dot(hankel[0], toeplitz[1], preferred_element_type=jnp.float32)
    for g in range(1, chans):
        acc = acc + jnp.dot(hankel[g], toeplitz[1 + g], preferred_element_type=jnp.float32)
    long_ref[...] = acc


def correlate_all(grad_seq, sources, block_len):
    chans, total_len = grad_seq.shape
    count = sources.shape[0]
    block_count = total_len // block_len
    grad_pad = jnp.pad(
        grad_seq.astype(jnp.float32).reshape(chans, block_count, block_len),
        ((0, 0), (0, block_count), (0, 0)),
    )
    blocks = sources.reshape(count, block_count, block_len)
    padded = jnp.pad(blocks, ((0, 0), (1, 1), (0, 0)))
    pairs = jnp.concatenate([padded[:, :-1], padded[:, 1:]], axis=2)
    rev = pairs[..., ::-1].astype(jnp.float32)
    lags = block_count + 1
    hidden, long = pl.pallas_call(
        conv_kernel,
        out_shape=(
            jax.ShapeDtypeStruct((chans, block_count, block_len), jnp.float32),
            jax.ShapeDtypeStruct((block_count, block_len), jnp.float32),
        ),
        scratch_shapes=[
            pltpu.VMEM((chans, block_count, lags * block_len), jnp.bfloat16),
            pltpu.VMEM((count, lags * block_len, block_len), jnp.bfloat16),
        ],
        compiler_params=pltpu.CompilerParams(vmem_limit_bytes=48 * 1024 * 1024),
    )(grad_pad, rev)
    return hidden.reshape(chans, total_len), long.reshape(total_len)


def per_device(inputs, short_filter, long_filter, grad_out):
    tap_count = short_filter.shape[0]
    filter_count, chan_count, shard_len = inputs.shape
    ctx_count = lax.axis_size("ctx")
    my_index = lax.axis_index("ctx")
    total_len = shard_len * ctx_count
    per_dev = filter_count * chan_count // ctx_count
    per_filter = chan_count // per_dev
    block_len = 128
    block_count = total_len // block_len

    send = jnp.concatenate(
        [
            grad_out.reshape(ctx_count, per_dev, shard_len),
            inputs.reshape(ctx_count, per_dev, shard_len),
            jnp.repeat(long_filter, per_filter, axis=0)[:, None, :],
        ],
        axis=1,
    )
    recv = lax.all_to_all(send, "ctx", 0, 0, tiled=True)
    seqs = recv.transpose(1, 0, 2).reshape(2 * per_dev + 1, total_len)
    grad_seq = seqs[:per_dev]
    in_seq = seqs[per_dev : 2 * per_dev].astype(jnp.float32)
    filt_seq = seqs[2 * per_dev :]
    taps = short_filter.reshape(tap_count, ctx_count, per_dev)
    taps = lax.dynamic_index_in_dim(taps, my_index, axis=1, keepdims=False)

    hidden = sum(
        (taps[offset][:, None] * delayed(in_seq, offset, total_len) for offset in range(tap_count))
    )
    hidden = hidden.astype(jnp.bfloat16)

    grad_hidden, grad_long = correlate_all(
        grad_seq, jnp.concatenate([filt_seq, hidden], axis=0), block_len
    )

    padded_grad = jnp.pad(grad_hidden, ((0, 0), (0, tap_count - 1)))
    grad_in = sum(
        (
            taps[offset][:, None] * padded_grad[:, offset : offset + total_len]
            for offset in range(tap_count)
        )
    )
    grad_in = grad_in.astype(jnp.bfloat16)
    grad_short = jnp.stack(
        [
            jnp.sum(grad_hidden * delayed(in_seq, offset, total_len), axis=1)
            for offset in range(tap_count)
        ]
    )

    short_row = jnp.pad(
        grad_short.reshape(1, tap_count * per_dev),
        ((0, 0), (0, shard_len - tap_count * per_dev)),
    )
    back = jnp.concatenate(
        [
            grad_in.astype(jnp.float32).reshape(per_dev, ctx_count, shard_len).transpose(1, 0, 2),
            grad_long.reshape(ctx_count, 1, shard_len),
            jnp.broadcast_to(short_row[None], (ctx_count, 1, shard_len)),
        ],
        axis=1,
    )
    got = lax.all_to_all(back, "ctx", 0, 0, tiled=True)
    grad_in_out = got[:, :per_dev].reshape(filter_count, chan_count, shard_len)
    grad_in_out = grad_in_out.astype(jnp.bfloat16)
    long_part = got[:, per_dev].reshape(filter_count, per_filter, shard_len).sum(axis=1)
    grad_long_out = lax.psum(long_part, "ch")
    short_all = got[:, per_dev + 1, : tap_count * per_dev].reshape(ctx_count, tap_count, per_dev)
    grad_short_out = short_all.transpose(1, 0, 2).reshape(tap_count, filter_count, chan_count)
    return (grad_in_out, grad_long_out, grad_short_out)


def solution(mesh):
    in_specs = (P(None, "ch", "ctx"), P(None, None, "ch"), P(None, "ctx"), P(None, "ch", "ctx"))
    out_specs = (P(None, "ch", "ctx"), P(None, "ctx"), P(None, None, "ch"))
    return jax.shard_map(
        per_device, mesh=mesh, in_specs=in_specs, out_specs=out_specs, check_vma=False
    )
```

```python
import jax
import jax.numpy as jnp
from jax import lax
from jax.experimental import pallas as pl
from jax.experimental.pallas import tpu as pltpu
from jax.sharding import Mesh
from jax.sharding import PartitionSpec as P

INNER = "z"
OUTER = ("x", "yh")
CTX = OUTER + (INNER,)


def exchange(chunks):
    inner = lax.axis_size(INNER)
    rest = chunks.shape[1:]
    split = chunks.reshape((chunks.shape[0] // inner, inner) + rest)
    split = lax.all_to_all(split, INNER, 1, 1, tiled=True)
    split = lax.all_to_all(split, OUTER, 0, 0, tiled=True)
    return split.reshape(chunks.shape)


def delayed(values, by, length):
    return jnp.pad(values, ((0, 0), (by, 0)))[:, :length]


def conv_kernel(grad_ref, rev_ref, hidden_ref, long_ref, hankel, toeplitz):
    chans, _, block_len = grad_ref.shape
    block_count = hidden_ref.shape[1]
    sources, lags, _ = rev_ref.shape

    def fill_hankel(lag, carry):
        col = pl.multiple_of(lag * block_len, block_len)
        for g in range(chans):
            hankel[g, :, pl.ds(col, block_len)] = grad_ref[g, pl.ds(lag, block_count), :].astype(
                hankel.dtype
            )
        return carry

    lax.fori_loop(0, lags, fill_hankel, 0)

    def fill_toeplitz(lag, carry):
        row = pl.multiple_of(lag * block_len, block_len)
        for s in range(sources):
            line = rev_ref[s, pl.ds(lag, 1), :]
            tiled = jnp.broadcast_to(line, (block_len, 2 * block_len))
            skewed = pltpu.roll(tiled, block_len + 1, 1, stride=1, stride_axis=0)
            toeplitz[s, pl.ds(row, block_len), :] = skewed[:, :block_len].astype(toeplitz.dtype)
        return carry

    lax.fori_loop(0, lags, fill_toeplitz, 0)

    for g in range(chans):
        hidden_ref[g] = jnp.dot(hankel[g], toeplitz[0], preferred_element_type=jnp.float32)
    acc = jnp.dot(hankel[0], toeplitz[1], preferred_element_type=jnp.float32)
    for g in range(1, chans):
        acc = acc + jnp.dot(hankel[g], toeplitz[1 + g], preferred_element_type=jnp.float32)
    long_ref[...] = acc


def correlate_all(grad_seq, sources, block_len):
    chans, total_len = grad_seq.shape
    count = sources.shape[0]
    block_count = total_len // block_len
    grad_pad = jnp.pad(
        grad_seq.astype(jnp.float32).reshape(chans, block_count, block_len),
        ((0, 0), (0, block_count), (0, 0)),
    )
    blocks = sources.reshape(count, block_count, block_len)
    padded = jnp.pad(blocks, ((0, 0), (1, 1), (0, 0)))
    pairs = jnp.concatenate([padded[:, :-1], padded[:, 1:]], axis=2)
    rev = pairs[..., ::-1].astype(jnp.float32)
    lags = block_count + 1
    hidden, long = pl.pallas_call(
        conv_kernel,
        out_shape=(
            jax.ShapeDtypeStruct((chans, block_count, block_len), jnp.float32),
            jax.ShapeDtypeStruct((block_count, block_len), jnp.float32),
        ),
        scratch_shapes=[
            pltpu.VMEM((chans, block_count, lags * block_len), jnp.bfloat16),
            pltpu.VMEM((count, lags * block_len, block_len), jnp.bfloat16),
        ],
        compiler_params=pltpu.CompilerParams(vmem_limit_bytes=48 * 1024 * 1024),
    )(grad_pad, rev)
    return hidden.reshape(chans, total_len), long.reshape(total_len)


def per_device(inputs, short_filter, long_filter, grad_out):
    tap_count = short_filter.shape[0]
    filter_count, chan_count, shard_len = inputs.shape
    ctx_count = lax.axis_size(CTX)
    my_index = lax.axis_index(CTX)
    total_len = shard_len * ctx_count
    per_dev = filter_count * chan_count // ctx_count
    per_filter = chan_count // per_dev
    block_len = 128
    block_count = total_len // block_len

    send = jnp.concatenate(
        [
            grad_out.reshape(ctx_count, per_dev, shard_len),
            inputs.reshape(ctx_count, per_dev, shard_len),
            jnp.repeat(long_filter, per_filter, axis=0)[:, None, :],
        ],
        axis=1,
    )
    recv = exchange(send)
    seqs = recv.transpose(1, 0, 2).reshape(2 * per_dev + 1, total_len)
    grad_seq = seqs[:per_dev]
    in_seq = seqs[per_dev : 2 * per_dev].astype(jnp.float32)
    filt_seq = seqs[2 * per_dev :]
    taps = short_filter.reshape(tap_count, ctx_count, per_dev)
    taps = lax.dynamic_index_in_dim(taps, my_index, axis=1, keepdims=False)

    hidden = sum(
        (taps[offset][:, None] * delayed(in_seq, offset, total_len) for offset in range(tap_count))
    )
    hidden = hidden.astype(jnp.bfloat16)

    grad_hidden, grad_long = correlate_all(
        grad_seq, jnp.concatenate([filt_seq, hidden], axis=0), block_len
    )

    padded_grad = jnp.pad(grad_hidden, ((0, 0), (0, tap_count - 1)))
    grad_in = sum(
        (
            taps[offset][:, None] * padded_grad[:, offset : offset + total_len]
            for offset in range(tap_count)
        )
    )
    grad_in = grad_in.astype(jnp.bfloat16)
    grad_short = jnp.stack(
        [
            jnp.sum(grad_hidden * delayed(in_seq, offset, total_len), axis=1)
            for offset in range(tap_count)
        ]
    )

    short_row = jnp.pad(
        grad_short.reshape(1, tap_count * per_dev),
        ((0, 0), (0, shard_len - tap_count * per_dev)),
    )
    back = jnp.concatenate(
        [
            grad_in.astype(jnp.float32).reshape(per_dev, ctx_count, shard_len).transpose(1, 0, 2),
            grad_long.reshape(ctx_count, 1, shard_len),
            jnp.broadcast_to(short_row[None], (ctx_count, 1, shard_len)),
        ],
        axis=1,
    )
    got = exchange(back)
    grad_in_out = got[:, :per_dev].reshape(filter_count, chan_count, shard_len)
    grad_in_out = grad_in_out.astype(jnp.bfloat16)
    long_part = got[:, per_dev].reshape(filter_count, per_filter, shard_len).sum(axis=1)
    grad_long_out = lax.psum(long_part, "ch")
    short_all = got[:, per_dev + 1, : tap_count * per_dev].reshape(ctx_count, tap_count, per_dev)
    grad_short_out = short_all.transpose(1, 0, 2).reshape(tap_count, filter_count, chan_count)
    return (grad_in_out, grad_long_out, grad_short_out)


def solution(mesh):
    ctx_count = mesh.shape["ctx"]
    inner = 8
    outer = ctx_count // inner
    devices = mesh.devices.reshape(outer // 2, 2, inner, mesh.shape["ch"])
    split_mesh = Mesh(devices, ("x", "yh", "z", "ch"))
    in_specs = (P(None, "ch", CTX), P(None, None, "ch"), P(None, CTX), P(None, "ch", CTX))
    out_specs = (P(None, "ch", CTX), P(None, CTX), P(None, None, "ch"))
    return jax.shard_map(
        per_device, mesh=split_mesh, in_specs=in_specs, out_specs=out_specs, check_vma=False
    )
```

```python
import jax
import jax.numpy as jnp
from jax import lax
from jax.experimental import pallas as pl
from jax.experimental.pallas import tpu as pltpu
from jax.sharding import PartitionSpec as P


def delayed(values, by, length):
    return jnp.pad(values, ((0, 0), (by, 0)))[:, :length]


def conv_kernel(grad_ref, rev_ref, hidden_ref, long_ref, hankel, toeplitz):
    chans, _, block_len = grad_ref.shape
    block_count = hidden_ref.shape[1]
    sources, lags, _ = rev_ref.shape

    def fill_hankel(lag, carry):
        col = pl.multiple_of(lag * block_len, block_len)
        for g in range(chans):
            hankel[g, :, pl.ds(col, block_len)] = grad_ref[g, pl.ds(lag, block_count), :].astype(
                hankel.dtype
            )
        return carry

    lax.fori_loop(0, lags, fill_hankel, 0)

    def fill_toeplitz(lag, carry):
        row = pl.multiple_of(lag * block_len, block_len)
        for s in range(sources):
            line = rev_ref[s, pl.ds(lag, 1), :]
            tiled = jnp.broadcast_to(line, (block_len, 2 * block_len))
            skewed = pltpu.roll(tiled, block_len + 1, 1, stride=1, stride_axis=0)
            toeplitz[s, pl.ds(row, block_len), :] = skewed[:, :block_len].astype(toeplitz.dtype)
        return carry

    lax.fori_loop(0, lags, fill_toeplitz, 0)

    for g in range(chans):
        hidden_ref[g] = jnp.dot(hankel[g], toeplitz[0], preferred_element_type=jnp.float32)
    acc = jnp.dot(hankel[0], toeplitz[1], preferred_element_type=jnp.float32)
    for g in range(1, chans):
        acc = acc + jnp.dot(hankel[g], toeplitz[1 + g], preferred_element_type=jnp.float32)
    long_ref[...] = acc


def correlate_all(grad_seq, sources, block_len):
    chans, total_len = grad_seq.shape
    count = sources.shape[0]
    block_count = total_len // block_len
    grad_pad = jnp.pad(
        grad_seq.astype(jnp.float32).reshape(chans, block_count, block_len),
        ((0, 0), (0, block_count), (0, 0)),
    )
    blocks = sources.reshape(count, block_count, block_len)
    padded = jnp.pad(blocks, ((0, 0), (1, 1), (0, 0)))
    pairs = jnp.concatenate([padded[:, :-1], padded[:, 1:]], axis=2)
    rev = pairs[..., ::-1].astype(jnp.float32)
    lags = block_count + 1
    hidden, long = pl.pallas_call(
        conv_kernel,
        out_shape=(
            jax.ShapeDtypeStruct((chans, block_count, block_len), jnp.float32),
            jax.ShapeDtypeStruct((block_count, block_len), jnp.float32),
        ),
        scratch_shapes=[
            pltpu.VMEM((chans, block_count, lags * block_len), jnp.bfloat16),
            pltpu.VMEM((count, lags * block_len, block_len), jnp.bfloat16),
        ],
        compiler_params=pltpu.CompilerParams(vmem_limit_bytes=48 * 1024 * 1024),
    )(grad_pad, rev)
    return hidden.reshape(chans, total_len), long.reshape(total_len)


def swap_kernel(send_ref, out_ref, landed, local_sem, send_sem, recv_sem):
    count = send_ref.shape[0]
    me = lax.axis_index("ctx")
    mine = lax.axis_index("ch")
    barrier = pltpu.get_barrier_semaphore()
    for step in range(1, count):
        peer = lax.rem(me + step, count)
        pl.semaphore_signal(
            barrier, 1, device_id=(peer, mine), device_id_type=pl.DeviceIdType.MESH
        )
    pl.semaphore_wait(barrier, count - 1)
    local = pltpu.make_async_copy(send_ref.at[me], landed.at[me], local_sem)
    local.start()
    copies = []
    for step in range(1, count):
        peer = lax.rem(me + step, count)
        copy = pltpu.make_async_remote_copy(
            src_ref=send_ref.at[peer],
            dst_ref=landed.at[me],
            send_sem=send_sem.at[peer],
            recv_sem=recv_sem.at[me],
            device_id=(peer, mine),
            device_id_type=pl.DeviceIdType.MESH,
        )
        copy.start()
        copies.append(copy)
    local.wait()
    for copy in copies:
        copy.wait_send()
    for step in range(1, count):
        source = lax.rem(me + step, count)
        pltpu.make_async_remote_copy(
            src_ref=send_ref.at[source],
            dst_ref=landed.at[source],
            send_sem=send_sem.at[source],
            recv_sem=recv_sem.at[source],
            device_id=(source, mine),
            device_id_type=pl.DeviceIdType.MESH,
        ).wait_recv()
    out_ref[...] = landed[...]


def swap(chunks, collective_id):
    return pl.pallas_call(
        swap_kernel,
        out_shape=jax.ShapeDtypeStruct(chunks.shape, chunks.dtype),
        in_specs=[pl.BlockSpec(memory_space=pltpu.VMEM)],
        out_specs=pl.BlockSpec(memory_space=pltpu.VMEM),
        scratch_shapes=[
            pltpu.VMEM(chunks.shape, chunks.dtype),
            pltpu.SemaphoreType.DMA,
            pltpu.SemaphoreType.DMA((chunks.shape[0],)),
            pltpu.SemaphoreType.DMA((chunks.shape[0],)),
        ],
        compiler_params=pltpu.CompilerParams(collective_id=collective_id, has_side_effects=True),
    )(chunks)


def per_device(inputs, short_filter, long_filter, grad_out):
    tap_count = short_filter.shape[0]
    filter_count, chan_count, shard_len = inputs.shape
    ctx_count = lax.axis_size("ctx")
    my_index = lax.axis_index("ctx")
    total_len = shard_len * ctx_count
    per_dev = filter_count * chan_count // ctx_count
    per_filter = chan_count // per_dev
    block_len = 128
    block_count = total_len // block_len

    send = jnp.concatenate(
        [
            grad_out.reshape(ctx_count, per_dev, shard_len),
            inputs.reshape(ctx_count, per_dev, shard_len),
            jnp.repeat(long_filter, per_filter, axis=0)[:, None, :],
        ],
        axis=1,
    )
    recv = swap(send, 0)
    seqs = recv.transpose(1, 0, 2).reshape(2 * per_dev + 1, total_len)
    grad_seq = seqs[:per_dev]
    in_seq = seqs[per_dev : 2 * per_dev].astype(jnp.float32)
    filt_seq = seqs[2 * per_dev :]
    taps = short_filter.reshape(tap_count, ctx_count, per_dev)
    taps = lax.dynamic_index_in_dim(taps, my_index, axis=1, keepdims=False)

    hidden = sum(
        (taps[offset][:, None] * delayed(in_seq, offset, total_len) for offset in range(tap_count))
    )
    hidden = hidden.astype(jnp.bfloat16)

    grad_hidden, grad_long = correlate_all(
        grad_seq, jnp.concatenate([filt_seq, hidden], axis=0), block_len
    )

    padded_grad = jnp.pad(grad_hidden, ((0, 0), (0, tap_count - 1)))
    grad_in = sum(
        (
            taps[offset][:, None] * padded_grad[:, offset : offset + total_len]
            for offset in range(tap_count)
        )
    )
    grad_in = grad_in.astype(jnp.bfloat16)
    grad_short = jnp.stack(
        [
            jnp.sum(grad_hidden * delayed(in_seq, offset, total_len), axis=1)
            for offset in range(tap_count)
        ]
    )

    short_row = jnp.pad(
        grad_short.reshape(1, tap_count * per_dev),
        ((0, 0), (0, shard_len - tap_count * per_dev)),
    )
    back = jnp.concatenate(
        [
            grad_in.astype(jnp.float32).reshape(per_dev, ctx_count, shard_len).transpose(1, 0, 2),
            grad_long.reshape(ctx_count, 1, shard_len),
            jnp.broadcast_to(short_row[None], (ctx_count, 1, shard_len)),
        ],
        axis=1,
    )
    got = swap(back, 1)
    grad_in_out = got[:, :per_dev].reshape(filter_count, chan_count, shard_len)
    grad_in_out = grad_in_out.astype(jnp.bfloat16)
    long_part = got[:, per_dev].reshape(filter_count, per_filter, shard_len).sum(axis=1)
    grad_long_out = lax.psum(long_part, "ch")
    short_all = got[:, per_dev + 1, : tap_count * per_dev].reshape(ctx_count, tap_count, per_dev)
    grad_short_out = short_all.transpose(1, 0, 2).reshape(tap_count, filter_count, chan_count)
    return (grad_in_out, grad_long_out, grad_short_out)


def solution(mesh):
    in_specs = (P(None, "ch", "ctx"), P(None, None, "ch"), P(None, "ctx"), P(None, "ch", "ctx"))
    out_specs = (P(None, "ch", "ctx"), P(None, "ctx"), P(None, None, "ch"))
    return jax.shard_map(
        per_device, mesh=mesh, in_specs=in_specs, out_specs=out_specs, check_vma=False
    )
```

```python
import jax
import jax.numpy as jnp
from jax import lax
from jax.experimental import pallas as pl
from jax.experimental.pallas import tpu as pltpu
from jax.sharding import PartitionSpec as P


def delayed(values, by, length):
    return jnp.pad(values, ((0, 0), (by, 0)))[:, :length]


def conv_kernel(grad_ref, rev_ref, hidden_ref, long_ref, hankel, toeplitz):
    chans, _, block_len = grad_ref.shape
    block_count = hidden_ref.shape[1]
    sources, lags, _ = rev_ref.shape

    def fill_hankel(lag, carry):
        col = pl.multiple_of(lag * block_len, block_len)
        for g in range(chans):
            hankel[g, :, pl.ds(col, block_len)] = grad_ref[g, pl.ds(lag, block_count), :].astype(
                hankel.dtype
            )
        return carry

    lax.fori_loop(0, lags, fill_hankel, 0)

    def fill_toeplitz(lag, carry):
        row = pl.multiple_of(lag * block_len, block_len)
        for s in range(sources):
            line = rev_ref[s, pl.ds(lag, 1), :]
            tiled = jnp.broadcast_to(line, (block_len, 2 * block_len))
            skewed = pltpu.roll(tiled, block_len + 1, 1, stride=1, stride_axis=0)
            toeplitz[s, pl.ds(row, block_len), :] = skewed[:, :block_len].astype(toeplitz.dtype)
        return carry

    lax.fori_loop(0, lags, fill_toeplitz, 0)

    for g in range(chans):
        hidden_ref[g] = jnp.dot(hankel[g], toeplitz[0], preferred_element_type=jnp.float32)
    acc = jnp.dot(hankel[0], toeplitz[1], preferred_element_type=jnp.float32)
    for g in range(1, chans):
        acc = acc + jnp.dot(hankel[g], toeplitz[1 + g], preferred_element_type=jnp.float32)
    long_ref[...] = acc


def correlate_all(grad_seq, sources, block_len):
    chans, total_len = grad_seq.shape
    count = sources.shape[0]
    block_count = total_len // block_len
    grad_pad = jnp.pad(
        grad_seq.astype(jnp.float32).reshape(chans, block_count, block_len),
        ((0, 0), (0, block_count), (0, 0)),
    )
    blocks = sources.reshape(count, block_count, block_len)
    padded = jnp.pad(blocks, ((0, 0), (1, 1), (0, 0)))
    pairs = jnp.concatenate([padded[:, :-1], padded[:, 1:]], axis=2)
    rev = pairs[..., ::-1].astype(jnp.float32)
    lags = block_count + 1
    hidden, long = pl.pallas_call(
        conv_kernel,
        out_shape=(
            jax.ShapeDtypeStruct((chans, block_count, block_len), jnp.float32),
            jax.ShapeDtypeStruct((block_count, block_len), jnp.float32),
        ),
        scratch_shapes=[
            pltpu.VMEM((chans, block_count, lags * block_len), jnp.bfloat16),
            pltpu.VMEM((count, lags * block_len, block_len), jnp.bfloat16),
        ],
        compiler_params=pltpu.CompilerParams(vmem_limit_bytes=48 * 1024 * 1024),
    )(grad_pad, rev)
    return hidden.reshape(chans, total_len), long.reshape(total_len)


def swap_kernel(send_ref, out_ref, landed, local_sem, send_sem, recv_sem):
    count = send_ref.shape[0]
    me = lax.axis_index("ctx")
    mine = lax.axis_index("ch")
    barrier = pltpu.get_barrier_semaphore()
    for step in range(1, count):
        peer = lax.rem(me + step, count)
        pl.semaphore_signal(
            barrier, 1, device_id=(peer, mine), device_id_type=pl.DeviceIdType.MESH
        )
    pl.semaphore_wait(barrier, count - 1)
    local = pltpu.make_async_copy(send_ref.at[me], landed.at[me], local_sem)
    local.start()
    copies = []
    for step in range(1, count):
        peer = lax.rem(me + step, count)
        copy = pltpu.make_async_remote_copy(
            src_ref=send_ref.at[peer],
            dst_ref=landed.at[me],
            send_sem=send_sem.at[peer],
            recv_sem=recv_sem.at[me],
            device_id=(peer, mine),
            device_id_type=pl.DeviceIdType.MESH,
        )
        copy.start()
        copies.append(copy)
    local.wait()
    for copy in copies:
        copy.wait_send()
    for step in range(1, count):
        source = lax.rem(me + step, count)
        pltpu.make_async_remote_copy(
            src_ref=send_ref.at[source],
            dst_ref=landed.at[source],
            send_sem=send_sem.at[source],
            recv_sem=recv_sem.at[source],
            device_id=(source, mine),
            device_id_type=pl.DeviceIdType.MESH,
        ).wait_recv()
    out_ref[...] = landed[...]


def swap(chunks, collective_id):
    return pl.pallas_call(
        swap_kernel,
        out_shape=jax.ShapeDtypeStruct(chunks.shape, chunks.dtype),
        in_specs=[pl.BlockSpec(memory_space=pltpu.VMEM)],
        out_specs=pl.BlockSpec(memory_space=pltpu.VMEM),
        scratch_shapes=[
            pltpu.VMEM(chunks.shape, chunks.dtype),
            pltpu.SemaphoreType.DMA,
            pltpu.SemaphoreType.DMA((chunks.shape[0],)),
            pltpu.SemaphoreType.DMA((chunks.shape[0],)),
        ],
        compiler_params=pltpu.CompilerParams(collective_id=collective_id, has_side_effects=True),
    )(chunks)


def gather_kernel(
    rows_ref, long_ref, rows_out, long_out, rows_in, long_in, local_sems,
    rows_send, rows_recv, long_send, long_recv,
):
    count = rows_ref.shape[0]
    groups = lax.axis_size("ch")
    me = lax.axis_index("ctx")
    mine = lax.axis_index("ch")
    mesh_id = pl.DeviceIdType.MESH
    peers = [(c, h) for c in range(count) for h in range(groups) if (c, h) != (0, 0)]
    barrier = pltpu.get_barrier_semaphore()
    for step_c, step_h in peers:
        peer, other = lax.rem(me + step_c, count), lax.rem(mine + step_h, groups)
        pl.semaphore_signal(barrier, 1, device_id=(peer, other), device_id_type=mesh_id)
    pl.semaphore_wait(barrier, len(peers))
    local_rows = pltpu.make_async_copy(rows_ref.at[me], rows_in.at[me], local_sems.at[0])
    local_long = pltpu.make_async_copy(long_ref.at[me], long_in.at[me, mine], local_sems.at[1])
    local_rows.start()
    local_long.start()
    copies = []
    for step in range(1, count):
        peer = lax.rem(me + step, count)
        copy = pltpu.make_async_remote_copy(
            src_ref=rows_ref.at[peer],
            dst_ref=rows_in.at[me],
            send_sem=rows_send.at[peer],
            recv_sem=rows_recv.at[me],
            device_id=(peer, mine),
            device_id_type=mesh_id,
        )
        copy.start()
        copies.append(copy)
    for step_c, step_h in peers:
        peer, other = lax.rem(me + step_c, count), lax.rem(mine + step_h, groups)
        copy = pltpu.make_async_remote_copy(
            src_ref=long_ref.at[peer],
            dst_ref=long_in.at[me, mine],
            send_sem=long_send.at[peer * groups + other],
            recv_sem=long_recv.at[me * groups + mine],
            device_id=(peer, other),
            device_id_type=mesh_id,
        )
        copy.start()
        copies.append(copy)
    local_rows.wait()
    local_long.wait()
    for copy in copies:
        copy.wait_send()
    for step in range(1, count):
        source = lax.rem(me + step, count)
        pltpu.make_async_remote_copy(
            src_ref=rows_ref.at[source],
            dst_ref=rows_in.at[source],
            send_sem=rows_send.at[source],
            recv_sem=rows_recv.at[source],
            device_id=(source, mine),
            device_id_type=mesh_id,
        ).wait_recv()
    for step_c, step_h in peers:
        source, other = lax.rem(me + step_c, count), lax.rem(mine + step_h, groups)
        pltpu.make_async_remote_copy(
            src_ref=long_ref.at[source],
            dst_ref=long_in.at[source, other],
            send_sem=long_send.at[source * groups + other],
            recv_sem=long_recv.at[source * groups + other],
            device_id=(source, other),
            device_id_type=mesh_id,
        ).wait_recv()
    rows_out[...] = rows_in[...]
    long_out[...] = long_in[...]


def gather(rows, longs, groups, collective_id):
    count = rows.shape[0]
    long_shape = (count, groups) + longs.shape[1:]
    vmem = pl.BlockSpec(memory_space=pltpu.VMEM)
    return pl.pallas_call(
        gather_kernel,
        out_shape=(
            jax.ShapeDtypeStruct(rows.shape, rows.dtype),
            jax.ShapeDtypeStruct(long_shape, longs.dtype),
        ),
        in_specs=[vmem, vmem],
        out_specs=(vmem, vmem),
        scratch_shapes=[
            pltpu.VMEM(rows.shape, rows.dtype),
            pltpu.VMEM(long_shape, longs.dtype),
            pltpu.SemaphoreType.DMA((2,)),
            pltpu.SemaphoreType.DMA((count,)),
            pltpu.SemaphoreType.DMA((count,)),
            pltpu.SemaphoreType.DMA((count * groups,)),
            pltpu.SemaphoreType.DMA((count * groups,)),
        ],
        compiler_params=pltpu.CompilerParams(collective_id=collective_id, has_side_effects=True),
    )(rows, longs)


def per_device(inputs, short_filter, long_filter, grad_out):
    tap_count = short_filter.shape[0]
    filter_count, chan_count, shard_len = inputs.shape
    ctx_count = lax.axis_size("ctx")
    my_index = lax.axis_index("ctx")
    total_len = shard_len * ctx_count
    per_dev = filter_count * chan_count // ctx_count
    per_filter = chan_count // per_dev
    block_len = 128
    block_count = total_len // block_len

    send = jnp.concatenate(
        [
            grad_out.reshape(ctx_count, per_dev, shard_len),
            inputs.reshape(ctx_count, per_dev, shard_len),
            jnp.repeat(long_filter, per_filter, axis=0)[:, None, :],
        ],
        axis=1,
    )
    recv = swap(send, 0)
    seqs = recv.transpose(1, 0, 2).reshape(2 * per_dev + 1, total_len)
    grad_seq = seqs[:per_dev]
    in_seq = seqs[per_dev : 2 * per_dev].astype(jnp.float32)
    filt_seq = seqs[2 * per_dev :]
    taps = short_filter.reshape(tap_count, ctx_count, per_dev)
    taps = lax.dynamic_index_in_dim(taps, my_index, axis=1, keepdims=False)

    hidden = sum(
        (taps[offset][:, None] * delayed(in_seq, offset, total_len) for offset in range(tap_count))
    )
    hidden = hidden.astype(jnp.bfloat16)

    grad_hidden, grad_long = correlate_all(
        grad_seq, jnp.concatenate([filt_seq, hidden], axis=0), block_len
    )

    padded_grad = jnp.pad(grad_hidden, ((0, 0), (0, tap_count - 1)))
    grad_in = sum(
        (
            taps[offset][:, None] * padded_grad[:, offset : offset + total_len]
            for offset in range(tap_count)
        )
    )
    grad_in = grad_in.astype(jnp.bfloat16)
    grad_short = jnp.stack(
        [
            jnp.sum(grad_hidden * delayed(in_seq, offset, total_len), axis=1)
            for offset in range(tap_count)
        ]
    )

    short_row = jnp.pad(
        grad_short.reshape(1, tap_count * per_dev),
        ((0, 0), (0, shard_len - tap_count * per_dev)),
    )
    back = jnp.concatenate(
        [
            grad_in.astype(jnp.float32).reshape(per_dev, ctx_count, shard_len).transpose(1, 0, 2),
            jnp.broadcast_to(short_row[None], (ctx_count, 1, shard_len)),
        ],
        axis=1,
    )
    groups = lax.axis_size("ch")
    got, got_long = gather(back, grad_long.reshape(ctx_count, 1, shard_len), groups, 1)
    grad_in_out = got[:, :per_dev].reshape(filter_count, chan_count, shard_len)
    grad_in_out = grad_in_out.astype(jnp.bfloat16)
    grad_long_out = got_long.reshape(filter_count, per_filter * groups, shard_len).sum(axis=1)
    short_all = got[:, per_dev, : tap_count * per_dev].reshape(ctx_count, tap_count, per_dev)
    grad_short_out = short_all.transpose(1, 0, 2).reshape(tap_count, filter_count, chan_count)
    return (grad_in_out, grad_long_out, grad_short_out)


def solution(mesh):
    in_specs = (P(None, "ch", "ctx"), P(None, None, "ch"), P(None, "ctx"), P(None, "ch", "ctx"))
    out_specs = (P(None, "ch", "ctx"), P(None, "ctx"), P(None, None, "ch"))
    return jax.shard_map(
        per_device, mesh=mesh, in_specs=in_specs, out_specs=out_specs, check_vma=False
    )
```

```python
import jax
import jax.numpy as jnp
from jax import lax
from jax.experimental import pallas as pl
from jax.experimental.pallas import tpu as pltpu
from jax.sharding import PartitionSpec as P


def delayed(values, by, length):
    return jnp.pad(values, ((0, 0), (by, 0)))[:, :length]


def conv_kernel(grad_ref, rev_ref, hidden_ref, long_ref, hankel, toeplitz):
    chans, _, block_len = grad_ref.shape
    block_count = hidden_ref.shape[1]
    sources, lags, _ = rev_ref.shape

    def fill_hankel(lag, carry):
        col = pl.multiple_of(lag * block_len, block_len)
        for g in range(chans):
            hankel[g, :, pl.ds(col, block_len)] = grad_ref[g, pl.ds(lag, block_count), :].astype(
                hankel.dtype
            )
        return carry

    lax.fori_loop(0, lags, fill_hankel, 0)

    def fill_toeplitz(lag, carry):
        row = pl.multiple_of(lag * block_len, block_len)
        for s in range(sources):
            line = rev_ref[s, pl.ds(lag, 1), :]
            tiled = jnp.broadcast_to(line, (block_len, 2 * block_len))
            skewed = pltpu.roll(tiled, block_len + 1, 1, stride=1, stride_axis=0)
            toeplitz[s, pl.ds(row, block_len), :] = skewed[:, :block_len].astype(toeplitz.dtype)
        return carry

    lax.fori_loop(0, lags, fill_toeplitz, 0)

    for g in range(chans):
        hidden_ref[g] = jnp.dot(hankel[g], toeplitz[0], preferred_element_type=jnp.float32)
    acc = jnp.dot(hankel[0], toeplitz[1], preferred_element_type=jnp.float32)
    for g in range(1, chans):
        acc = acc + jnp.dot(hankel[g], toeplitz[1 + g], preferred_element_type=jnp.float32)
    long_ref[...] = acc


def correlate_all(grad_seq, sources, block_len):
    chans, total_len = grad_seq.shape
    count = sources.shape[0]
    block_count = total_len // block_len
    grad_pad = jnp.pad(
        grad_seq.astype(jnp.float32).reshape(chans, block_count, block_len),
        ((0, 0), (0, block_count), (0, 0)),
    )
    blocks = sources.reshape(count, block_count, block_len)
    padded = jnp.pad(blocks, ((0, 0), (1, 1), (0, 0)))
    pairs = jnp.concatenate([padded[:, :-1], padded[:, 1:]], axis=2)
    rev = pairs[..., ::-1].astype(jnp.float32)
    lags = block_count + 1
    hidden, long = pl.pallas_call(
        conv_kernel,
        out_shape=(
            jax.ShapeDtypeStruct((chans, block_count, block_len), jnp.float32),
            jax.ShapeDtypeStruct((block_count, block_len), jnp.float32),
        ),
        scratch_shapes=[
            pltpu.VMEM((chans, block_count, lags * block_len), jnp.bfloat16),
            pltpu.VMEM((count, lags * block_len, block_len), jnp.bfloat16),
        ],
        compiler_params=pltpu.CompilerParams(vmem_limit_bytes=48 * 1024 * 1024),
    )(grad_pad, rev)
    return hidden.reshape(chans, total_len), long.reshape(total_len)


def swap_kernel(send_ref, out_ref, landed, local_sem, send_sem, recv_sem):
    count = send_ref.shape[0]
    me = lax.axis_index("ctx")
    mine = lax.axis_index("ch")
    barrier = pltpu.get_barrier_semaphore()
    for step in range(1, count):
        peer = lax.rem(me + step, count)
        pl.semaphore_signal(
            barrier, 1, device_id=(peer, mine), device_id_type=pl.DeviceIdType.MESH
        )
    pl.semaphore_wait(barrier, count - 1)
    local = pltpu.make_async_copy(send_ref.at[me], landed.at[me], local_sem)
    local.start()
    copies = []
    for step in range(1, count):
        peer = lax.rem(me + step, count)
        copy = pltpu.make_async_remote_copy(
            src_ref=send_ref.at[peer],
            dst_ref=landed.at[me],
            send_sem=send_sem.at[peer],
            recv_sem=recv_sem.at[me],
            device_id=(peer, mine),
            device_id_type=pl.DeviceIdType.MESH,
        )
        copy.start()
        copies.append(copy)
    local.wait()
    for copy in copies:
        copy.wait_send()
    for step in range(1, count):
        source = lax.rem(me + step, count)
        pltpu.make_async_remote_copy(
            src_ref=send_ref.at[source],
            dst_ref=landed.at[source],
            send_sem=send_sem.at[source],
            recv_sem=recv_sem.at[source],
            device_id=(source, mine),
            device_id_type=pl.DeviceIdType.MESH,
        ).wait_recv()
    out_ref[...] = landed[...]


def swap(chunks, collective_id):
    return pl.pallas_call(
        swap_kernel,
        out_shape=jax.ShapeDtypeStruct(chunks.shape, chunks.dtype),
        in_specs=[pl.BlockSpec(memory_space=pltpu.VMEM)],
        out_specs=pl.BlockSpec(memory_space=pltpu.VMEM),
        scratch_shapes=[
            pltpu.VMEM(chunks.shape, chunks.dtype),
            pltpu.SemaphoreType.DMA,
            pltpu.SemaphoreType.DMA((chunks.shape[0],)),
            pltpu.SemaphoreType.DMA((chunks.shape[0],)),
        ],
        compiler_params=pltpu.CompilerParams(collective_id=collective_id, has_side_effects=True),
    )(chunks)


def gather_kernel(
    rows_ref, long_ref, rows_out, long_out, rows_in, long_in, local_sems,
    rows_send, rows_recv, long_send, long_recv,
):
    count = rows_ref.shape[0]
    groups = lax.axis_size("ch")
    me = lax.axis_index("ctx")
    mine = lax.axis_index("ch")
    mesh_id = pl.DeviceIdType.MESH
    peers = [(c, h) for c in range(count) for h in range(groups) if (c, h) != (0, 0)]
    barrier = pltpu.get_barrier_semaphore()
    for step_c, step_h in peers:
        peer, other = lax.rem(me + step_c, count), lax.rem(mine + step_h, groups)
        pl.semaphore_signal(barrier, 1, device_id=(peer, other), device_id_type=mesh_id)
    pl.semaphore_wait(barrier, len(peers))
    local_rows = pltpu.make_async_copy(rows_ref.at[me], rows_in.at[me], local_sems.at[0])
    local_long = pltpu.make_async_copy(long_ref.at[me], long_in.at[me, mine], local_sems.at[1])
    local_rows.start()
    local_long.start()
    copies = []
    for step in range(1, count):
        peer = lax.rem(me + step, count)
        copy = pltpu.make_async_remote_copy(
            src_ref=rows_ref.at[peer],
            dst_ref=rows_in.at[me],
            send_sem=rows_send.at[peer],
            recv_sem=rows_recv.at[me],
            device_id=(peer, mine),
            device_id_type=mesh_id,
        )
        copy.start()
        copies.append(copy)
    for step_c, step_h in peers:
        peer, other = lax.rem(me + step_c, count), lax.rem(mine + step_h, groups)
        copy = pltpu.make_async_remote_copy(
            src_ref=long_ref.at[peer],
            dst_ref=long_in.at[me, mine],
            send_sem=long_send.at[peer * groups + other],
            recv_sem=long_recv.at[me * groups + mine],
            device_id=(peer, other),
            device_id_type=mesh_id,
        )
        copy.start()
        copies.append(copy)
    local_rows.wait()
    local_long.wait()
    for copy in copies:
        copy.wait_send()
    for step in range(1, count):
        source = lax.rem(me + step, count)
        pltpu.make_async_remote_copy(
            src_ref=rows_ref.at[source],
            dst_ref=rows_in.at[source],
            send_sem=rows_send.at[source],
            recv_sem=rows_recv.at[source],
            device_id=(source, mine),
            device_id_type=mesh_id,
        ).wait_recv()
    for step_c, step_h in peers:
        source, other = lax.rem(me + step_c, count), lax.rem(mine + step_h, groups)
        pltpu.make_async_remote_copy(
            src_ref=long_ref.at[source],
            dst_ref=long_in.at[source, other],
            send_sem=long_send.at[source * groups + other],
            recv_sem=long_recv.at[source * groups + other],
            device_id=(source, other),
            device_id_type=mesh_id,
        ).wait_recv()
    rows_out[...] = rows_in[...]
    long_out[...] = long_in[...]


def gather(rows, longs, groups, collective_id):
    count = rows.shape[0]
    long_shape = (count, groups) + longs.shape[1:]
    vmem = pl.BlockSpec(memory_space=pltpu.VMEM)
    return pl.pallas_call(
        gather_kernel,
        out_shape=(
            jax.ShapeDtypeStruct(rows.shape, rows.dtype),
            jax.ShapeDtypeStruct(long_shape, longs.dtype),
        ),
        in_specs=[vmem, vmem],
        out_specs=(vmem, vmem),
        scratch_shapes=[
            pltpu.VMEM(rows.shape, rows.dtype),
            pltpu.VMEM(long_shape, longs.dtype),
            pltpu.SemaphoreType.DMA((2,)),
            pltpu.SemaphoreType.DMA((count,)),
            pltpu.SemaphoreType.DMA((count,)),
            pltpu.SemaphoreType.DMA((count * groups,)),
            pltpu.SemaphoreType.DMA((count * groups,)),
        ],
        compiler_params=pltpu.CompilerParams(collective_id=collective_id, has_side_effects=True),
    )(rows, longs)


def fused_kernel(
    grad_ref, rev_ref, in_ref, taps_ref, rows_out, long_out,
    hankel, toeplitz, grad_buf, rows_buf, long_buf, rows_in, long_in, local_sems,
    rows_send, rows_recv, long_send, long_recv,
):
    count = rows_buf.shape[0]
    chans, _, block_len = grad_ref.shape
    block_count = count
    sources, lags, _ = rev_ref.shape
    tap_count = taps_ref.shape[0]
    groups = lax.axis_size("ch")
    me = lax.axis_index("ctx")
    mine = lax.axis_index("ch")
    mesh_id = pl.DeviceIdType.MESH
    peers = [(c, h) for c in range(count) for h in range(groups) if (c, h) != (0, 0)]
    barrier = pltpu.get_barrier_semaphore()
    for step_c, step_h in peers:
        peer, other = lax.rem(me + step_c, count), lax.rem(mine + step_h, groups)
        pl.semaphore_signal(barrier, 1, device_id=(peer, other), device_id_type=mesh_id)

    def fill_hankel(lag, carry):
        col = pl.multiple_of(lag * block_len, block_len)
        for g in range(chans):
            hankel[g, :, pl.ds(col, block_len)] = grad_ref[g, pl.ds(lag, block_count), :].astype(
                hankel.dtype
            )
        return carry

    lax.fori_loop(0, lags, fill_hankel, 0)

    def fill_toeplitz(lag, carry):
        row = pl.multiple_of(lag * block_len, block_len)
        for s in range(sources):
            line = rev_ref[s, pl.ds(lag, 1), :]
            tiled = jnp.broadcast_to(line, (block_len, 2 * block_len))
            skewed = pltpu.roll(tiled, block_len + 1, 1, stride=1, stride_axis=0)
            toeplitz[s, pl.ds(row, block_len), :] = skewed[:, :block_len].astype(toeplitz.dtype)
        return carry

    lax.fori_loop(0, lags, fill_toeplitz, 0)

    acc = jnp.dot(hankel[0], toeplitz[1], preferred_element_type=jnp.float32)
    for g in range(1, chans):
        acc = acc + jnp.dot(hankel[g], toeplitz[1 + g], preferred_element_type=jnp.float32)
    long_buf[:, 0, :] = acc

    lane = lax.broadcasted_iota(jnp.int32, (block_count, block_len), 1)
    short_row = jnp.zeros((block_count, block_len), jnp.float32)
    grad_buf[...] = jnp.zeros_like(grad_buf)
    for g in range(chans):
        hidden_grad = jnp.dot(hankel[g], toeplitz[0], preferred_element_type=jnp.float32)
        grad_buf[g, pl.ds(0, block_count), :] = hidden_grad
        following = grad_buf[g, pl.ds(1, block_count), :]
        total = taps_ref[0, g] * hidden_grad
        for offset in range(1, tap_count):
            here = pltpu.roll(hidden_grad, block_len - offset, 1)
            there = pltpu.roll(following, block_len - offset, 1)
            total = total + taps_ref[offset, g] * jnp.where(
                lane >= block_len - offset, there, here
            )
        rows_buf[:, g, :] = total.astype(jnp.bfloat16).astype(jnp.float32)
        current = in_ref[g, pl.ds(1, block_count), :]
        previous = in_ref[g, pl.ds(0, block_count), :]
        for offset in range(tap_count):
            if offset == 0:
                delayed_in = current
            else:
                delayed_in = jnp.where(
                    lane < offset,
                    pltpu.roll(previous, offset, 1),
                    pltpu.roll(current, offset, 1),
                )
            value = jnp.sum(hidden_grad * delayed_in)
            short_row = jnp.where(lane == offset * chans + g, value, short_row)
    rows_buf[:, chans, :] = short_row

    pl.semaphore_wait(barrier, len(peers))
    local_rows = pltpu.make_async_copy(rows_buf.at[me], rows_in.at[me], local_sems.at[0])
    local_long = pltpu.make_async_copy(long_buf.at[me], long_in.at[me, mine], local_sems.at[1])
    local_rows.start()
    local_long.start()
    copies = []
    for step in range(1, count):
        peer = lax.rem(me + step, count)
        copy = pltpu.make_async_remote_copy(
            src_ref=rows_buf.at[peer],
            dst_ref=rows_in.at[me],
            send_sem=rows_send.at[peer],
            recv_sem=rows_recv.at[me],
            device_id=(peer, mine),
            device_id_type=mesh_id,
        )
        copy.start()
        copies.append(copy)
    for step_c, step_h in peers:
        peer, other = lax.rem(me + step_c, count), lax.rem(mine + step_h, groups)
        copy = pltpu.make_async_remote_copy(
            src_ref=long_buf.at[peer],
            dst_ref=long_in.at[me, mine],
            send_sem=long_send.at[peer * groups + other],
            recv_sem=long_recv.at[me * groups + mine],
            device_id=(peer, other),
            device_id_type=mesh_id,
        )
        copy.start()
        copies.append(copy)
    local_rows.wait()
    local_long.wait()
    for copy in copies:
        copy.wait_send()
    for step in range(1, count):
        source = lax.rem(me + step, count)
        pltpu.make_async_remote_copy(
            src_ref=rows_buf.at[source],
            dst_ref=rows_in.at[source],
            send_sem=rows_send.at[source],
            recv_sem=rows_recv.at[source],
            device_id=(source, mine),
            device_id_type=mesh_id,
        ).wait_recv()
    for step_c, step_h in peers:
        source, other = lax.rem(me + step_c, count), lax.rem(mine + step_h, groups)
        pltpu.make_async_remote_copy(
            src_ref=long_buf.at[source],
            dst_ref=long_in.at[source, other],
            send_sem=long_send.at[source * groups + other],
            recv_sem=long_recv.at[source * groups + other],
            device_id=(source, other),
            device_id_type=mesh_id,
        ).wait_recv()
    rows_out[...] = rows_in[...]
    long_out[...] = long_in[...]


def fused(grad_seq, sources, in_seq, taps, groups, block_len, collective_id):
    chans, total_len = grad_seq.shape
    count = sources.shape[0]
    block_count = total_len // block_len
    grad_pad = jnp.pad(
        grad_seq.astype(jnp.float32).reshape(chans, block_count, block_len),
        ((0, 0), (0, block_count), (0, 0)),
    )
    blocks = sources.reshape(count, block_count, block_len)
    padded = jnp.pad(blocks, ((0, 0), (1, 1), (0, 0)))
    pairs = jnp.concatenate([padded[:, :-1], padded[:, 1:]], axis=2)
    rev = pairs[..., ::-1].astype(jnp.float32)
    in_pad = jnp.pad(in_seq.reshape(chans, block_count, block_len), ((0, 0), (1, 0), (0, 0)))
    lags = block_count + 1
    rows_shape = (block_count, chans + 1, block_len)
    long_shape = (block_count, groups, 1, block_len)
    vmem = pl.BlockSpec(memory_space=pltpu.VMEM)
    return pl.pallas_call(
        fused_kernel,
        out_shape=(
            jax.ShapeDtypeStruct(rows_shape, jnp.float32),
            jax.ShapeDtypeStruct(long_shape, jnp.float32),
        ),
        in_specs=[vmem, vmem, vmem, pl.BlockSpec(memory_space=pltpu.SMEM)],
        out_specs=(vmem, vmem),
        scratch_shapes=[
            pltpu.VMEM((chans, block_count, lags * block_len), jnp.bfloat16),
            pltpu.VMEM((count, lags * block_len, block_len), jnp.bfloat16),
            pltpu.VMEM((chans, block_count + 8, block_len), jnp.float32),
            pltpu.VMEM(rows_shape, jnp.float32),
            pltpu.VMEM((block_count, 1, block_len), jnp.float32),
            pltpu.VMEM(rows_shape, jnp.float32),
            pltpu.VMEM(long_shape, jnp.float32),
            pltpu.SemaphoreType.DMA((2,)),
            pltpu.SemaphoreType.DMA((block_count,)),
            pltpu.SemaphoreType.DMA((block_count,)),
            pltpu.SemaphoreType.DMA((block_count * groups,)),
            pltpu.SemaphoreType.DMA((block_count * groups,)),
        ],
        compiler_params=pltpu.CompilerParams(
            collective_id=collective_id,
            has_side_effects=True,
            vmem_limit_bytes=48 * 1024 * 1024,
        ),
    )(grad_pad, rev, in_pad, taps)


def per_device(inputs, short_filter, long_filter, grad_out):
    tap_count = short_filter.shape[0]
    filter_count, chan_count, shard_len = inputs.shape
    ctx_count = lax.axis_size("ctx")
    my_index = lax.axis_index("ctx")
    total_len = shard_len * ctx_count
    per_dev = filter_count * chan_count // ctx_count
    per_filter = chan_count // per_dev
    block_len = 128
    block_count = total_len // block_len

    send = jnp.concatenate(
        [
            grad_out.reshape(ctx_count, per_dev, shard_len),
            inputs.reshape(ctx_count, per_dev, shard_len),
            jnp.repeat(long_filter, per_filter, axis=0)[:, None, :],
        ],
        axis=1,
    )
    recv = swap(send, 0)
    seqs = recv.transpose(1, 0, 2).reshape(2 * per_dev + 1, total_len)
    grad_seq = seqs[:per_dev]
    in_seq = seqs[per_dev : 2 * per_dev].astype(jnp.float32)
    filt_seq = seqs[2 * per_dev :]
    taps = short_filter.reshape(tap_count, ctx_count, per_dev)
    taps = lax.dynamic_index_in_dim(taps, my_index, axis=1, keepdims=False)

    hidden = sum(
        (taps[offset][:, None] * delayed(in_seq, offset, total_len) for offset in range(tap_count))
    )
    hidden = hidden.astype(jnp.bfloat16)

    groups = lax.axis_size("ch")
    got, got_long = fused(
        grad_seq,
        jnp.concatenate([filt_seq, hidden], axis=0),
        in_seq,
        taps,
        groups,
        block_len,
        1,
    )
    grad_in_out = got[:, :per_dev].reshape(filter_count, chan_count, shard_len)
    grad_in_out = grad_in_out.astype(jnp.bfloat16)
    grad_long_out = got_long.reshape(filter_count, per_filter * groups, shard_len).sum(axis=1)
    short_all = got[:, per_dev, : tap_count * per_dev].reshape(ctx_count, tap_count, per_dev)
    grad_short_out = short_all.transpose(1, 0, 2).reshape(tap_count, filter_count, chan_count)
    return (grad_in_out, grad_long_out, grad_short_out)


def solution(mesh):
    in_specs = (P(None, "ch", "ctx"), P(None, None, "ch"), P(None, "ctx"), P(None, "ch", "ctx"))
    out_specs = (P(None, "ch", "ctx"), P(None, "ctx"), P(None, None, "ch"))
    return jax.shard_map(
        per_device, mesh=mesh, in_specs=in_specs, out_specs=out_specs, check_vma=False
    )
```

```python
import jax
import jax.numpy as jnp
from jax import lax
from jax.experimental import pallas as pl
from jax.experimental.pallas import tpu as pltpu
from jax.sharding import PartitionSpec as P


def delayed(values, by, length):
    return jnp.pad(values, ((0, 0), (by, 0)))[:, :length]


def conv_kernel(grad_ref, rev_ref, hidden_ref, long_ref, hankel, toeplitz):
    chans, _, block_len = grad_ref.shape
    block_count = hidden_ref.shape[1]
    sources, lags, _ = rev_ref.shape

    def fill_hankel(lag, carry):
        col = pl.multiple_of(lag * block_len, block_len)
        for g in range(chans):
            hankel[g, :, pl.ds(col, block_len)] = grad_ref[g, pl.ds(lag, block_count), :].astype(
                hankel.dtype
            )
        return carry

    lax.fori_loop(0, lags, fill_hankel, 0)

    def fill_toeplitz(lag, carry):
        row = pl.multiple_of(lag * block_len, block_len)
        for s in range(sources):
            line = rev_ref[s, pl.ds(lag, 1), :]
            tiled = jnp.broadcast_to(line, (block_len, 2 * block_len))
            skewed = pltpu.roll(tiled, block_len + 1, 1, stride=1, stride_axis=0)
            toeplitz[s, pl.ds(row, block_len), :] = skewed[:, :block_len].astype(toeplitz.dtype)
        return carry

    lax.fori_loop(0, lags, fill_toeplitz, 0)

    for g in range(chans):
        hidden_ref[g] = jnp.dot(hankel[g], toeplitz[0], preferred_element_type=jnp.float32)
    acc = jnp.dot(hankel[0], toeplitz[1], preferred_element_type=jnp.float32)
    for g in range(1, chans):
        acc = acc + jnp.dot(hankel[g], toeplitz[1 + g], preferred_element_type=jnp.float32)
    long_ref[...] = acc


def correlate_all(grad_seq, sources, block_len):
    chans, total_len = grad_seq.shape
    count = sources.shape[0]
    block_count = total_len // block_len
    grad_pad = jnp.pad(
        grad_seq.astype(jnp.float32).reshape(chans, block_count, block_len),
        ((0, 0), (0, block_count), (0, 0)),
    )
    blocks = sources.reshape(count, block_count, block_len)
    padded = jnp.pad(blocks, ((0, 0), (1, 1), (0, 0)))
    pairs = jnp.concatenate([padded[:, :-1], padded[:, 1:]], axis=2)
    rev = pairs[..., ::-1].astype(jnp.float32)
    lags = block_count + 1
    hidden, long = pl.pallas_call(
        conv_kernel,
        out_shape=(
            jax.ShapeDtypeStruct((chans, block_count, block_len), jnp.float32),
            jax.ShapeDtypeStruct((block_count, block_len), jnp.float32),
        ),
        scratch_shapes=[
            pltpu.VMEM((chans, block_count, lags * block_len), jnp.bfloat16),
            pltpu.VMEM((count, lags * block_len, block_len), jnp.bfloat16),
        ],
        compiler_params=pltpu.CompilerParams(vmem_limit_bytes=48 * 1024 * 1024),
    )(grad_pad, rev)
    return hidden.reshape(chans, total_len), long.reshape(total_len)


def swap_kernel(send_ref, out_ref, landed, local_sem, send_sem, recv_sem):
    count = send_ref.shape[0]
    me = lax.axis_index("ctx")
    mine = lax.axis_index("ch")
    barrier = pltpu.get_barrier_semaphore()
    for step in range(1, count):
        peer = lax.rem(me + step, count)
        pl.semaphore_signal(
            barrier, 1, device_id=(peer, mine), device_id_type=pl.DeviceIdType.MESH
        )
    pl.semaphore_wait(barrier, count - 1)
    local = pltpu.make_async_copy(send_ref.at[me], landed.at[me], local_sem)
    local.start()
    copies = []
    for step in range(1, count):
        peer = lax.rem(me + step, count)
        copy = pltpu.make_async_remote_copy(
            src_ref=send_ref.at[peer],
            dst_ref=landed.at[me],
            send_sem=send_sem.at[peer],
            recv_sem=recv_sem.at[me],
            device_id=(peer, mine),
            device_id_type=pl.DeviceIdType.MESH,
        )
        copy.start()
        copies.append(copy)
    local.wait()
    for copy in copies:
        copy.wait_send()
    for step in range(1, count):
        source = lax.rem(me + step, count)
        pltpu.make_async_remote_copy(
            src_ref=send_ref.at[source],
            dst_ref=landed.at[source],
            send_sem=send_sem.at[source],
            recv_sem=recv_sem.at[source],
            device_id=(source, mine),
            device_id_type=pl.DeviceIdType.MESH,
        ).wait_recv()
    out_ref[...] = landed[...]


def swap(chunks, collective_id):
    return pl.pallas_call(
        swap_kernel,
        out_shape=jax.ShapeDtypeStruct(chunks.shape, chunks.dtype),
        in_specs=[pl.BlockSpec(memory_space=pltpu.VMEM)],
        out_specs=pl.BlockSpec(memory_space=pltpu.VMEM),
        scratch_shapes=[
            pltpu.VMEM(chunks.shape, chunks.dtype),
            pltpu.SemaphoreType.DMA,
            pltpu.SemaphoreType.DMA((chunks.shape[0],)),
            pltpu.SemaphoreType.DMA((chunks.shape[0],)),
        ],
        compiler_params=pltpu.CompilerParams(collective_id=collective_id, has_side_effects=True),
    )(chunks)


def gather_kernel(
    rows_ref, long_ref, rows_out, long_out, rows_in, long_in, local_sems,
    rows_send, rows_recv, long_send, long_recv,
):
    count = rows_ref.shape[0]
    groups = lax.axis_size("ch")
    me = lax.axis_index("ctx")
    mine = lax.axis_index("ch")
    mesh_id = pl.DeviceIdType.MESH
    peers = [(c, h) for c in range(count) for h in range(groups) if (c, h) != (0, 0)]
    barrier = pltpu.get_barrier_semaphore()
    for step_c, step_h in peers:
        peer, other = lax.rem(me + step_c, count), lax.rem(mine + step_h, groups)
        pl.semaphore_signal(barrier, 1, device_id=(peer, other), device_id_type=mesh_id)
    pl.semaphore_wait(barrier, len(peers))
    local_rows = pltpu.make_async_copy(rows_ref.at[me], rows_in.at[me], local_sems.at[0])
    local_long = pltpu.make_async_copy(long_ref.at[me], long_in.at[me, mine], local_sems.at[1])
    local_rows.start()
    local_long.start()
    copies = []
    for step in range(1, count):
        peer = lax.rem(me + step, count)
        copy = pltpu.make_async_remote_copy(
            src_ref=rows_ref.at[peer],
            dst_ref=rows_in.at[me],
            send_sem=rows_send.at[peer],
            recv_sem=rows_recv.at[me],
            device_id=(peer, mine),
            device_id_type=mesh_id,
        )
        copy.start()
        copies.append(copy)
    for step_c, step_h in peers:
        peer, other = lax.rem(me + step_c, count), lax.rem(mine + step_h, groups)
        copy = pltpu.make_async_remote_copy(
            src_ref=long_ref.at[peer],
            dst_ref=long_in.at[me, mine],
            send_sem=long_send.at[peer * groups + other],
            recv_sem=long_recv.at[me * groups + mine],
            device_id=(peer, other),
            device_id_type=mesh_id,
        )
        copy.start()
        copies.append(copy)
    local_rows.wait()
    local_long.wait()
    for copy in copies:
        copy.wait_send()
    for step in range(1, count):
        source = lax.rem(me + step, count)
        pltpu.make_async_remote_copy(
            src_ref=rows_ref.at[source],
            dst_ref=rows_in.at[source],
            send_sem=rows_send.at[source],
            recv_sem=rows_recv.at[source],
            device_id=(source, mine),
            device_id_type=mesh_id,
        ).wait_recv()
    for step_c, step_h in peers:
        source, other = lax.rem(me + step_c, count), lax.rem(mine + step_h, groups)
        pltpu.make_async_remote_copy(
            src_ref=long_ref.at[source],
            dst_ref=long_in.at[source, other],
            send_sem=long_send.at[source * groups + other],
            recv_sem=long_recv.at[source * groups + other],
            device_id=(source, other),
            device_id_type=mesh_id,
        ).wait_recv()
    rows_out[...] = rows_in[...]
    long_out[...] = long_in[...]


def gather(rows, longs, groups, collective_id):
    count = rows.shape[0]
    long_shape = (count, groups) + longs.shape[1:]
    vmem = pl.BlockSpec(memory_space=pltpu.VMEM)
    return pl.pallas_call(
        gather_kernel,
        out_shape=(
            jax.ShapeDtypeStruct(rows.shape, rows.dtype),
            jax.ShapeDtypeStruct(long_shape, longs.dtype),
        ),
        in_specs=[vmem, vmem],
        out_specs=(vmem, vmem),
        scratch_shapes=[
            pltpu.VMEM(rows.shape, rows.dtype),
            pltpu.VMEM(long_shape, longs.dtype),
            pltpu.SemaphoreType.DMA((2,)),
            pltpu.SemaphoreType.DMA((count,)),
            pltpu.SemaphoreType.DMA((count,)),
            pltpu.SemaphoreType.DMA((count * groups,)),
            pltpu.SemaphoreType.DMA((count * groups,)),
        ],
        compiler_params=pltpu.CompilerParams(collective_id=collective_id, has_side_effects=True),
    )(rows, longs)


def fused_kernel(
    grad_ref, rev_ref, in_ref, taps_ref, rows_out,
    hankel, toeplitz, grad_buf, rows_buf, ch_in, rows_in, local_sems,
    rows_send, rows_recv, ch_send, ch_recv,
):
    count = rows_buf.shape[0]
    chans, _, block_len = grad_ref.shape
    block_count = count
    sources, lags, _ = rev_ref.shape
    tap_count = taps_ref.shape[0]
    groups = lax.axis_size("ch")
    me = lax.axis_index("ctx")
    mine = lax.axis_index("ch")
    mesh_id = pl.DeviceIdType.MESH
    peers = [(c, 0) for c in range(1, count)] + [(0, h) for h in range(1, groups)]
    barrier = pltpu.get_barrier_semaphore()
    for step_c, step_h in peers:
        peer, other = lax.rem(me + step_c, count), lax.rem(mine + step_h, groups)
        pl.semaphore_signal(barrier, 1, device_id=(peer, other), device_id_type=mesh_id)

    def fill_hankel(lag, carry):
        col = pl.multiple_of(lag * block_len, block_len)
        for g in range(chans):
            hankel[g, :, pl.ds(col, block_len)] = grad_ref[g, pl.ds(lag, block_count), :].astype(
                hankel.dtype
            )
        return carry

    lax.fori_loop(0, lags, fill_hankel, 0)

    def fill_toeplitz(lag, carry):
        row = pl.multiple_of(lag * block_len, block_len)
        for s in range(sources):
            line = rev_ref[s, pl.ds(lag, 1), :]
            tiled = jnp.broadcast_to(line, (block_len, 2 * block_len))
            skewed = pltpu.roll(tiled, block_len + 1, 1, stride=1, stride_axis=0)
            toeplitz[s, pl.ds(row, block_len), :] = skewed[:, :block_len].astype(toeplitz.dtype)
        return carry

    lax.fori_loop(0, lags, fill_toeplitz, 0)

    acc = jnp.dot(hankel[0], toeplitz[1], preferred_element_type=jnp.float32)
    for g in range(1, chans):
        acc = acc + jnp.dot(hankel[g], toeplitz[1 + g], preferred_element_type=jnp.float32)
    ch_in[mine] = acc

    lane = lax.broadcasted_iota(jnp.int32, (block_count, block_len), 1)
    short_row = jnp.zeros((block_count, block_len), jnp.float32)
    grad_buf[...] = jnp.zeros_like(grad_buf)
    for g in range(chans):
        hidden_grad = jnp.dot(hankel[g], toeplitz[0], preferred_element_type=jnp.float32)
        grad_buf[g, pl.ds(0, block_count), :] = hidden_grad
        following = grad_buf[g, pl.ds(1, block_count), :]
        total = taps_ref[0, g] * hidden_grad
        for offset in range(1, tap_count):
            here = pltpu.roll(hidden_grad, block_len - offset, 1)
            there = pltpu.roll(following, block_len - offset, 1)
            total = total + taps_ref[offset, g] * jnp.where(
                lane >= block_len - offset, there, here
            )
        rows_buf[:, g, :] = total.astype(jnp.bfloat16).astype(jnp.float32)
        current = in_ref[g, pl.ds(1, block_count), :]
        previous = in_ref[g, pl.ds(0, block_count), :]
        for offset in range(tap_count):
            if offset == 0:
                delayed_in = current
            else:
                delayed_in = jnp.where(
                    lane < offset,
                    pltpu.roll(previous, offset, 1),
                    pltpu.roll(current, offset, 1),
                )
            value = jnp.sum(hidden_grad * delayed_in)
            short_row = jnp.where(lane == offset * chans + g, value, short_row)
    rows_buf[:, chans, :] = short_row

    pl.semaphore_wait(barrier, len(peers))
    partials = []
    for step in range(1, groups):
        other = lax.rem(mine + step, groups)
        copy = pltpu.make_async_remote_copy(
            src_ref=ch_in.at[mine],
            dst_ref=ch_in.at[mine],
            send_sem=ch_send.at[other],
            recv_sem=ch_recv.at[mine],
            device_id=(me, other),
            device_id_type=mesh_id,
        )
        copy.start()
        partials.append(copy)
    for copy in partials:
        copy.wait_send()
    for step in range(1, groups):
        source = lax.rem(mine + step, groups)
        pltpu.make_async_remote_copy(
            src_ref=ch_in.at[source],
            dst_ref=ch_in.at[source],
            send_sem=ch_send.at[source],
            recv_sem=ch_recv.at[source],
            device_id=(me, source),
            device_id_type=mesh_id,
        ).wait_recv()
    summed = ch_in[0]
    for h in range(1, groups):
        summed = summed + ch_in[h]
    rows_buf[:, chans + 1, :] = summed

    local_rows = pltpu.make_async_copy(rows_buf.at[me], rows_in.at[me], local_sems.at[0])
    local_rows.start()
    copies = []
    for step in range(1, count):
        peer = lax.rem(me + step, count)
        copy = pltpu.make_async_remote_copy(
            src_ref=rows_buf.at[peer],
            dst_ref=rows_in.at[me],
            send_sem=rows_send.at[peer],
            recv_sem=rows_recv.at[me],
            device_id=(peer, mine),
            device_id_type=mesh_id,
        )
        copy.start()
        copies.append(copy)
    local_rows.wait()
    for copy in copies:
        copy.wait_send()
    for step in range(1, count):
        source = lax.rem(me + step, count)
        pltpu.make_async_remote_copy(
            src_ref=rows_buf.at[source],
            dst_ref=rows_in.at[source],
            send_sem=rows_send.at[source],
            recv_sem=rows_recv.at[source],
            device_id=(source, mine),
            device_id_type=mesh_id,
        ).wait_recv()
    rows_out[...] = rows_in[...]


def fused(grad_seq, sources, in_seq, taps, groups, block_len, collective_id):
    chans, total_len = grad_seq.shape
    count = sources.shape[0]
    block_count = total_len // block_len
    grad_pad = jnp.pad(
        grad_seq.astype(jnp.float32).reshape(chans, block_count, block_len),
        ((0, 0), (0, block_count), (0, 0)),
    )
    blocks = sources.reshape(count, block_count, block_len)
    padded = jnp.pad(blocks, ((0, 0), (1, 1), (0, 0)))
    pairs = jnp.concatenate([padded[:, :-1], padded[:, 1:]], axis=2)
    rev = pairs[..., ::-1].astype(jnp.float32)
    in_pad = jnp.pad(in_seq.reshape(chans, block_count, block_len), ((0, 0), (1, 0), (0, 0)))
    lags = block_count + 1
    rows_shape = (block_count, chans + 2, block_len)
    vmem = pl.BlockSpec(memory_space=pltpu.VMEM)
    return pl.pallas_call(
        fused_kernel,
        out_shape=jax.ShapeDtypeStruct(rows_shape, jnp.float32),
        in_specs=[vmem, vmem, vmem, pl.BlockSpec(memory_space=pltpu.SMEM)],
        out_specs=vmem,
        scratch_shapes=[
            pltpu.VMEM((chans, block_count, lags * block_len), jnp.bfloat16),
            pltpu.VMEM((count, lags * block_len, block_len), jnp.bfloat16),
            pltpu.VMEM((chans, block_count + 8, block_len), jnp.float32),
            pltpu.VMEM(rows_shape, jnp.float32),
            pltpu.VMEM((groups, block_count, block_len), jnp.float32),
            pltpu.VMEM(rows_shape, jnp.float32),
            pltpu.SemaphoreType.DMA((1,)),
            pltpu.SemaphoreType.DMA((block_count,)),
            pltpu.SemaphoreType.DMA((block_count,)),
            pltpu.SemaphoreType.DMA((groups,)),
            pltpu.SemaphoreType.DMA((groups,)),
        ],
        compiler_params=pltpu.CompilerParams(
            collective_id=collective_id,
            has_side_effects=True,
            vmem_limit_bytes=48 * 1024 * 1024,
        ),
    )(grad_pad, rev, in_pad, taps)


def per_device(inputs, short_filter, long_filter, grad_out):
    tap_count = short_filter.shape[0]
    filter_count, chan_count, shard_len = inputs.shape
    ctx_count = lax.axis_size("ctx")
    my_index = lax.axis_index("ctx")
    total_len = shard_len * ctx_count
    per_dev = filter_count * chan_count // ctx_count
    per_filter = chan_count // per_dev
    block_len = 128
    block_count = total_len // block_len

    send = jnp.concatenate(
        [
            grad_out.reshape(ctx_count, per_dev, shard_len),
            inputs.reshape(ctx_count, per_dev, shard_len),
            jnp.repeat(long_filter, per_filter, axis=0)[:, None, :],
        ],
        axis=1,
    )
    recv = swap(send, 0)
    seqs = recv.transpose(1, 0, 2).reshape(2 * per_dev + 1, total_len)
    grad_seq = seqs[:per_dev]
    in_seq = seqs[per_dev : 2 * per_dev].astype(jnp.float32)
    filt_seq = seqs[2 * per_dev :]
    taps = short_filter.reshape(tap_count, ctx_count, per_dev)
    taps = lax.dynamic_index_in_dim(taps, my_index, axis=1, keepdims=False)

    hidden = sum(
        (taps[offset][:, None] * delayed(in_seq, offset, total_len) for offset in range(tap_count))
    )
    hidden = hidden.astype(jnp.bfloat16)

    groups = lax.axis_size("ch")
    got = fused(
        grad_seq,
        jnp.concatenate([filt_seq, hidden], axis=0),
        in_seq,
        taps,
        groups,
        block_len,
        1,
    )
    grad_in_out = got[:, :per_dev].reshape(filter_count, chan_count, shard_len)
    grad_in_out = grad_in_out.astype(jnp.bfloat16)
    grad_long_out = got[:, per_dev + 1].reshape(filter_count, per_filter, shard_len).sum(axis=1)
    short_all = got[:, per_dev, : tap_count * per_dev].reshape(ctx_count, tap_count, per_dev)
    grad_short_out = short_all.transpose(1, 0, 2).reshape(tap_count, filter_count, chan_count)
    return (grad_in_out, grad_long_out, grad_short_out)


def solution(mesh):
    in_specs = (P(None, "ch", "ctx"), P(None, None, "ch"), P(None, "ctx"), P(None, "ch", "ctx"))
    out_specs = (P(None, "ch", "ctx"), P(None, "ctx"), P(None, None, "ch"))
    return jax.shard_map(
        per_device, mesh=mesh, in_specs=in_specs, out_specs=out_specs, check_vma=False
    )
```

```python
import jax
import jax.numpy as jnp
from jax import lax
from jax.experimental import pallas as pl
from jax.experimental.pallas import tpu as pltpu
from jax.sharding import PartitionSpec as P


def delayed(values, by, length):
    return jnp.pad(values, ((0, 0), (by, 0)))[:, :length]


def conv_kernel(grad_ref, rev_ref, hidden_ref, long_ref, hankel, toeplitz):
    chans, _, block_len = grad_ref.shape
    block_count = hidden_ref.shape[1]
    sources, lags, _ = rev_ref.shape

    def fill_hankel(lag, carry):
        col = pl.multiple_of(lag * block_len, block_len)
        for g in range(chans):
            hankel[g, :, pl.ds(col, block_len)] = grad_ref[g, pl.ds(lag, block_count), :].astype(
                hankel.dtype
            )
        return carry

    lax.fori_loop(0, lags, fill_hankel, 0)

    def fill_toeplitz(lag, carry):
        row = pl.multiple_of(lag * block_len, block_len)
        for s in range(sources):
            line = rev_ref[s, pl.ds(lag, 1), :]
            tiled = jnp.broadcast_to(line, (block_len, 2 * block_len))
            skewed = pltpu.roll(tiled, block_len + 1, 1, stride=1, stride_axis=0)
            toeplitz[s, pl.ds(row, block_len), :] = skewed[:, :block_len].astype(toeplitz.dtype)
        return carry

    lax.fori_loop(0, lags, fill_toeplitz, 0)

    for g in range(chans):
        hidden_ref[g] = jnp.dot(hankel[g], toeplitz[0], preferred_element_type=jnp.float32)
    acc = jnp.dot(hankel[0], toeplitz[1], preferred_element_type=jnp.float32)
    for g in range(1, chans):
        acc = acc + jnp.dot(hankel[g], toeplitz[1 + g], preferred_element_type=jnp.float32)
    long_ref[...] = acc


def correlate_all(grad_seq, sources, block_len):
    chans, total_len = grad_seq.shape
    count = sources.shape[0]
    block_count = total_len // block_len
    grad_pad = jnp.pad(
        grad_seq.astype(jnp.float32).reshape(chans, block_count, block_len),
        ((0, 0), (0, block_count), (0, 0)),
    )
    blocks = sources.reshape(count, block_count, block_len)
    padded = jnp.pad(blocks, ((0, 0), (1, 1), (0, 0)))
    pairs = jnp.concatenate([padded[:, :-1], padded[:, 1:]], axis=2)
    rev = pairs[..., ::-1].astype(jnp.float32)
    lags = block_count + 1
    hidden, long = pl.pallas_call(
        conv_kernel,
        out_shape=(
            jax.ShapeDtypeStruct((chans, block_count, block_len), jnp.float32),
            jax.ShapeDtypeStruct((block_count, block_len), jnp.float32),
        ),
        scratch_shapes=[
            pltpu.VMEM((chans, block_count, lags * block_len), jnp.bfloat16),
            pltpu.VMEM((count, lags * block_len, block_len), jnp.bfloat16),
        ],
        compiler_params=pltpu.CompilerParams(vmem_limit_bytes=48 * 1024 * 1024),
    )(grad_pad, rev)
    return hidden.reshape(chans, total_len), long.reshape(total_len)


def swap_kernel(send_ref, out_ref, landed, local_sem, send_sem, recv_sem):
    count = send_ref.shape[0]
    me = lax.axis_index("ctx")
    mine = lax.axis_index("ch")
    barrier = pltpu.get_barrier_semaphore()
    for step in range(1, count):
        peer = lax.rem(me + step, count)
        pl.semaphore_signal(
            barrier, 1, device_id=(peer, mine), device_id_type=pl.DeviceIdType.MESH
        )
    pl.semaphore_wait(barrier, count - 1)
    local = pltpu.make_async_copy(send_ref.at[me], landed.at[me], local_sem)
    local.start()
    copies = []
    for step in range(1, count):
        peer = lax.rem(me + step, count)
        copy = pltpu.make_async_remote_copy(
            src_ref=send_ref.at[peer],
            dst_ref=landed.at[me],
            send_sem=send_sem.at[peer],
            recv_sem=recv_sem.at[me],
            device_id=(peer, mine),
            device_id_type=pl.DeviceIdType.MESH,
        )
        copy.start()
        copies.append(copy)
    local.wait()
    for copy in copies:
        copy.wait_send()
    for step in range(1, count):
        source = lax.rem(me + step, count)
        pltpu.make_async_remote_copy(
            src_ref=send_ref.at[source],
            dst_ref=landed.at[source],
            send_sem=send_sem.at[source],
            recv_sem=recv_sem.at[source],
            device_id=(source, mine),
            device_id_type=pl.DeviceIdType.MESH,
        ).wait_recv()
    out_ref[...] = landed[...]


def swap(chunks, collective_id):
    return pl.pallas_call(
        swap_kernel,
        out_shape=jax.ShapeDtypeStruct(chunks.shape, chunks.dtype),
        in_specs=[pl.BlockSpec(memory_space=pltpu.VMEM)],
        out_specs=pl.BlockSpec(memory_space=pltpu.VMEM),
        scratch_shapes=[
            pltpu.VMEM(chunks.shape, chunks.dtype),
            pltpu.SemaphoreType.DMA,
            pltpu.SemaphoreType.DMA((chunks.shape[0],)),
            pltpu.SemaphoreType.DMA((chunks.shape[0],)),
        ],
        compiler_params=pltpu.CompilerParams(collective_id=collective_id, has_side_effects=True),
    )(chunks)


def gather_kernel(
    rows_ref, long_ref, rows_out, long_out, rows_in, long_in, local_sems,
    rows_send, rows_recv, long_send, long_recv,
):
    count = rows_ref.shape[0]
    groups = lax.axis_size("ch")
    me = lax.axis_index("ctx")
    mine = lax.axis_index("ch")
    mesh_id = pl.DeviceIdType.MESH
    peers = [(c, h) for c in range(count) for h in range(groups) if (c, h) != (0, 0)]
    barrier = pltpu.get_barrier_semaphore()
    for step_c, step_h in peers:
        peer, other = lax.rem(me + step_c, count), lax.rem(mine + step_h, groups)
        pl.semaphore_signal(barrier, 1, device_id=(peer, other), device_id_type=mesh_id)
    pl.semaphore_wait(barrier, len(peers))
    local_rows = pltpu.make_async_copy(rows_ref.at[me], rows_in.at[me], local_sems.at[0])
    local_long = pltpu.make_async_copy(long_ref.at[me], long_in.at[me, mine], local_sems.at[1])
    local_rows.start()
    local_long.start()
    copies = []
    for step in range(1, count):
        peer = lax.rem(me + step, count)
        copy = pltpu.make_async_remote_copy(
            src_ref=rows_ref.at[peer],
            dst_ref=rows_in.at[me],
            send_sem=rows_send.at[peer],
            recv_sem=rows_recv.at[me],
            device_id=(peer, mine),
            device_id_type=mesh_id,
        )
        copy.start()
        copies.append(copy)
    for step_c, step_h in peers:
        peer, other = lax.rem(me + step_c, count), lax.rem(mine + step_h, groups)
        copy = pltpu.make_async_remote_copy(
            src_ref=long_ref.at[peer],
            dst_ref=long_in.at[me, mine],
            send_sem=long_send.at[peer * groups + other],
            recv_sem=long_recv.at[me * groups + mine],
            device_id=(peer, other),
            device_id_type=mesh_id,
        )
        copy.start()
        copies.append(copy)
    local_rows.wait()
    local_long.wait()
    for copy in copies:
        copy.wait_send()
    for step in range(1, count):
        source = lax.rem(me + step, count)
        pltpu.make_async_remote_copy(
            src_ref=rows_ref.at[source],
            dst_ref=rows_in.at[source],
            send_sem=rows_send.at[source],
            recv_sem=rows_recv.at[source],
            device_id=(source, mine),
            device_id_type=mesh_id,
        ).wait_recv()
    for step_c, step_h in peers:
        source, other = lax.rem(me + step_c, count), lax.rem(mine + step_h, groups)
        pltpu.make_async_remote_copy(
            src_ref=long_ref.at[source],
            dst_ref=long_in.at[source, other],
            send_sem=long_send.at[source * groups + other],
            recv_sem=long_recv.at[source * groups + other],
            device_id=(source, other),
            device_id_type=mesh_id,
        ).wait_recv()
    rows_out[...] = rows_in[...]
    long_out[...] = long_in[...]


def gather(rows, longs, groups, collective_id):
    count = rows.shape[0]
    long_shape = (count, groups) + longs.shape[1:]
    vmem = pl.BlockSpec(memory_space=pltpu.VMEM)
    return pl.pallas_call(
        gather_kernel,
        out_shape=(
            jax.ShapeDtypeStruct(rows.shape, rows.dtype),
            jax.ShapeDtypeStruct(long_shape, longs.dtype),
        ),
        in_specs=[vmem, vmem],
        out_specs=(vmem, vmem),
        scratch_shapes=[
            pltpu.VMEM(rows.shape, rows.dtype),
            pltpu.VMEM(long_shape, longs.dtype),
            pltpu.SemaphoreType.DMA((2,)),
            pltpu.SemaphoreType.DMA((count,)),
            pltpu.SemaphoreType.DMA((count,)),
            pltpu.SemaphoreType.DMA((count * groups,)),
            pltpu.SemaphoreType.DMA((count * groups,)),
        ],
        compiler_params=pltpu.CompilerParams(collective_id=collective_id, has_side_effects=True),
    )(rows, longs)


def fused_kernel(
    grad_ref, rev_ref, in_ref, taps_ref, rows_out,
    hankel, toeplitz, grad_buf, rows_buf, ch_in, rows_in, local_sems,
    rows_send, rows_recv, ch_send, ch_recv,
):
    count = rows_buf.shape[0]
    chans, _, block_len = grad_ref.shape
    block_count = count
    sources, lags, _ = rev_ref.shape
    tap_count = taps_ref.shape[0]
    groups = lax.axis_size("ch")
    me = lax.axis_index("ctx")
    mine = lax.axis_index("ch")
    mesh_id = pl.DeviceIdType.MESH
    peers = [(c, 0) for c in range(1, count)] + [(0, h) for h in range(1, groups)]
    barrier = pltpu.get_barrier_semaphore()
    for step_c, step_h in peers:
        peer, other = lax.rem(me + step_c, count), lax.rem(mine + step_h, groups)
        pl.semaphore_signal(barrier, 1, device_id=(peer, other), device_id_type=mesh_id)

    def fill_hankel(lag, carry):
        col = pl.multiple_of(lag * block_len, block_len)
        for g in range(chans):
            hankel[g, :, pl.ds(col, block_len)] = grad_ref[g, pl.ds(lag, block_count), :].astype(
                hankel.dtype
            )
        return carry

    lax.fori_loop(0, lags, fill_hankel, 0)

    def fill_toeplitz(picked):
        def fill(lag, carry):
            row = pl.multiple_of(lag * block_len, block_len)
            for s in picked:
                line = rev_ref[s, pl.ds(lag, 1), :]
                tiled = jnp.broadcast_to(line, (block_len, 2 * block_len))
                skewed = pltpu.roll(tiled, block_len + 1, 1, stride=1, stride_axis=0)
                toeplitz[s, pl.ds(row, block_len), :] = skewed[:, :block_len].astype(
                    toeplitz.dtype
                )
            return carry

        lax.fori_loop(0, lags, fill, 0)

    fill_toeplitz(range(1, sources))

    acc = jnp.dot(hankel[0], toeplitz[1], preferred_element_type=jnp.float32)
    for g in range(1, chans):
        acc = acc + jnp.dot(hankel[g], toeplitz[1 + g], preferred_element_type=jnp.float32)
    ch_in[mine] = acc
    pl.semaphore_wait(barrier, len(peers))
    partials = []
    for step in range(1, groups):
        other = lax.rem(mine + step, groups)
        copy = pltpu.make_async_remote_copy(
            src_ref=ch_in.at[mine],
            dst_ref=ch_in.at[mine],
            send_sem=ch_send.at[other],
            recv_sem=ch_recv.at[mine],
            device_id=(me, other),
            device_id_type=mesh_id,
        )
        copy.start()
        partials.append(copy)
    fill_toeplitz(range(1))

    lane = lax.broadcasted_iota(jnp.int32, (block_count, block_len), 1)
    short_row = jnp.zeros((block_count, block_len), jnp.float32)
    grad_buf[...] = jnp.zeros_like(grad_buf)
    for g in range(chans):
        hidden_grad = jnp.dot(hankel[g], toeplitz[0], preferred_element_type=jnp.float32)
        grad_buf[g, pl.ds(0, block_count), :] = hidden_grad
        following = grad_buf[g, pl.ds(1, block_count), :]
        total = taps_ref[0, g] * hidden_grad
        for offset in range(1, tap_count):
            here = pltpu.roll(hidden_grad, block_len - offset, 1)
            there = pltpu.roll(following, block_len - offset, 1)
            total = total + taps_ref[offset, g] * jnp.where(
                lane >= block_len - offset, there, here
            )
        rows_buf[:, g, :] = total.astype(jnp.bfloat16).astype(jnp.float32)
        current = in_ref[g, pl.ds(1, block_count), :]
        previous = in_ref[g, pl.ds(0, block_count), :]
        for offset in range(tap_count):
            if offset == 0:
                delayed_in = current
            else:
                delayed_in = jnp.where(
                    lane < offset,
                    pltpu.roll(previous, offset, 1),
                    pltpu.roll(current, offset, 1),
                )
            value = jnp.sum(hidden_grad * delayed_in)
            short_row = jnp.where(lane == offset * chans + g, value, short_row)
    rows_buf[:, chans, :] = short_row

    for copy in partials:
        copy.wait_send()
    for step in range(1, groups):
        source = lax.rem(mine + step, groups)
        pltpu.make_async_remote_copy(
            src_ref=ch_in.at[source],
            dst_ref=ch_in.at[source],
            send_sem=ch_send.at[source],
            recv_sem=ch_recv.at[source],
            device_id=(me, source),
            device_id_type=mesh_id,
        ).wait_recv()
    summed = ch_in[0]
    for h in range(1, groups):
        summed = summed + ch_in[h]
    rows_buf[:, chans + 1, :] = summed

    local_rows = pltpu.make_async_copy(rows_buf.at[me], rows_in.at[me], local_sems.at[0])
    local_rows.start()
    copies = []
    for step in range(1, count):
        peer = lax.rem(me + step, count)
        copy = pltpu.make_async_remote_copy(
            src_ref=rows_buf.at[peer],
            dst_ref=rows_in.at[me],
            send_sem=rows_send.at[peer],
            recv_sem=rows_recv.at[me],
            device_id=(peer, mine),
            device_id_type=mesh_id,
        )
        copy.start()
        copies.append(copy)
    local_rows.wait()
    for copy in copies:
        copy.wait_send()
    for step in range(1, count):
        source = lax.rem(me + step, count)
        pltpu.make_async_remote_copy(
            src_ref=rows_buf.at[source],
            dst_ref=rows_in.at[source],
            send_sem=rows_send.at[source],
            recv_sem=rows_recv.at[source],
            device_id=(source, mine),
            device_id_type=mesh_id,
        ).wait_recv()
    rows_out[...] = rows_in[...]


def fused(grad_seq, sources, in_seq, taps, groups, block_len, collective_id):
    chans, total_len = grad_seq.shape
    count = sources.shape[0]
    block_count = total_len // block_len
    grad_pad = jnp.pad(
        grad_seq.astype(jnp.float32).reshape(chans, block_count, block_len),
        ((0, 0), (0, block_count), (0, 0)),
    )
    blocks = sources.reshape(count, block_count, block_len)
    padded = jnp.pad(blocks, ((0, 0), (1, 1), (0, 0)))
    pairs = jnp.concatenate([padded[:, :-1], padded[:, 1:]], axis=2)
    rev = pairs[..., ::-1].astype(jnp.float32)
    in_pad = jnp.pad(in_seq.reshape(chans, block_count, block_len), ((0, 0), (1, 0), (0, 0)))
    lags = block_count + 1
    rows_shape = (block_count, chans + 2, block_len)
    vmem = pl.BlockSpec(memory_space=pltpu.VMEM)
    return pl.pallas_call(
        fused_kernel,
        out_shape=jax.ShapeDtypeStruct(rows_shape, jnp.float32),
        in_specs=[vmem, vmem, vmem, pl.BlockSpec(memory_space=pltpu.SMEM)],
        out_specs=vmem,
        scratch_shapes=[
            pltpu.VMEM((chans, block_count, lags * block_len), jnp.bfloat16),
            pltpu.VMEM((count, lags * block_len, block_len), jnp.bfloat16),
            pltpu.VMEM((chans, block_count + 8, block_len), jnp.float32),
            pltpu.VMEM(rows_shape, jnp.float32),
            pltpu.VMEM((groups, block_count, block_len), jnp.float32),
            pltpu.VMEM(rows_shape, jnp.float32),
            pltpu.SemaphoreType.DMA((1,)),
            pltpu.SemaphoreType.DMA((block_count,)),
            pltpu.SemaphoreType.DMA((block_count,)),
            pltpu.SemaphoreType.DMA((groups,)),
            pltpu.SemaphoreType.DMA((groups,)),
        ],
        compiler_params=pltpu.CompilerParams(
            collective_id=collective_id,
            has_side_effects=True,
            vmem_limit_bytes=48 * 1024 * 1024,
        ),
    )(grad_pad, rev, in_pad, taps)


def per_device(inputs, short_filter, long_filter, grad_out):
    tap_count = short_filter.shape[0]
    filter_count, chan_count, shard_len = inputs.shape
    ctx_count = lax.axis_size("ctx")
    my_index = lax.axis_index("ctx")
    total_len = shard_len * ctx_count
    per_dev = filter_count * chan_count // ctx_count
    per_filter = chan_count // per_dev
    block_len = 128
    block_count = total_len // block_len

    send = jnp.concatenate(
        [
            grad_out.reshape(ctx_count, per_dev, shard_len),
            inputs.reshape(ctx_count, per_dev, shard_len),
            jnp.repeat(long_filter, per_filter, axis=0)[:, None, :],
        ],
        axis=1,
    )
    recv = swap(send, 0)
    seqs = recv.transpose(1, 0, 2).reshape(2 * per_dev + 1, total_len)
    grad_seq = seqs[:per_dev]
    in_seq = seqs[per_dev : 2 * per_dev].astype(jnp.float32)
    filt_seq = seqs[2 * per_dev :]
    taps = short_filter.reshape(tap_count, ctx_count, per_dev)
    taps = lax.dynamic_index_in_dim(taps, my_index, axis=1, keepdims=False)

    hidden = sum(
        (taps[offset][:, None] * delayed(in_seq, offset, total_len) for offset in range(tap_count))
    )
    hidden = hidden.astype(jnp.bfloat16)

    groups = lax.axis_size("ch")
    got = fused(
        grad_seq,
        jnp.concatenate([filt_seq, hidden], axis=0),
        in_seq,
        taps,
        groups,
        block_len,
        1,
    )
    grad_in_out = got[:, :per_dev].reshape(filter_count, chan_count, shard_len)
    grad_in_out = grad_in_out.astype(jnp.bfloat16)
    grad_long_out = got[:, per_dev + 1].reshape(filter_count, per_filter, shard_len).sum(axis=1)
    short_all = got[:, per_dev, : tap_count * per_dev].reshape(ctx_count, tap_count, per_dev)
    grad_short_out = short_all.transpose(1, 0, 2).reshape(tap_count, filter_count, chan_count)
    return (grad_in_out, grad_long_out, grad_short_out)


def solution(mesh):
    in_specs = (P(None, "ch", "ctx"), P(None, None, "ch"), P(None, "ctx"), P(None, "ch", "ctx"))
    out_specs = (P(None, "ch", "ctx"), P(None, "ctx"), P(None, None, "ch"))
    return jax.shard_map(
        per_device, mesh=mesh, in_specs=in_specs, out_specs=out_specs, check_vma=False
    )
```

```python
import jax
import jax.numpy as jnp
from jax import lax
from jax.experimental import pallas as pl
from jax.experimental.pallas import tpu as pltpu
from jax.sharding import PartitionSpec as P


def delayed(values, by, length):
    return jnp.pad(values, ((0, 0), (by, 0)))[:, :length]


def conv_kernel(grad_ref, rev_ref, hidden_ref, long_ref, hankel, toeplitz):
    chans, _, block_len = grad_ref.shape
    block_count = hidden_ref.shape[1]
    sources, lags, _ = rev_ref.shape

    def fill_hankel(lag, carry):
        col = pl.multiple_of(lag * block_len, block_len)
        for g in range(chans):
            hankel[g, :, pl.ds(col, block_len)] = grad_ref[g, pl.ds(lag, block_count), :].astype(
                hankel.dtype
            )
        return carry

    lax.fori_loop(0, lags, fill_hankel, 0)

    def fill_toeplitz(lag, carry):
        row = pl.multiple_of(lag * block_len, block_len)
        for s in range(sources):
            line = rev_ref[s, pl.ds(lag, 1), :]
            tiled = jnp.broadcast_to(line, (block_len, 2 * block_len))
            skewed = pltpu.roll(tiled, block_len + 1, 1, stride=1, stride_axis=0)
            toeplitz[s, pl.ds(row, block_len), :] = skewed[:, :block_len].astype(toeplitz.dtype)
        return carry

    lax.fori_loop(0, lags, fill_toeplitz, 0)

    for g in range(chans):
        hidden_ref[g] = jnp.dot(hankel[g], toeplitz[0], preferred_element_type=jnp.float32)
    acc = jnp.dot(hankel[0], toeplitz[1], preferred_element_type=jnp.float32)
    for g in range(1, chans):
        acc = acc + jnp.dot(hankel[g], toeplitz[1 + g], preferred_element_type=jnp.float32)
    long_ref[...] = acc


def correlate_all(grad_seq, sources, block_len):
    chans, total_len = grad_seq.shape
    count = sources.shape[0]
    block_count = total_len // block_len
    grad_pad = jnp.pad(
        grad_seq.astype(jnp.float32).reshape(chans, block_count, block_len),
        ((0, 0), (0, block_count), (0, 0)),
    )
    blocks = sources.reshape(count, block_count, block_len)
    padded = jnp.pad(blocks, ((0, 0), (1, 1), (0, 0)))
    pairs = jnp.concatenate([padded[:, :-1], padded[:, 1:]], axis=2)
    rev = pairs[..., ::-1].astype(jnp.float32)
    lags = block_count + 1
    hidden, long = pl.pallas_call(
        conv_kernel,
        out_shape=(
            jax.ShapeDtypeStruct((chans, block_count, block_len), jnp.float32),
            jax.ShapeDtypeStruct((block_count, block_len), jnp.float32),
        ),
        scratch_shapes=[
            pltpu.VMEM((chans, block_count, lags * block_len), jnp.bfloat16),
            pltpu.VMEM((count, lags * block_len, block_len), jnp.bfloat16),
        ],
        compiler_params=pltpu.CompilerParams(vmem_limit_bytes=48 * 1024 * 1024),
    )(grad_pad, rev)
    return hidden.reshape(chans, total_len), long.reshape(total_len)


def swap_kernel(send_ref, out_ref, landed, local_sem, send_sem, recv_sem):
    count = send_ref.shape[0]
    me = lax.axis_index("ctx")
    mine = lax.axis_index("ch")
    barrier = pltpu.get_barrier_semaphore()
    for step in range(1, count):
        peer = lax.rem(me + step, count)
        pl.semaphore_signal(
            barrier, 1, device_id=(peer, mine), device_id_type=pl.DeviceIdType.MESH
        )
    pl.semaphore_wait(barrier, count - 1)
    local = pltpu.make_async_copy(send_ref.at[me], landed.at[me], local_sem)
    local.start()
    copies = []
    for step in range(1, count):
        peer = lax.rem(me + step, count)
        copy = pltpu.make_async_remote_copy(
            src_ref=send_ref.at[peer],
            dst_ref=landed.at[me],
            send_sem=send_sem.at[peer],
            recv_sem=recv_sem.at[me],
            device_id=(peer, mine),
            device_id_type=pl.DeviceIdType.MESH,
        )
        copy.start()
        copies.append(copy)
    local.wait()
    for copy in copies:
        copy.wait_send()
    for step in range(1, count):
        source = lax.rem(me + step, count)
        pltpu.make_async_remote_copy(
            src_ref=send_ref.at[source],
            dst_ref=landed.at[source],
            send_sem=send_sem.at[source],
            recv_sem=recv_sem.at[source],
            device_id=(source, mine),
            device_id_type=pl.DeviceIdType.MESH,
        ).wait_recv()
    out_ref[...] = landed[...]


def swap(chunks, collective_id):
    return pl.pallas_call(
        swap_kernel,
        out_shape=jax.ShapeDtypeStruct(chunks.shape, chunks.dtype),
        in_specs=[pl.BlockSpec(memory_space=pltpu.VMEM)],
        out_specs=pl.BlockSpec(memory_space=pltpu.VMEM),
        scratch_shapes=[
            pltpu.VMEM(chunks.shape, chunks.dtype),
            pltpu.SemaphoreType.DMA,
            pltpu.SemaphoreType.DMA((chunks.shape[0],)),
            pltpu.SemaphoreType.DMA((chunks.shape[0],)),
        ],
        compiler_params=pltpu.CompilerParams(collective_id=collective_id, has_side_effects=True),
    )(chunks)


def gather_kernel(
    rows_ref, long_ref, rows_out, long_out, rows_in, long_in, local_sems,
    rows_send, rows_recv, long_send, long_recv,
):
    count = rows_ref.shape[0]
    groups = lax.axis_size("ch")
    me = lax.axis_index("ctx")
    mine = lax.axis_index("ch")
    mesh_id = pl.DeviceIdType.MESH
    peers = [(c, h) for c in range(count) for h in range(groups) if (c, h) != (0, 0)]
    barrier = pltpu.get_barrier_semaphore()
    for step_c, step_h in peers:
        peer, other = lax.rem(me + step_c, count), lax.rem(mine + step_h, groups)
        pl.semaphore_signal(barrier, 1, device_id=(peer, other), device_id_type=mesh_id)
    pl.semaphore_wait(barrier, len(peers))
    local_rows = pltpu.make_async_copy(rows_ref.at[me], rows_in.at[me], local_sems.at[0])
    local_long = pltpu.make_async_copy(long_ref.at[me], long_in.at[me, mine], local_sems.at[1])
    local_rows.start()
    local_long.start()
    copies = []
    for step in range(1, count):
        peer = lax.rem(me + step, count)
        copy = pltpu.make_async_remote_copy(
            src_ref=rows_ref.at[peer],
            dst_ref=rows_in.at[me],
            send_sem=rows_send.at[peer],
            recv_sem=rows_recv.at[me],
            device_id=(peer, mine),
            device_id_type=mesh_id,
        )
        copy.start()
        copies.append(copy)
    for step_c, step_h in peers:
        peer, other = lax.rem(me + step_c, count), lax.rem(mine + step_h, groups)
        copy = pltpu.make_async_remote_copy(
            src_ref=long_ref.at[peer],
            dst_ref=long_in.at[me, mine],
            send_sem=long_send.at[peer * groups + other],
            recv_sem=long_recv.at[me * groups + mine],
            device_id=(peer, other),
            device_id_type=mesh_id,
        )
        copy.start()
        copies.append(copy)
    local_rows.wait()
    local_long.wait()
    for copy in copies:
        copy.wait_send()
    for step in range(1, count):
        source = lax.rem(me + step, count)
        pltpu.make_async_remote_copy(
            src_ref=rows_ref.at[source],
            dst_ref=rows_in.at[source],
            send_sem=rows_send.at[source],
            recv_sem=rows_recv.at[source],
            device_id=(source, mine),
            device_id_type=mesh_id,
        ).wait_recv()
    for step_c, step_h in peers:
        source, other = lax.rem(me + step_c, count), lax.rem(mine + step_h, groups)
        pltpu.make_async_remote_copy(
            src_ref=long_ref.at[source],
            dst_ref=long_in.at[source, other],
            send_sem=long_send.at[source * groups + other],
            recv_sem=long_recv.at[source * groups + other],
            device_id=(source, other),
            device_id_type=mesh_id,
        ).wait_recv()
    rows_out[...] = rows_in[...]
    long_out[...] = long_in[...]


def gather(rows, longs, groups, collective_id):
    count = rows.shape[0]
    long_shape = (count, groups) + longs.shape[1:]
    vmem = pl.BlockSpec(memory_space=pltpu.VMEM)
    return pl.pallas_call(
        gather_kernel,
        out_shape=(
            jax.ShapeDtypeStruct(rows.shape, rows.dtype),
            jax.ShapeDtypeStruct(long_shape, longs.dtype),
        ),
        in_specs=[vmem, vmem],
        out_specs=(vmem, vmem),
        scratch_shapes=[
            pltpu.VMEM(rows.shape, rows.dtype),
            pltpu.VMEM(long_shape, longs.dtype),
            pltpu.SemaphoreType.DMA((2,)),
            pltpu.SemaphoreType.DMA((count,)),
            pltpu.SemaphoreType.DMA((count,)),
            pltpu.SemaphoreType.DMA((count * groups,)),
            pltpu.SemaphoreType.DMA((count * groups,)),
        ],
        compiler_params=pltpu.CompilerParams(collective_id=collective_id, has_side_effects=True),
    )(rows, longs)


def fused_kernel(
    grad_ref, rev_ref, in_ref, taps_ref, rows_out,
    hankel, toeplitz, grad_buf, rows_buf, ch_in, rows_in, local_sems,
    rows_send, rows_recv, ch_send, ch_recv,
):
    count = rows_buf.shape[0]
    chans, _, block_len = grad_ref.shape
    block_count = count
    sources, lags, _ = rev_ref.shape
    tap_count = taps_ref.shape[0]
    groups = lax.axis_size("ch")
    me = lax.axis_index("ctx")
    mine = lax.axis_index("ch")
    mesh_id = pl.DeviceIdType.MESH
    peers = [(c, 0) for c in range(1, count)] + [(0, h) for h in range(1, groups)]
    barrier = pltpu.get_barrier_semaphore()
    for step_c, step_h in peers:
        peer, other = lax.rem(me + step_c, count), lax.rem(mine + step_h, groups)
        pl.semaphore_signal(barrier, 1, device_id=(peer, other), device_id_type=mesh_id)

    def fill_hankel(lag, carry):
        col = pl.multiple_of(lag * block_len, block_len)
        for g in range(chans):
            hankel[g, :, pl.ds(col, block_len)] = grad_ref[g, pl.ds(lag, block_count), :].astype(
                hankel.dtype
            )
        return carry

    lax.fori_loop(0, lags, fill_hankel, 0)

    def fill_toeplitz(picked):
        def fill(lag, carry):
            row = pl.multiple_of(lag * block_len, block_len)
            for s in picked:
                line = rev_ref[s, pl.ds(lag, 1), :]
                tiled = jnp.broadcast_to(line, (block_len, 2 * block_len))
                skewed = pltpu.roll(tiled, block_len + 1, 1, stride=1, stride_axis=0)
                toeplitz[s, pl.ds(row, block_len), :] = skewed[:, :block_len].astype(
                    toeplitz.dtype
                )
            return carry

        lax.fori_loop(0, lags, fill, 0)

    fill_toeplitz(range(1, sources))

    acc = jnp.dot(hankel[0], toeplitz[1], preferred_element_type=jnp.float32)
    for g in range(1, chans):
        acc = acc + jnp.dot(hankel[g], toeplitz[1 + g], preferred_element_type=jnp.float32)
    ch_in[mine] = acc
    pl.semaphore_wait(barrier, len(peers))
    partials = []
    for step in range(1, groups):
        other = lax.rem(mine + step, groups)
        copy = pltpu.make_async_remote_copy(
            src_ref=ch_in.at[mine],
            dst_ref=ch_in.at[mine],
            send_sem=ch_send.at[other],
            recv_sem=ch_recv.at[mine],
            device_id=(me, other),
            device_id_type=mesh_id,
        )
        copy.start()
        partials.append(copy)
    fill_toeplitz(range(1))

    lane = lax.broadcasted_iota(jnp.int32, (block_count, block_len), 1)
    short_row = jnp.zeros((block_count, block_len), jnp.float32)
    grad_buf[...] = jnp.zeros_like(grad_buf)
    for g in range(chans):
        hidden_grad = jnp.dot(hankel[g], toeplitz[0], preferred_element_type=jnp.float32)
        grad_buf[g, pl.ds(0, block_count), :] = hidden_grad
        following = grad_buf[g, pl.ds(1, block_count), :]
        total = taps_ref[0, g] * hidden_grad
        for offset in range(1, tap_count):
            here = pltpu.roll(hidden_grad, block_len - offset, 1)
            there = pltpu.roll(following, block_len - offset, 1)
            total = total + taps_ref[offset, g] * jnp.where(
                lane >= block_len - offset, there, here
            )
        rows_buf[:, g, :] = total.astype(jnp.bfloat16).astype(jnp.float32)
        current = in_ref[g, pl.ds(1, block_count), :]
        previous = in_ref[g, pl.ds(0, block_count), :]
        for offset in range(tap_count):
            if offset == 0:
                delayed_in = current
            else:
                delayed_in = jnp.where(
                    lane < offset,
                    pltpu.roll(previous, offset, 1),
                    pltpu.roll(current, offset, 1),
                )
            value = jnp.sum(hidden_grad * delayed_in)
            short_row = jnp.where(lane == offset * chans + g, value, short_row)
    rows_buf[:, chans, :] = short_row

    for copy in partials:
        copy.wait_send()
    for step in range(1, groups):
        source = lax.rem(mine + step, groups)
        pltpu.make_async_remote_copy(
            src_ref=ch_in.at[source],
            dst_ref=ch_in.at[source],
            send_sem=ch_send.at[source],
            recv_sem=ch_recv.at[source],
            device_id=(me, source),
            device_id_type=mesh_id,
        ).wait_recv()
    summed = ch_in[0]
    for h in range(1, groups):
        summed = summed + ch_in[h]
    rows_buf[:, chans + 1, :] = summed

    local_rows = pltpu.make_async_copy(rows_buf.at[me], rows_in.at[me], local_sems.at[0])
    local_rows.start()
    copies = []
    for step in range(1, count):
        peer = lax.rem(me + step, count)
        copy = pltpu.make_async_remote_copy(
            src_ref=rows_buf.at[peer],
            dst_ref=rows_in.at[me],
            send_sem=rows_send.at[peer],
            recv_sem=rows_recv.at[me],
            device_id=(peer, mine),
            device_id_type=mesh_id,
        )
        copy.start()
        copies.append(copy)
    local_rows.wait()
    for copy in copies:
        copy.wait_send()
    for step in range(1, count):
        source = lax.rem(me + step, count)
        pltpu.make_async_remote_copy(
            src_ref=rows_buf.at[source],
            dst_ref=rows_in.at[source],
            send_sem=rows_send.at[source],
            recv_sem=rows_recv.at[source],
            device_id=(source, mine),
            device_id_type=mesh_id,
        ).wait_recv()
    rows_out[...] = rows_in[...]


def fused(grad_seq, sources, in_seq, taps, groups, block_len, collective_id):
    chans, total_len = grad_seq.shape
    count = sources.shape[0]
    block_count = total_len // block_len
    grad_pad = jnp.pad(
        grad_seq.astype(jnp.float32).reshape(chans, block_count, block_len),
        ((0, 0), (0, block_count), (0, 0)),
    )
    blocks = sources.reshape(count, block_count, block_len)
    padded = jnp.pad(blocks, ((0, 0), (1, 1), (0, 0)))
    pairs = jnp.concatenate([padded[:, :-1], padded[:, 1:]], axis=2)
    rev = pairs[..., ::-1].astype(jnp.float32)
    in_pad = jnp.pad(in_seq.reshape(chans, block_count, block_len), ((0, 0), (1, 0), (0, 0)))
    lags = block_count + 1
    rows_shape = (block_count, chans + 2, block_len)
    vmem = pl.BlockSpec(memory_space=pltpu.VMEM)
    return pl.pallas_call(
        fused_kernel,
        out_shape=jax.ShapeDtypeStruct(rows_shape, jnp.float32),
        in_specs=[vmem, vmem, vmem, pl.BlockSpec(memory_space=pltpu.SMEM)],
        out_specs=vmem,
        scratch_shapes=[
            pltpu.VMEM((chans, block_count, lags * block_len), jnp.bfloat16),
            pltpu.VMEM((count, lags * block_len, block_len), jnp.bfloat16),
            pltpu.VMEM((chans, block_count + 8, block_len), jnp.float32),
            pltpu.VMEM(rows_shape, jnp.float32),
            pltpu.VMEM((groups, block_count, block_len), jnp.float32),
            pltpu.VMEM(rows_shape, jnp.float32),
            pltpu.SemaphoreType.DMA((1,)),
            pltpu.SemaphoreType.DMA((block_count,)),
            pltpu.SemaphoreType.DMA((block_count,)),
            pltpu.SemaphoreType.DMA((groups,)),
            pltpu.SemaphoreType.DMA((groups,)),
        ],
        compiler_params=pltpu.CompilerParams(
            collective_id=collective_id,
            has_side_effects=True,
            vmem_limit_bytes=48 * 1024 * 1024,
        ),
    )(grad_pad, rev, in_pad, taps)


def relay_kernel(send_ref, out_ref, middle, landed, local_sems, first_send, first_recv, second_send, second_recv):
    inner, outer = send_ref.shape[0], send_ref.shape[1]
    me = lax.axis_index("ctx")
    mine = lax.axis_index("ch")
    row, col = me // inner, lax.rem(me, inner)
    mesh_id = pl.DeviceIdType.MESH
    barrier = pltpu.get_barrier_semaphore()
    for step in range(1, inner):
        peer = row * inner + lax.rem(col + step, inner)
        pl.semaphore_signal(barrier, 1, device_id=(peer, mine), device_id_type=mesh_id)
    for step in range(1, outer):
        peer = lax.rem(row + step, outer) * inner + col
        pl.semaphore_signal(barrier, 1, device_id=(peer, mine), device_id_type=mesh_id)
    pl.semaphore_wait(barrier, inner - 1 + outer - 1)
    local = pltpu.make_async_copy(send_ref.at[col], middle.at[:, col], local_sems.at[0])
    local.start()
    copies = []
    for step in range(1, inner):
        target = lax.rem(col + step, inner)
        copy = pltpu.make_async_remote_copy(
            src_ref=send_ref.at[target],
            dst_ref=middle.at[:, col],
            send_sem=first_send.at[target],
            recv_sem=first_recv.at[col],
            device_id=(row * inner + target, mine),
            device_id_type=mesh_id,
        )
        copy.start()
        copies.append(copy)
    local.wait()
    for copy in copies:
        copy.wait_send()
    for step in range(1, inner):
        source = lax.rem(col + step, inner)
        pltpu.make_async_remote_copy(
            src_ref=send_ref.at[source],
            dst_ref=middle.at[:, source],
            send_sem=first_send.at[source],
            recv_sem=first_recv.at[source],
            device_id=(row * inner + source, mine),
            device_id_type=mesh_id,
        ).wait_recv()
    local = pltpu.make_async_copy(middle.at[row], landed.at[row], local_sems.at[1])
    local.start()
    copies = []
    for step in range(1, outer):
        target = lax.rem(row + step, outer)
        copy = pltpu.make_async_remote_copy(
            src_ref=middle.at[target],
            dst_ref=landed.at[row],
            send_sem=second_send.at[target],
            recv_sem=second_recv.at[row],
            device_id=(target * inner + col, mine),
            device_id_type=mesh_id,
        )
        copy.start()
        copies.append(copy)
    local.wait()
    for copy in copies:
        copy.wait_send()
    for step in range(1, outer):
        source = lax.rem(row + step, outer)
        pltpu.make_async_remote_copy(
            src_ref=middle.at[source],
            dst_ref=landed.at[source],
            send_sem=second_send.at[source],
            recv_sem=second_recv.at[source],
            device_id=(source * inner + col, mine),
            device_id_type=mesh_id,
        ).wait_recv()
    out_ref[...] = landed[...]


def relay(chunks, inner, collective_id):
    count = chunks.shape[0]
    outer = count // inner
    rest = chunks.shape[1:]
    by_inner = chunks.reshape((outer, inner) + rest).swapaxes(0, 1)
    grid_shape = (outer, inner) + rest
    landed = pl.pallas_call(
        relay_kernel,
        out_shape=jax.ShapeDtypeStruct(grid_shape, chunks.dtype),
        in_specs=[pl.BlockSpec(memory_space=pltpu.VMEM)],
        out_specs=pl.BlockSpec(memory_space=pltpu.VMEM),
        scratch_shapes=[
            pltpu.VMEM(grid_shape, chunks.dtype),
            pltpu.VMEM(grid_shape, chunks.dtype),
            pltpu.SemaphoreType.DMA((2,)),
            pltpu.SemaphoreType.DMA((inner,)),
            pltpu.SemaphoreType.DMA((inner,)),
            pltpu.SemaphoreType.DMA((outer,)),
            pltpu.SemaphoreType.DMA((outer,)),
        ],
        compiler_params=pltpu.CompilerParams(collective_id=collective_id, has_side_effects=True),
    )(by_inner)
    return landed.reshape(chunks.shape)


def per_device(inputs, short_filter, long_filter, grad_out):
    tap_count = short_filter.shape[0]
    filter_count, chan_count, shard_len = inputs.shape
    ctx_count = lax.axis_size("ctx")
    my_index = lax.axis_index("ctx")
    total_len = shard_len * ctx_count
    per_dev = filter_count * chan_count // ctx_count
    per_filter = chan_count // per_dev
    block_len = 128
    block_count = total_len // block_len

    send = jnp.concatenate(
        [
            grad_out.reshape(ctx_count, per_dev, shard_len),
            inputs.reshape(ctx_count, per_dev, shard_len),
            jnp.repeat(long_filter, per_filter, axis=0)[:, None, :],
        ],
        axis=1,
    )
    recv = relay(send, 8, 0)
    seqs = recv.transpose(1, 0, 2).reshape(2 * per_dev + 1, total_len)
    grad_seq = seqs[:per_dev]
    in_seq = seqs[per_dev : 2 * per_dev].astype(jnp.float32)
    filt_seq = seqs[2 * per_dev :]
    taps = short_filter.reshape(tap_count, ctx_count, per_dev)
    taps = lax.dynamic_index_in_dim(taps, my_index, axis=1, keepdims=False)

    hidden = sum(
        (taps[offset][:, None] * delayed(in_seq, offset, total_len) for offset in range(tap_count))
    )
    hidden = hidden.astype(jnp.bfloat16)

    groups = lax.axis_size("ch")
    got = fused(
        grad_seq,
        jnp.concatenate([filt_seq, hidden], axis=0),
        in_seq,
        taps,
        groups,
        block_len,
        1,
    )
    grad_in_out = got[:, :per_dev].reshape(filter_count, chan_count, shard_len)
    grad_in_out = grad_in_out.astype(jnp.bfloat16)
    grad_long_out = got[:, per_dev + 1].reshape(filter_count, per_filter, shard_len).sum(axis=1)
    short_all = got[:, per_dev, : tap_count * per_dev].reshape(ctx_count, tap_count, per_dev)
    grad_short_out = short_all.transpose(1, 0, 2).reshape(tap_count, filter_count, chan_count)
    return (grad_in_out, grad_long_out, grad_short_out)


def solution(mesh):
    in_specs = (P(None, "ch", "ctx"), P(None, None, "ch"), P(None, "ctx"), P(None, "ch", "ctx"))
    out_specs = (P(None, "ch", "ctx"), P(None, "ctx"), P(None, None, "ch"))
    return jax.shard_map(
        per_device, mesh=mesh, in_specs=in_specs, out_specs=out_specs, check_vma=False
    )
```

```python
import jax
import jax.numpy as jnp
from jax import lax
from jax.experimental import pallas as pl
from jax.experimental.pallas import tpu as pltpu
from jax.sharding import PartitionSpec as P


def delayed(values, by, length):
    return jnp.pad(values, ((0, 0), (by, 0)))[:, :length]


def conv_kernel(grad_ref, rev_ref, hidden_ref, long_ref, hankel, toeplitz):
    chans, _, block_len = grad_ref.shape
    block_count = hidden_ref.shape[1]
    sources, lags, _ = rev_ref.shape

    def fill_hankel(lag, carry):
        col = pl.multiple_of(lag * block_len, block_len)
        for g in range(chans):
            hankel[g, :, pl.ds(col, block_len)] = grad_ref[g, pl.ds(lag, block_count), :].astype(
                hankel.dtype
            )
        return carry

    lax.fori_loop(0, lags, fill_hankel, 0)

    def fill_toeplitz(lag, carry):
        row = pl.multiple_of(lag * block_len, block_len)
        for s in range(sources):
            line = rev_ref[s, pl.ds(lag, 1), :]
            tiled = jnp.broadcast_to(line, (block_len, 2 * block_len))
            skewed = pltpu.roll(tiled, block_len + 1, 1, stride=1, stride_axis=0)
            toeplitz[s, pl.ds(row, block_len), :] = skewed[:, :block_len].astype(toeplitz.dtype)
        return carry

    lax.fori_loop(0, lags, fill_toeplitz, 0)

    for g in range(chans):
        hidden_ref[g] = jnp.dot(hankel[g], toeplitz[0], preferred_element_type=jnp.float32)
    acc = jnp.dot(hankel[0], toeplitz[1], preferred_element_type=jnp.float32)
    for g in range(1, chans):
        acc = acc + jnp.dot(hankel[g], toeplitz[1 + g], preferred_element_type=jnp.float32)
    long_ref[...] = acc


def correlate_all(grad_seq, sources, block_len):
    chans, total_len = grad_seq.shape
    count = sources.shape[0]
    block_count = total_len // block_len
    grad_pad = jnp.pad(
        grad_seq.astype(jnp.float32).reshape(chans, block_count, block_len),
        ((0, 0), (0, block_count), (0, 0)),
    )
    blocks = sources.reshape(count, block_count, block_len)
    padded = jnp.pad(blocks, ((0, 0), (1, 1), (0, 0)))
    pairs = jnp.concatenate([padded[:, :-1], padded[:, 1:]], axis=2)
    rev = pairs[..., ::-1].astype(jnp.float32)
    lags = block_count + 1
    hidden, long = pl.pallas_call(
        conv_kernel,
        out_shape=(
            jax.ShapeDtypeStruct((chans, block_count, block_len), jnp.float32),
            jax.ShapeDtypeStruct((block_count, block_len), jnp.float32),
        ),
        scratch_shapes=[
            pltpu.VMEM((chans, block_count, lags * block_len), jnp.bfloat16),
            pltpu.VMEM((count, lags * block_len, block_len), jnp.bfloat16),
        ],
        compiler_params=pltpu.CompilerParams(vmem_limit_bytes=48 * 1024 * 1024),
    )(grad_pad, rev)
    return hidden.reshape(chans, total_len), long.reshape(total_len)


def swap_kernel(send_ref, out_ref, landed, local_sem, send_sem, recv_sem):
    count = send_ref.shape[0]
    me = lax.axis_index("ctx")
    mine = lax.axis_index("ch")
    barrier = pltpu.get_barrier_semaphore()
    for step in range(1, count):
        peer = lax.rem(me + step, count)
        pl.semaphore_signal(
            barrier, 1, device_id=(peer, mine), device_id_type=pl.DeviceIdType.MESH
        )
    pl.semaphore_wait(barrier, count - 1)
    local = pltpu.make_async_copy(send_ref.at[me], landed.at[me], local_sem)
    local.start()
    copies = []
    for step in range(1, count):
        peer = lax.rem(me + step, count)
        copy = pltpu.make_async_remote_copy(
            src_ref=send_ref.at[peer],
            dst_ref=landed.at[me],
            send_sem=send_sem.at[peer],
            recv_sem=recv_sem.at[me],
            device_id=(peer, mine),
            device_id_type=pl.DeviceIdType.MESH,
        )
        copy.start()
        copies.append(copy)
    local.wait()
    for copy in copies:
        copy.wait_send()
    for step in range(1, count):
        source = lax.rem(me + step, count)
        pltpu.make_async_remote_copy(
            src_ref=send_ref.at[source],
            dst_ref=landed.at[source],
            send_sem=send_sem.at[source],
            recv_sem=recv_sem.at[source],
            device_id=(source, mine),
            device_id_type=pl.DeviceIdType.MESH,
        ).wait_recv()
    out_ref[...] = landed[...]


def swap(chunks, collective_id):
    return pl.pallas_call(
        swap_kernel,
        out_shape=jax.ShapeDtypeStruct(chunks.shape, chunks.dtype),
        in_specs=[pl.BlockSpec(memory_space=pltpu.VMEM)],
        out_specs=pl.BlockSpec(memory_space=pltpu.VMEM),
        scratch_shapes=[
            pltpu.VMEM(chunks.shape, chunks.dtype),
            pltpu.SemaphoreType.DMA,
            pltpu.SemaphoreType.DMA((chunks.shape[0],)),
            pltpu.SemaphoreType.DMA((chunks.shape[0],)),
        ],
        compiler_params=pltpu.CompilerParams(collective_id=collective_id, has_side_effects=True),
    )(chunks)


def gather_kernel(
    rows_ref, long_ref, rows_out, long_out, rows_in, long_in, local_sems,
    rows_send, rows_recv, long_send, long_recv,
):
    count = rows_ref.shape[0]
    groups = lax.axis_size("ch")
    me = lax.axis_index("ctx")
    mine = lax.axis_index("ch")
    mesh_id = pl.DeviceIdType.MESH
    peers = [(c, h) for c in range(count) for h in range(groups) if (c, h) != (0, 0)]
    barrier = pltpu.get_barrier_semaphore()
    for step_c, step_h in peers:
        peer, other = lax.rem(me + step_c, count), lax.rem(mine + step_h, groups)
        pl.semaphore_signal(barrier, 1, device_id=(peer, other), device_id_type=mesh_id)
    pl.semaphore_wait(barrier, len(peers))
    local_rows = pltpu.make_async_copy(rows_ref.at[me], rows_in.at[me], local_sems.at[0])
    local_long = pltpu.make_async_copy(long_ref.at[me], long_in.at[me, mine], local_sems.at[1])
    local_rows.start()
    local_long.start()
    copies = []
    for step in range(1, count):
        peer = lax.rem(me + step, count)
        copy = pltpu.make_async_remote_copy(
            src_ref=rows_ref.at[peer],
            dst_ref=rows_in.at[me],
            send_sem=rows_send.at[peer],
            recv_sem=rows_recv.at[me],
            device_id=(peer, mine),
            device_id_type=mesh_id,
        )
        copy.start()
        copies.append(copy)
    for step_c, step_h in peers:
        peer, other = lax.rem(me + step_c, count), lax.rem(mine + step_h, groups)
        copy = pltpu.make_async_remote_copy(
            src_ref=long_ref.at[peer],
            dst_ref=long_in.at[me, mine],
            send_sem=long_send.at[peer * groups + other],
            recv_sem=long_recv.at[me * groups + mine],
            device_id=(peer, other),
            device_id_type=mesh_id,
        )
        copy.start()
        copies.append(copy)
    local_rows.wait()
    local_long.wait()
    for copy in copies:
        copy.wait_send()
    for step in range(1, count):
        source = lax.rem(me + step, count)
        pltpu.make_async_remote_copy(
            src_ref=rows_ref.at[source],
            dst_ref=rows_in.at[source],
            send_sem=rows_send.at[source],
            recv_sem=rows_recv.at[source],
            device_id=(source, mine),
            device_id_type=mesh_id,
        ).wait_recv()
    for step_c, step_h in peers:
        source, other = lax.rem(me + step_c, count), lax.rem(mine + step_h, groups)
        pltpu.make_async_remote_copy(
            src_ref=long_ref.at[source],
            dst_ref=long_in.at[source, other],
            send_sem=long_send.at[source * groups + other],
            recv_sem=long_recv.at[source * groups + other],
            device_id=(source, other),
            device_id_type=mesh_id,
        ).wait_recv()
    rows_out[...] = rows_in[...]
    long_out[...] = long_in[...]


def gather(rows, longs, groups, collective_id):
    count = rows.shape[0]
    long_shape = (count, groups) + longs.shape[1:]
    vmem = pl.BlockSpec(memory_space=pltpu.VMEM)
    return pl.pallas_call(
        gather_kernel,
        out_shape=(
            jax.ShapeDtypeStruct(rows.shape, rows.dtype),
            jax.ShapeDtypeStruct(long_shape, longs.dtype),
        ),
        in_specs=[vmem, vmem],
        out_specs=(vmem, vmem),
        scratch_shapes=[
            pltpu.VMEM(rows.shape, rows.dtype),
            pltpu.VMEM(long_shape, longs.dtype),
            pltpu.SemaphoreType.DMA((2,)),
            pltpu.SemaphoreType.DMA((count,)),
            pltpu.SemaphoreType.DMA((count,)),
            pltpu.SemaphoreType.DMA((count * groups,)),
            pltpu.SemaphoreType.DMA((count * groups,)),
        ],
        compiler_params=pltpu.CompilerParams(collective_id=collective_id, has_side_effects=True),
    )(rows, longs)


def fused_kernel(
    grad_ref, rev_ref, in_ref, taps_ref, rows_out,
    hankel, toeplitz, grad_buf, rows_buf, ch_in, middle, rows_in, local_sems,
    first_send, first_recv, second_send, second_recv, ch_send, ch_recv,
):
    outer, inner = rows_buf.shape[0], rows_buf.shape[1]
    count = outer * inner
    chans, _, block_len = grad_ref.shape
    block_count = count
    sources, lags, _ = rev_ref.shape
    tap_count = taps_ref.shape[0]
    groups = lax.axis_size("ch")
    me = lax.axis_index("ctx")
    mine = lax.axis_index("ch")
    mesh_id = pl.DeviceIdType.MESH
    row, col = me // inner, lax.rem(me, inner)
    peers = [(row * inner + lax.rem(col + step, inner), mine) for step in range(1, inner)]
    peers += [(lax.rem(row + step, outer) * inner + col, mine) for step in range(1, outer)]
    peers += [(me, lax.rem(mine + step, groups)) for step in range(1, groups)]
    barrier = pltpu.get_barrier_semaphore()
    for peer, other in peers:
        pl.semaphore_signal(barrier, 1, device_id=(peer, other), device_id_type=mesh_id)

    def fill_hankel(lag, carry):
        col = pl.multiple_of(lag * block_len, block_len)
        for g in range(chans):
            hankel[g, :, pl.ds(col, block_len)] = grad_ref[g, pl.ds(lag, block_count), :].astype(
                hankel.dtype
            )
        return carry

    lax.fori_loop(0, lags, fill_hankel, 0)

    def fill_toeplitz(picked):
        def fill(lag, carry):
            row = pl.multiple_of(lag * block_len, block_len)
            for s in picked:
                line = rev_ref[s, pl.ds(lag, 1), :]
                tiled = jnp.broadcast_to(line, (block_len, 2 * block_len))
                skewed = pltpu.roll(tiled, block_len + 1, 1, stride=1, stride_axis=0)
                toeplitz[s, pl.ds(row, block_len), :] = skewed[:, :block_len].astype(
                    toeplitz.dtype
                )
            return carry

        lax.fori_loop(0, lags, fill, 0)

    fill_toeplitz(range(1, sources))

    acc = jnp.dot(hankel[0], toeplitz[1], preferred_element_type=jnp.float32)
    for g in range(1, chans):
        acc = acc + jnp.dot(hankel[g], toeplitz[1 + g], preferred_element_type=jnp.float32)
    ch_in[mine] = acc
    pl.semaphore_wait(barrier, len(peers))
    partials = []
    for step in range(1, groups):
        other = lax.rem(mine + step, groups)
        copy = pltpu.make_async_remote_copy(
            src_ref=ch_in.at[mine],
            dst_ref=ch_in.at[mine],
            send_sem=ch_send.at[other],
            recv_sem=ch_recv.at[mine],
            device_id=(me, other),
            device_id_type=mesh_id,
        )
        copy.start()
        partials.append(copy)
    fill_toeplitz(range(1))

    lane = lax.broadcasted_iota(jnp.int32, (block_count, block_len), 1)
    short_row = jnp.zeros((block_count, block_len), jnp.float32)
    grad_buf[...] = jnp.zeros_like(grad_buf)
    for g in range(chans):
        hidden_grad = jnp.dot(hankel[g], toeplitz[0], preferred_element_type=jnp.float32)
        grad_buf[g, pl.ds(0, block_count), :] = hidden_grad
        following = grad_buf[g, pl.ds(1, block_count), :]
        total = taps_ref[0, g] * hidden_grad
        for offset in range(1, tap_count):
            here = pltpu.roll(hidden_grad, block_len - offset, 1)
            there = pltpu.roll(following, block_len - offset, 1)
            total = total + taps_ref[offset, g] * jnp.where(
                lane >= block_len - offset, there, here
            )
        rows_buf[:, :, g, :] = (
            total.astype(jnp.bfloat16).astype(jnp.float32).reshape(outer, inner, block_len)
        )
        current = in_ref[g, pl.ds(1, block_count), :]
        previous = in_ref[g, pl.ds(0, block_count), :]
        for offset in range(tap_count):
            if offset == 0:
                delayed_in = current
            else:
                delayed_in = jnp.where(
                    lane < offset,
                    pltpu.roll(previous, offset, 1),
                    pltpu.roll(current, offset, 1),
                )
            value = jnp.sum(hidden_grad * delayed_in)
            short_row = jnp.where(lane == offset * chans + g, value, short_row)
    rows_buf[:, :, chans, :] = short_row.reshape(outer, inner, block_len)

    for copy in partials:
        copy.wait_send()
    for step in range(1, groups):
        source = lax.rem(mine + step, groups)
        pltpu.make_async_remote_copy(
            src_ref=ch_in.at[source],
            dst_ref=ch_in.at[source],
            send_sem=ch_send.at[source],
            recv_sem=ch_recv.at[source],
            device_id=(me, source),
            device_id_type=mesh_id,
        ).wait_recv()
    summed = ch_in[0]
    for h in range(1, groups):
        summed = summed + ch_in[h]
    rows_buf[:, :, chans + 1, :] = summed.reshape(outer, inner, block_len)

    local = pltpu.make_async_copy(rows_buf.at[:, col], middle.at[:, col], local_sems.at[0])
    local.start()
    copies = []
    for step in range(1, inner):
        target = lax.rem(col + step, inner)
        copy = pltpu.make_async_remote_copy(
            src_ref=rows_buf.at[:, target],
            dst_ref=middle.at[:, col],
            send_sem=first_send.at[target],
            recv_sem=first_recv.at[col],
            device_id=(row * inner + target, mine),
            device_id_type=mesh_id,
        )
        copy.start()
        copies.append(copy)
    local.wait()
    for copy in copies:
        copy.wait_send()
    for step in range(1, inner):
        source = lax.rem(col + step, inner)
        pltpu.make_async_remote_copy(
            src_ref=rows_buf.at[:, source],
            dst_ref=middle.at[:, source],
            send_sem=first_send.at[source],
            recv_sem=first_recv.at[source],
            device_id=(row * inner + source, mine),
            device_id_type=mesh_id,
        ).wait_recv()
    local = pltpu.make_async_copy(middle.at[row], rows_in.at[row], local_sems.at[1])
    local.start()
    copies = []
    for step in range(1, outer):
        target = lax.rem(row + step, outer)
        copy = pltpu.make_async_remote_copy(
            src_ref=middle.at[target],
            dst_ref=rows_in.at[row],
            send_sem=second_send.at[target],
            recv_sem=second_recv.at[row],
            device_id=(target * inner + col, mine),
            device_id_type=mesh_id,
        )
        copy.start()
        copies.append(copy)
    local.wait()
    for copy in copies:
        copy.wait_send()
    for step in range(1, outer):
        source = lax.rem(row + step, outer)
        pltpu.make_async_remote_copy(
            src_ref=middle.at[source],
            dst_ref=rows_in.at[source],
            send_sem=second_send.at[source],
            recv_sem=second_recv.at[source],
            device_id=(source * inner + col, mine),
            device_id_type=mesh_id,
        ).wait_recv()
    rows_out[...] = rows_in[...]


def fused(grad_seq, sources, in_seq, taps, groups, inner, block_len, collective_id):
    chans, total_len = grad_seq.shape
    count = sources.shape[0]
    block_count = total_len // block_len
    grad_pad = jnp.pad(
        grad_seq.astype(jnp.float32).reshape(chans, block_count, block_len),
        ((0, 0), (0, block_count), (0, 0)),
    )
    blocks = sources.reshape(count, block_count, block_len)
    padded = jnp.pad(blocks, ((0, 0), (1, 1), (0, 0)))
    pairs = jnp.concatenate([padded[:, :-1], padded[:, 1:]], axis=2)
    rev = pairs[..., ::-1].astype(jnp.float32)
    in_pad = jnp.pad(in_seq.reshape(chans, block_count, block_len), ((0, 0), (1, 0), (0, 0)))
    lags = block_count + 1
    outer = block_count // inner
    rows_shape = (outer, inner, chans + 2, block_len)
    vmem = pl.BlockSpec(memory_space=pltpu.VMEM)
    return pl.pallas_call(
        fused_kernel,
        out_shape=jax.ShapeDtypeStruct(rows_shape, jnp.float32),
        in_specs=[vmem, vmem, vmem, pl.BlockSpec(memory_space=pltpu.SMEM)],
        out_specs=vmem,
        scratch_shapes=[
            pltpu.VMEM((chans, block_count, lags * block_len), jnp.bfloat16),
            pltpu.VMEM((count, lags * block_len, block_len), jnp.bfloat16),
            pltpu.VMEM((chans, block_count + 8, block_len), jnp.float32),
            pltpu.VMEM(rows_shape, jnp.float32),
            pltpu.VMEM((groups, block_count, block_len), jnp.float32),
            pltpu.VMEM(rows_shape, jnp.float32),
            pltpu.VMEM(rows_shape, jnp.float32),
            pltpu.SemaphoreType.DMA((2,)),
            pltpu.SemaphoreType.DMA((inner,)),
            pltpu.SemaphoreType.DMA((inner,)),
            pltpu.SemaphoreType.DMA((outer,)),
            pltpu.SemaphoreType.DMA((outer,)),
            pltpu.SemaphoreType.DMA((groups,)),
            pltpu.SemaphoreType.DMA((groups,)),
        ],
        compiler_params=pltpu.CompilerParams(
            collective_id=collective_id,
            has_side_effects=True,
            vmem_limit_bytes=48 * 1024 * 1024,
        ),
    )(grad_pad, rev, in_pad, taps).reshape((block_count,) + rows_shape[2:])


def relay_kernel(send_ref, out_ref, middle, landed, local_sems, first_send, first_recv, second_send, second_recv):
    inner, outer = send_ref.shape[0], send_ref.shape[1]
    me = lax.axis_index("ctx")
    mine = lax.axis_index("ch")
    row, col = me // inner, lax.rem(me, inner)
    mesh_id = pl.DeviceIdType.MESH
    barrier = pltpu.get_barrier_semaphore()
    for step in range(1, inner):
        peer = row * inner + lax.rem(col + step, inner)
        pl.semaphore_signal(barrier, 1, device_id=(peer, mine), device_id_type=mesh_id)
    for step in range(1, outer):
        peer = lax.rem(row + step, outer) * inner + col
        pl.semaphore_signal(barrier, 1, device_id=(peer, mine), device_id_type=mesh_id)
    pl.semaphore_wait(barrier, inner - 1 + outer - 1)
    local = pltpu.make_async_copy(send_ref.at[col], middle.at[:, col], local_sems.at[0])
    local.start()
    copies = []
    for step in range(1, inner):
        target = lax.rem(col + step, inner)
        copy = pltpu.make_async_remote_copy(
            src_ref=send_ref.at[target],
            dst_ref=middle.at[:, col],
            send_sem=first_send.at[target],
            recv_sem=first_recv.at[col],
            device_id=(row * inner + target, mine),
            device_id_type=mesh_id,
        )
        copy.start()
        copies.append(copy)
    local.wait()
    for copy in copies:
        copy.wait_send()
    for step in range(1, inner):
        source = lax.rem(col + step, inner)
        pltpu.make_async_remote_copy(
            src_ref=send_ref.at[source],
            dst_ref=middle.at[:, source],
            send_sem=first_send.at[source],
            recv_sem=first_recv.at[source],
            device_id=(row * inner + source, mine),
            device_id_type=mesh_id,
        ).wait_recv()
    local = pltpu.make_async_copy(middle.at[row], landed.at[row], local_sems.at[1])
    local.start()
    copies = []
    for step in range(1, outer):
        target = lax.rem(row + step, outer)
        copy = pltpu.make_async_remote_copy(
            src_ref=middle.at[target],
            dst_ref=landed.at[row],
            send_sem=second_send.at[target],
            recv_sem=second_recv.at[row],
            device_id=(target * inner + col, mine),
            device_id_type=mesh_id,
        )
        copy.start()
        copies.append(copy)
    local.wait()
    for copy in copies:
        copy.wait_send()
    for step in range(1, outer):
        source = lax.rem(row + step, outer)
        pltpu.make_async_remote_copy(
            src_ref=middle.at[source],
            dst_ref=landed.at[source],
            send_sem=second_send.at[source],
            recv_sem=second_recv.at[source],
            device_id=(source * inner + col, mine),
            device_id_type=mesh_id,
        ).wait_recv()
    out_ref[...] = landed[...]


def relay(chunks, inner, collective_id):
    count = chunks.shape[0]
    outer = count // inner
    rest = chunks.shape[1:]
    by_inner = chunks.reshape((outer, inner) + rest).swapaxes(0, 1)
    grid_shape = (outer, inner) + rest
    landed = pl.pallas_call(
        relay_kernel,
        out_shape=jax.ShapeDtypeStruct(grid_shape, chunks.dtype),
        in_specs=[pl.BlockSpec(memory_space=pltpu.VMEM)],
        out_specs=pl.BlockSpec(memory_space=pltpu.VMEM),
        scratch_shapes=[
            pltpu.VMEM(grid_shape, chunks.dtype),
            pltpu.VMEM(grid_shape, chunks.dtype),
            pltpu.SemaphoreType.DMA((2,)),
            pltpu.SemaphoreType.DMA((inner,)),
            pltpu.SemaphoreType.DMA((inner,)),
            pltpu.SemaphoreType.DMA((outer,)),
            pltpu.SemaphoreType.DMA((outer,)),
        ],
        compiler_params=pltpu.CompilerParams(collective_id=collective_id, has_side_effects=True),
    )(by_inner)
    return landed.reshape(chunks.shape)


def per_device(inputs, short_filter, long_filter, grad_out):
    tap_count = short_filter.shape[0]
    filter_count, chan_count, shard_len = inputs.shape
    ctx_count = lax.axis_size("ctx")
    my_index = lax.axis_index("ctx")
    total_len = shard_len * ctx_count
    per_dev = filter_count * chan_count // ctx_count
    per_filter = chan_count // per_dev
    block_len = 128
    block_count = total_len // block_len

    send = jnp.concatenate(
        [
            grad_out.reshape(ctx_count, per_dev, shard_len),
            inputs.reshape(ctx_count, per_dev, shard_len),
            jnp.repeat(long_filter, per_filter, axis=0)[:, None, :],
        ],
        axis=1,
    )
    recv = relay(send, 8, 0)
    seqs = recv.transpose(1, 0, 2).reshape(2 * per_dev + 1, total_len)
    grad_seq = seqs[:per_dev]
    in_seq = seqs[per_dev : 2 * per_dev].astype(jnp.float32)
    filt_seq = seqs[2 * per_dev :]
    taps = short_filter.reshape(tap_count, ctx_count, per_dev)
    taps = lax.dynamic_index_in_dim(taps, my_index, axis=1, keepdims=False)

    hidden = sum(
        (taps[offset][:, None] * delayed(in_seq, offset, total_len) for offset in range(tap_count))
    )
    hidden = hidden.astype(jnp.bfloat16)

    groups = lax.axis_size("ch")
    got = fused(
        grad_seq,
        jnp.concatenate([filt_seq, hidden], axis=0),
        in_seq,
        taps,
        groups,
        8,
        block_len,
        1,
    )
    grad_in_out = got[:, :per_dev].reshape(filter_count, chan_count, shard_len)
    grad_in_out = grad_in_out.astype(jnp.bfloat16)
    grad_long_out = got[:, per_dev + 1].reshape(filter_count, per_filter, shard_len).sum(axis=1)
    short_all = got[:, per_dev, : tap_count * per_dev].reshape(ctx_count, tap_count, per_dev)
    grad_short_out = short_all.transpose(1, 0, 2).reshape(tap_count, filter_count, chan_count)
    return (grad_in_out, grad_long_out, grad_short_out)


def solution(mesh):
    in_specs = (P(None, "ch", "ctx"), P(None, None, "ch"), P(None, "ctx"), P(None, "ch", "ctx"))
    out_specs = (P(None, "ch", "ctx"), P(None, "ctx"), P(None, None, "ch"))
    return jax.shard_map(
        per_device, mesh=mesh, in_specs=in_specs, out_specs=out_specs, check_vma=False
    )
```

```python
import jax
import jax.numpy as jnp
from jax import lax
from jax.experimental import pallas as pl
from jax.experimental.pallas import tpu as pltpu
from jax.sharding import PartitionSpec as P


def delayed(values, by, length):
    return jnp.pad(values, ((0, 0), (by, 0)))[:, :length]


def conv_kernel(grad_ref, rev_ref, hidden_ref, long_ref, hankel, toeplitz):
    chans, _, block_len = grad_ref.shape
    block_count = hidden_ref.shape[1]
    sources, lags, _ = rev_ref.shape

    def fill_hankel(lag, carry):
        col = pl.multiple_of(lag * block_len, block_len)
        for g in range(chans):
            hankel[g, :, pl.ds(col, block_len)] = grad_ref[g, pl.ds(lag, block_count), :].astype(
                hankel.dtype
            )
        return carry

    lax.fori_loop(0, lags, fill_hankel, 0)

    def fill_toeplitz(lag, carry):
        row = pl.multiple_of(lag * block_len, block_len)
        for s in range(sources):
            line = rev_ref[s, pl.ds(lag, 1), :]
            tiled = jnp.broadcast_to(line, (block_len, 2 * block_len))
            skewed = pltpu.roll(tiled, block_len + 1, 1, stride=1, stride_axis=0)
            toeplitz[s, pl.ds(row, block_len), :] = skewed[:, :block_len].astype(toeplitz.dtype)
        return carry

    lax.fori_loop(0, lags, fill_toeplitz, 0)

    for g in range(chans):
        hidden_ref[g] = jnp.dot(hankel[g], toeplitz[0], preferred_element_type=jnp.float32)
    acc = jnp.dot(hankel[0], toeplitz[1], preferred_element_type=jnp.float32)
    for g in range(1, chans):
        acc = acc + jnp.dot(hankel[g], toeplitz[1 + g], preferred_element_type=jnp.float32)
    long_ref[...] = acc


def correlate_all(grad_seq, sources, block_len):
    chans, total_len = grad_seq.shape
    count = sources.shape[0]
    block_count = total_len // block_len
    grad_pad = jnp.pad(
        grad_seq.astype(jnp.float32).reshape(chans, block_count, block_len),
        ((0, 0), (0, block_count), (0, 0)),
    )
    blocks = sources.reshape(count, block_count, block_len)
    padded = jnp.pad(blocks, ((0, 0), (1, 1), (0, 0)))
    pairs = jnp.concatenate([padded[:, :-1], padded[:, 1:]], axis=2)
    rev = pairs[..., ::-1].astype(jnp.float32)
    lags = block_count + 1
    hidden, long = pl.pallas_call(
        conv_kernel,
        out_shape=(
            jax.ShapeDtypeStruct((chans, block_count, block_len), jnp.float32),
            jax.ShapeDtypeStruct((block_count, block_len), jnp.float32),
        ),
        scratch_shapes=[
            pltpu.VMEM((chans, block_count, lags * block_len), jnp.bfloat16),
            pltpu.VMEM((count, lags * block_len, block_len), jnp.bfloat16),
        ],
        compiler_params=pltpu.CompilerParams(vmem_limit_bytes=48 * 1024 * 1024),
    )(grad_pad, rev)
    return hidden.reshape(chans, total_len), long.reshape(total_len)


def swap_kernel(send_ref, out_ref, landed, local_sem, send_sem, recv_sem):
    count = send_ref.shape[0]
    me = lax.axis_index("ctx")
    mine = lax.axis_index("ch")
    barrier = pltpu.get_barrier_semaphore()
    for step in range(1, count):
        peer = lax.rem(me + step, count)
        pl.semaphore_signal(
            barrier, 1, device_id=(peer, mine), device_id_type=pl.DeviceIdType.MESH
        )
    pl.semaphore_wait(barrier, count - 1)
    local = pltpu.make_async_copy(send_ref.at[me], landed.at[me], local_sem)
    local.start()
    copies = []
    for step in range(1, count):
        peer = lax.rem(me + step, count)
        copy = pltpu.make_async_remote_copy(
            src_ref=send_ref.at[peer],
            dst_ref=landed.at[me],
            send_sem=send_sem.at[peer],
            recv_sem=recv_sem.at[me],
            device_id=(peer, mine),
            device_id_type=pl.DeviceIdType.MESH,
        )
        copy.start()
        copies.append(copy)
    local.wait()
    for copy in copies:
        copy.wait_send()
    for step in range(1, count):
        source = lax.rem(me + step, count)
        pltpu.make_async_remote_copy(
            src_ref=send_ref.at[source],
            dst_ref=landed.at[source],
            send_sem=send_sem.at[source],
            recv_sem=recv_sem.at[source],
            device_id=(source, mine),
            device_id_type=pl.DeviceIdType.MESH,
        ).wait_recv()
    out_ref[...] = landed[...]


def swap(chunks, collective_id):
    return pl.pallas_call(
        swap_kernel,
        out_shape=jax.ShapeDtypeStruct(chunks.shape, chunks.dtype),
        in_specs=[pl.BlockSpec(memory_space=pltpu.VMEM)],
        out_specs=pl.BlockSpec(memory_space=pltpu.VMEM),
        scratch_shapes=[
            pltpu.VMEM(chunks.shape, chunks.dtype),
            pltpu.SemaphoreType.DMA,
            pltpu.SemaphoreType.DMA((chunks.shape[0],)),
            pltpu.SemaphoreType.DMA((chunks.shape[0],)),
        ],
        compiler_params=pltpu.CompilerParams(collective_id=collective_id, has_side_effects=True),
    )(chunks)


def gather_kernel(
    rows_ref, long_ref, rows_out, long_out, rows_in, long_in, local_sems,
    rows_send, rows_recv, long_send, long_recv,
):
    count = rows_ref.shape[0]
    groups = lax.axis_size("ch")
    me = lax.axis_index("ctx")
    mine = lax.axis_index("ch")
    mesh_id = pl.DeviceIdType.MESH
    peers = [(c, h) for c in range(count) for h in range(groups) if (c, h) != (0, 0)]
    barrier = pltpu.get_barrier_semaphore()
    for step_c, step_h in peers:
        peer, other = lax.rem(me + step_c, count), lax.rem(mine + step_h, groups)
        pl.semaphore_signal(barrier, 1, device_id=(peer, other), device_id_type=mesh_id)
    pl.semaphore_wait(barrier, len(peers))
    local_rows = pltpu.make_async_copy(rows_ref.at[me], rows_in.at[me], local_sems.at[0])
    local_long = pltpu.make_async_copy(long_ref.at[me], long_in.at[me, mine], local_sems.at[1])
    local_rows.start()
    local_long.start()
    copies = []
    for step in range(1, count):
        peer = lax.rem(me + step, count)
        copy = pltpu.make_async_remote_copy(
            src_ref=rows_ref.at[peer],
            dst_ref=rows_in.at[me],
            send_sem=rows_send.at[peer],
            recv_sem=rows_recv.at[me],
            device_id=(peer, mine),
            device_id_type=mesh_id,
        )
        copy.start()
        copies.append(copy)
    for step_c, step_h in peers:
        peer, other = lax.rem(me + step_c, count), lax.rem(mine + step_h, groups)
        copy = pltpu.make_async_remote_copy(
            src_ref=long_ref.at[peer],
            dst_ref=long_in.at[me, mine],
            send_sem=long_send.at[peer * groups + other],
            recv_sem=long_recv.at[me * groups + mine],
            device_id=(peer, other),
            device_id_type=mesh_id,
        )
        copy.start()
        copies.append(copy)
    local_rows.wait()
    local_long.wait()
    for copy in copies:
        copy.wait_send()
    for step in range(1, count):
        source = lax.rem(me + step, count)
        pltpu.make_async_remote_copy(
            src_ref=rows_ref.at[source],
            dst_ref=rows_in.at[source],
            send_sem=rows_send.at[source],
            recv_sem=rows_recv.at[source],
            device_id=(source, mine),
            device_id_type=mesh_id,
        ).wait_recv()
    for step_c, step_h in peers:
        source, other = lax.rem(me + step_c, count), lax.rem(mine + step_h, groups)
        pltpu.make_async_remote_copy(
            src_ref=long_ref.at[source],
            dst_ref=long_in.at[source, other],
            send_sem=long_send.at[source * groups + other],
            recv_sem=long_recv.at[source * groups + other],
            device_id=(source, other),
            device_id_type=mesh_id,
        ).wait_recv()
    rows_out[...] = rows_in[...]
    long_out[...] = long_in[...]


def gather(rows, longs, groups, collective_id):
    count = rows.shape[0]
    long_shape = (count, groups) + longs.shape[1:]
    vmem = pl.BlockSpec(memory_space=pltpu.VMEM)
    return pl.pallas_call(
        gather_kernel,
        out_shape=(
            jax.ShapeDtypeStruct(rows.shape, rows.dtype),
            jax.ShapeDtypeStruct(long_shape, longs.dtype),
        ),
        in_specs=[vmem, vmem],
        out_specs=(vmem, vmem),
        scratch_shapes=[
            pltpu.VMEM(rows.shape, rows.dtype),
            pltpu.VMEM(long_shape, longs.dtype),
            pltpu.SemaphoreType.DMA((2,)),
            pltpu.SemaphoreType.DMA((count,)),
            pltpu.SemaphoreType.DMA((count,)),
            pltpu.SemaphoreType.DMA((count * groups,)),
            pltpu.SemaphoreType.DMA((count * groups,)),
        ],
        compiler_params=pltpu.CompilerParams(collective_id=collective_id, has_side_effects=True),
    )(rows, longs)


def fused_kernel(
    grad_ref, rev_ref, in_ref, taps_ref, rows_out,
    hankel, toeplitz, grad_buf, rows_buf, ch_in, rows_in, local_sems,
    rows_send, rows_recv, ch_send, ch_recv,
):
    count = rows_buf.shape[0]
    chans, _, block_len = grad_ref.shape
    block_count = count
    sources, lags, _ = rev_ref.shape
    tap_count = taps_ref.shape[0]
    groups = lax.axis_size("ch")
    me = lax.axis_index("ctx")
    mine = lax.axis_index("ch")
    mesh_id = pl.DeviceIdType.MESH
    peers = [(c, 0) for c in range(1, count)] + [(0, h) for h in range(1, groups)]
    barrier = pltpu.get_barrier_semaphore()
    for step_c, step_h in peers:
        peer, other = lax.rem(me + step_c, count), lax.rem(mine + step_h, groups)
        pl.semaphore_signal(barrier, 1, device_id=(peer, other), device_id_type=mesh_id)

    def fill_hankel(lag, carry):
        col = pl.multiple_of(lag * block_len, block_len)
        for g in range(chans):
            hankel[g, :, pl.ds(col, block_len)] = grad_ref[g, pl.ds(lag, block_count), :].astype(
                hankel.dtype
            )
        return carry

    lax.fori_loop(0, lags, fill_hankel, 0)

    def fill_toeplitz(picked):
        def fill(lag, carry):
            row = pl.multiple_of(lag * block_len, block_len)
            for s in picked:
                line = rev_ref[s, pl.ds(lag, 1), :]
                tiled = jnp.broadcast_to(line, (block_len, 2 * block_len))
                skewed = pltpu.roll(tiled, block_len + 1, 1, stride=1, stride_axis=0)
                toeplitz[s, pl.ds(row, block_len), :] = skewed[:, :block_len].astype(
                    toeplitz.dtype
                )
            return carry

        lax.fori_loop(0, lags, fill, 0)

    fill_toeplitz(range(1, sources))

    acc = jnp.dot(hankel[0], toeplitz[1], preferred_element_type=jnp.float32)
    for g in range(1, chans):
        acc = acc + jnp.dot(hankel[g], toeplitz[1 + g], preferred_element_type=jnp.float32)
    ch_in[mine] = acc
    pl.semaphore_wait(barrier, len(peers))
    partials = []
    for step in range(1, groups):
        other = lax.rem(mine + step, groups)
        copy = pltpu.make_async_remote_copy(
            src_ref=ch_in.at[mine],
            dst_ref=ch_in.at[mine],
            send_sem=ch_send.at[other],
            recv_sem=ch_recv.at[mine],
            device_id=(me, other),
            device_id_type=mesh_id,
        )
        copy.start()
        partials.append(copy)
    fill_toeplitz(range(1))

    lane = lax.broadcasted_iota(jnp.int32, (block_count, block_len), 1)
    short_row = jnp.zeros((block_count, block_len), jnp.float32)
    grad_buf[...] = jnp.zeros_like(grad_buf)
    for g in range(chans):
        hidden_grad = jnp.dot(hankel[g], toeplitz[0], preferred_element_type=jnp.float32)
        grad_buf[g, pl.ds(0, block_count), :] = hidden_grad
        following = grad_buf[g, pl.ds(1, block_count), :]
        total = taps_ref[0, g] * hidden_grad
        for offset in range(1, tap_count):
            here = pltpu.roll(hidden_grad, block_len - offset, 1)
            there = pltpu.roll(following, block_len - offset, 1)
            total = total + taps_ref[offset, g] * jnp.where(
                lane >= block_len - offset, there, here
            )
        rows_buf[:, g, :] = total.astype(jnp.bfloat16).astype(jnp.float32)
        current = in_ref[g, pl.ds(1, block_count), :]
        previous = in_ref[g, pl.ds(0, block_count), :]
        for offset in range(tap_count):
            if offset == 0:
                delayed_in = current
            else:
                delayed_in = jnp.where(
                    lane < offset,
                    pltpu.roll(previous, offset, 1),
                    pltpu.roll(current, offset, 1),
                )
            value = jnp.sum(hidden_grad * delayed_in)
            short_row = jnp.where(lane == offset * chans + g, value, short_row)
    rows_buf[:, chans, :] = short_row

    for copy in partials:
        copy.wait_send()
    for step in range(1, groups):
        source = lax.rem(mine + step, groups)
        pltpu.make_async_remote_copy(
            src_ref=ch_in.at[source],
            dst_ref=ch_in.at[source],
            send_sem=ch_send.at[source],
            recv_sem=ch_recv.at[source],
            device_id=(me, source),
            device_id_type=mesh_id,
        ).wait_recv()
    summed = ch_in[0]
    for h in range(1, groups):
        summed = summed + ch_in[h]
    rows_buf[:, chans + 1, :] = summed

    local_rows = pltpu.make_async_copy(rows_buf.at[me], rows_in.at[me], local_sems.at[0])
    local_rows.start()
    copies = []
    for step in range(1, count):
        peer = lax.rem(me + step, count)
        copy = pltpu.make_async_remote_copy(
            src_ref=rows_buf.at[peer],
            dst_ref=rows_in.at[me],
            send_sem=rows_send.at[peer],
            recv_sem=rows_recv.at[me],
            device_id=(peer, mine),
            device_id_type=mesh_id,
        )
        copy.start()
        copies.append(copy)
    local_rows.wait()
    for copy in copies:
        copy.wait_send()
    for step in range(1, count):
        source = lax.rem(me + step, count)
        pltpu.make_async_remote_copy(
            src_ref=rows_buf.at[source],
            dst_ref=rows_in.at[source],
            send_sem=rows_send.at[source],
            recv_sem=rows_recv.at[source],
            device_id=(source, mine),
            device_id_type=mesh_id,
        ).wait_recv()
    rows_out[...] = rows_in[...]


def fused(grad_seq, sources, in_seq, taps, groups, block_len, collective_id):
    chans, total_len = grad_seq.shape
    count = sources.shape[0]
    block_count = total_len // block_len
    grad_pad = jnp.pad(
        grad_seq.astype(jnp.float32).reshape(chans, block_count, block_len),
        ((0, 0), (0, block_count), (0, 0)),
    )
    blocks = sources.reshape(count, block_count, block_len)
    padded = jnp.pad(blocks, ((0, 0), (1, 1), (0, 0)))
    pairs = jnp.concatenate([padded[:, :-1], padded[:, 1:]], axis=2)
    rev = pairs[..., ::-1].astype(jnp.float32)
    in_pad = jnp.pad(in_seq.reshape(chans, block_count, block_len), ((0, 0), (1, 0), (0, 0)))
    lags = block_count + 1
    rows_shape = (block_count, chans + 2, block_len)
    vmem = pl.BlockSpec(memory_space=pltpu.VMEM)
    return pl.pallas_call(
        fused_kernel,
        out_shape=jax.ShapeDtypeStruct(rows_shape, jnp.float32),
        in_specs=[vmem, vmem, vmem, pl.BlockSpec(memory_space=pltpu.SMEM)],
        out_specs=vmem,
        scratch_shapes=[
            pltpu.VMEM((chans, block_count, lags * block_len), jnp.bfloat16),
            pltpu.VMEM((count, lags * block_len, block_len), jnp.bfloat16),
            pltpu.VMEM((chans, block_count + 8, block_len), jnp.float32),
            pltpu.VMEM(rows_shape, jnp.float32),
            pltpu.VMEM((groups, block_count, block_len), jnp.float32),
            pltpu.VMEM(rows_shape, jnp.float32),
            pltpu.SemaphoreType.DMA((1,)),
            pltpu.SemaphoreType.DMA((block_count,)),
            pltpu.SemaphoreType.DMA((block_count,)),
            pltpu.SemaphoreType.DMA((groups,)),
            pltpu.SemaphoreType.DMA((groups,)),
        ],
        compiler_params=pltpu.CompilerParams(
            collective_id=collective_id,
            has_side_effects=True,
            vmem_limit_bytes=48 * 1024 * 1024,
        ),
    )(grad_pad, rev, in_pad, taps)


def relay_kernel(send_ref, out_ref, middle, landed, local_sems, first_send, first_recv, second_send, second_recv):
    inner, outer = send_ref.shape[0], send_ref.shape[1]
    me = lax.axis_index("ctx")
    mine = lax.axis_index("ch")
    row, col = me // inner, lax.rem(me, inner)
    mesh_id = pl.DeviceIdType.MESH
    barrier = pltpu.get_barrier_semaphore()
    for step in range(1, inner):
        peer = row * inner + lax.rem(col + step, inner)
        pl.semaphore_signal(barrier, 1, device_id=(peer, mine), device_id_type=mesh_id)
    for step in range(1, outer):
        peer = lax.rem(row + step, outer) * inner + col
        pl.semaphore_signal(barrier, 1, device_id=(peer, mine), device_id_type=mesh_id)
    pl.semaphore_wait(barrier, inner - 1 + outer - 1)
    local = pltpu.make_async_copy(send_ref.at[col], middle.at[:, col], local_sems.at[0])
    local.start()
    copies = []
    for step in range(1, inner):
        target = lax.rem(col + step, inner)
        copy = pltpu.make_async_remote_copy(
            src_ref=send_ref.at[target],
            dst_ref=middle.at[:, col],
            send_sem=first_send.at[target],
            recv_sem=first_recv.at[col],
            device_id=(row * inner + target, mine),
            device_id_type=mesh_id,
        )
        copy.start()
        copies.append(copy)
    local.wait()
    for copy in copies:
        copy.wait_send()
    for step in range(1, inner):
        source = lax.rem(col + step, inner)
        pltpu.make_async_remote_copy(
            src_ref=send_ref.at[source],
            dst_ref=middle.at[:, source],
            send_sem=first_send.at[source],
            recv_sem=first_recv.at[source],
            device_id=(row * inner + source, mine),
            device_id_type=mesh_id,
        ).wait_recv()
    local = pltpu.make_async_copy(middle.at[row], landed.at[row], local_sems.at[1])
    local.start()
    copies = []
    for step in range(1, outer):
        target = lax.rem(row + step, outer)
        copy = pltpu.make_async_remote_copy(
            src_ref=middle.at[target],
            dst_ref=landed.at[row],
            send_sem=second_send.at[target],
            recv_sem=second_recv.at[row],
            device_id=(target * inner + col, mine),
            device_id_type=mesh_id,
        )
        copy.start()
        copies.append(copy)
    local.wait()
    for copy in copies:
        copy.wait_send()
    for step in range(1, outer):
        source = lax.rem(row + step, outer)
        pltpu.make_async_remote_copy(
            src_ref=middle.at[source],
            dst_ref=landed.at[source],
            send_sem=second_send.at[source],
            recv_sem=second_recv.at[source],
            device_id=(source * inner + col, mine),
            device_id_type=mesh_id,
        ).wait_recv()
    out_ref[...] = landed[...]


def relay(chunks, inner, collective_id):
    count = chunks.shape[0]
    outer = count // inner
    rest = chunks.shape[1:]
    by_inner = chunks.reshape((outer, inner) + rest).swapaxes(0, 1)
    grid_shape = (outer, inner) + rest
    landed = pl.pallas_call(
        relay_kernel,
        out_shape=jax.ShapeDtypeStruct(grid_shape, chunks.dtype),
        in_specs=[pl.BlockSpec(memory_space=pltpu.VMEM)],
        out_specs=pl.BlockSpec(memory_space=pltpu.VMEM),
        scratch_shapes=[
            pltpu.VMEM(grid_shape, chunks.dtype),
            pltpu.VMEM(grid_shape, chunks.dtype),
            pltpu.SemaphoreType.DMA((2,)),
            pltpu.SemaphoreType.DMA((inner,)),
            pltpu.SemaphoreType.DMA((inner,)),
            pltpu.SemaphoreType.DMA((outer,)),
            pltpu.SemaphoreType.DMA((outer,)),
        ],
        compiler_params=pltpu.CompilerParams(collective_id=collective_id, has_side_effects=True),
    )(by_inner)
    return landed.reshape(chunks.shape)


def per_device(inputs, short_filter, long_filter, grad_out):
    tap_count = short_filter.shape[0]
    filter_count, chan_count, shard_len = inputs.shape
    ctx_count = lax.axis_size("ctx")
    my_index = lax.axis_index("ctx")
    total_len = shard_len * ctx_count
    per_dev = filter_count * chan_count // ctx_count
    per_filter = chan_count // per_dev
    block_len = 128
    block_count = total_len // block_len

    send = jnp.concatenate(
        [
            grad_out.reshape(ctx_count, per_dev, shard_len),
            inputs.reshape(ctx_count, per_dev, shard_len),
            jnp.repeat(long_filter, per_filter, axis=0)[:, None, :],
        ],
        axis=1,
    )
    recv = relay(send, 16, 0)
    seqs = recv.transpose(1, 0, 2).reshape(2 * per_dev + 1, total_len)
    grad_seq = seqs[:per_dev]
    in_seq = seqs[per_dev : 2 * per_dev].astype(jnp.float32)
    filt_seq = seqs[2 * per_dev :]
    taps = short_filter.reshape(tap_count, ctx_count, per_dev)
    taps = lax.dynamic_index_in_dim(taps, my_index, axis=1, keepdims=False)

    hidden = sum(
        (taps[offset][:, None] * delayed(in_seq, offset, total_len) for offset in range(tap_count))
    )
    hidden = hidden.astype(jnp.bfloat16)

    groups = lax.axis_size("ch")
    got = fused(
        grad_seq,
        jnp.concatenate([filt_seq, hidden], axis=0),
        in_seq,
        taps,
        groups,
        block_len,
        1,
    )
    grad_in_out = got[:, :per_dev].reshape(filter_count, chan_count, shard_len)
    grad_in_out = grad_in_out.astype(jnp.bfloat16)
    grad_long_out = got[:, per_dev + 1].reshape(filter_count, per_filter, shard_len).sum(axis=1)
    short_all = got[:, per_dev, : tap_count * per_dev].reshape(ctx_count, tap_count, per_dev)
    grad_short_out = short_all.transpose(1, 0, 2).reshape(tap_count, filter_count, chan_count)
    return (grad_in_out, grad_long_out, grad_short_out)


def solution(mesh):
    in_specs = (P(None, "ch", "ctx"), P(None, None, "ch"), P(None, "ctx"), P(None, "ch", "ctx"))
    out_specs = (P(None, "ch", "ctx"), P(None, "ctx"), P(None, None, "ch"))
    return jax.shard_map(
        per_device, mesh=mesh, in_specs=in_specs, out_specs=out_specs, check_vma=False
    )
```

```python
import jax
import jax.numpy as jnp
from jax import lax
from jax.experimental import pallas as pl
from jax.experimental.pallas import tpu as pltpu
from jax.sharding import PartitionSpec as P


def delayed(values, by, length):
    return jnp.pad(values, ((0, 0), (by, 0)))[:, :length]


def conv_kernel(grad_ref, rev_ref, hidden_ref, long_ref, hankel, toeplitz):
    chans, _, block_len = grad_ref.shape
    block_count = hidden_ref.shape[1]
    sources, lags, _ = rev_ref.shape

    def fill_hankel(lag, carry):
        col = pl.multiple_of(lag * block_len, block_len)
        for g in range(chans):
            hankel[g, :, pl.ds(col, block_len)] = grad_ref[g, pl.ds(lag, block_count), :].astype(
                hankel.dtype
            )
        return carry

    lax.fori_loop(0, lags, fill_hankel, 0)

    def fill_toeplitz(lag, carry):
        row = pl.multiple_of(lag * block_len, block_len)
        for s in range(sources):
            line = rev_ref[s, pl.ds(lag, 1), :]
            tiled = jnp.broadcast_to(line, (block_len, 2 * block_len))
            skewed = pltpu.roll(tiled, block_len + 1, 1, stride=1, stride_axis=0)
            toeplitz[s, pl.ds(row, block_len), :] = skewed[:, :block_len].astype(toeplitz.dtype)
        return carry

    lax.fori_loop(0, lags, fill_toeplitz, 0)

    for g in range(chans):
        hidden_ref[g] = jnp.dot(hankel[g], toeplitz[0], preferred_element_type=jnp.float32)
    acc = jnp.dot(hankel[0], toeplitz[1], preferred_element_type=jnp.float32)
    for g in range(1, chans):
        acc = acc + jnp.dot(hankel[g], toeplitz[1 + g], preferred_element_type=jnp.float32)
    long_ref[...] = acc


def correlate_all(grad_seq, sources, block_len):
    chans, total_len = grad_seq.shape
    count = sources.shape[0]
    block_count = total_len // block_len
    grad_pad = jnp.pad(
        grad_seq.astype(jnp.float32).reshape(chans, block_count, block_len),
        ((0, 0), (0, block_count), (0, 0)),
    )
    blocks = sources.reshape(count, block_count, block_len)
    padded = jnp.pad(blocks, ((0, 0), (1, 1), (0, 0)))
    pairs = jnp.concatenate([padded[:, :-1], padded[:, 1:]], axis=2)
    rev = pairs[..., ::-1].astype(jnp.float32)
    lags = block_count + 1
    hidden, long = pl.pallas_call(
        conv_kernel,
        out_shape=(
            jax.ShapeDtypeStruct((chans, block_count, block_len), jnp.float32),
            jax.ShapeDtypeStruct((block_count, block_len), jnp.float32),
        ),
        scratch_shapes=[
            pltpu.VMEM((chans, block_count, lags * block_len), jnp.bfloat16),
            pltpu.VMEM((count, lags * block_len, block_len), jnp.bfloat16),
        ],
        compiler_params=pltpu.CompilerParams(vmem_limit_bytes=48 * 1024 * 1024),
    )(grad_pad, rev)
    return hidden.reshape(chans, total_len), long.reshape(total_len)


def swap_kernel(send_ref, out_ref, landed, local_sem, send_sem, recv_sem):
    count = send_ref.shape[0]
    me = lax.axis_index("ctx")
    mine = lax.axis_index("ch")
    barrier = pltpu.get_barrier_semaphore()
    for step in range(1, count):
        peer = lax.rem(me + step, count)
        pl.semaphore_signal(
            barrier, 1, device_id=(peer, mine), device_id_type=pl.DeviceIdType.MESH
        )
    pl.semaphore_wait(barrier, count - 1)
    local = pltpu.make_async_copy(send_ref.at[me], landed.at[me], local_sem)
    local.start()
    copies = []
    for step in range(1, count):
        peer = lax.rem(me + step, count)
        copy = pltpu.make_async_remote_copy(
            src_ref=send_ref.at[peer],
            dst_ref=landed.at[me],
            send_sem=send_sem.at[peer],
            recv_sem=recv_sem.at[me],
            device_id=(peer, mine),
            device_id_type=pl.DeviceIdType.MESH,
        )
        copy.start()
        copies.append(copy)
    local.wait()
    for copy in copies:
        copy.wait_send()
    for step in range(1, count):
        source = lax.rem(me + step, count)
        pltpu.make_async_remote_copy(
            src_ref=send_ref.at[source],
            dst_ref=landed.at[source],
            send_sem=send_sem.at[source],
            recv_sem=recv_sem.at[source],
            device_id=(source, mine),
            device_id_type=pl.DeviceIdType.MESH,
        ).wait_recv()
    out_ref[...] = landed[...]


def swap(chunks, collective_id):
    return pl.pallas_call(
        swap_kernel,
        out_shape=jax.ShapeDtypeStruct(chunks.shape, chunks.dtype),
        in_specs=[pl.BlockSpec(memory_space=pltpu.VMEM)],
        out_specs=pl.BlockSpec(memory_space=pltpu.VMEM),
        scratch_shapes=[
            pltpu.VMEM(chunks.shape, chunks.dtype),
            pltpu.SemaphoreType.DMA,
            pltpu.SemaphoreType.DMA((chunks.shape[0],)),
            pltpu.SemaphoreType.DMA((chunks.shape[0],)),
        ],
        compiler_params=pltpu.CompilerParams(collective_id=collective_id, has_side_effects=True),
    )(chunks)


def gather_kernel(
    rows_ref, long_ref, rows_out, long_out, rows_in, long_in, local_sems,
    rows_send, rows_recv, long_send, long_recv,
):
    count = rows_ref.shape[0]
    groups = lax.axis_size("ch")
    me = lax.axis_index("ctx")
    mine = lax.axis_index("ch")
    mesh_id = pl.DeviceIdType.MESH
    peers = [(c, h) for c in range(count) for h in range(groups) if (c, h) != (0, 0)]
    barrier = pltpu.get_barrier_semaphore()
    for step_c, step_h in peers:
        peer, other = lax.rem(me + step_c, count), lax.rem(mine + step_h, groups)
        pl.semaphore_signal(barrier, 1, device_id=(peer, other), device_id_type=mesh_id)
    pl.semaphore_wait(barrier, len(peers))
    local_rows = pltpu.make_async_copy(rows_ref.at[me], rows_in.at[me], local_sems.at[0])
    local_long = pltpu.make_async_copy(long_ref.at[me], long_in.at[me, mine], local_sems.at[1])
    local_rows.start()
    local_long.start()
    copies = []
    for step in range(1, count):
        peer = lax.rem(me + step, count)
        copy = pltpu.make_async_remote_copy(
            src_ref=rows_ref.at[peer],
            dst_ref=rows_in.at[me],
            send_sem=rows_send.at[peer],
            recv_sem=rows_recv.at[me],
            device_id=(peer, mine),
            device_id_type=mesh_id,
        )
        copy.start()
        copies.append(copy)
    for step_c, step_h in peers:
        peer, other = lax.rem(me + step_c, count), lax.rem(mine + step_h, groups)
        copy = pltpu.make_async_remote_copy(
            src_ref=long_ref.at[peer],
            dst_ref=long_in.at[me, mine],
            send_sem=long_send.at[peer * groups + other],
            recv_sem=long_recv.at[me * groups + mine],
            device_id=(peer, other),
            device_id_type=mesh_id,
        )
        copy.start()
        copies.append(copy)
    local_rows.wait()
    local_long.wait()
    for copy in copies:
        copy.wait_send()
    for step in range(1, count):
        source = lax.rem(me + step, count)
        pltpu.make_async_remote_copy(
            src_ref=rows_ref.at[source],
            dst_ref=rows_in.at[source],
            send_sem=rows_send.at[source],
            recv_sem=rows_recv.at[source],
            device_id=(source, mine),
            device_id_type=mesh_id,
        ).wait_recv()
    for step_c, step_h in peers:
        source, other = lax.rem(me + step_c, count), lax.rem(mine + step_h, groups)
        pltpu.make_async_remote_copy(
            src_ref=long_ref.at[source],
            dst_ref=long_in.at[source, other],
            send_sem=long_send.at[source * groups + other],
            recv_sem=long_recv.at[source * groups + other],
            device_id=(source, other),
            device_id_type=mesh_id,
        ).wait_recv()
    rows_out[...] = rows_in[...]
    long_out[...] = long_in[...]


def gather(rows, longs, groups, collective_id):
    count = rows.shape[0]
    long_shape = (count, groups) + longs.shape[1:]
    vmem = pl.BlockSpec(memory_space=pltpu.VMEM)
    return pl.pallas_call(
        gather_kernel,
        out_shape=(
            jax.ShapeDtypeStruct(rows.shape, rows.dtype),
            jax.ShapeDtypeStruct(long_shape, longs.dtype),
        ),
        in_specs=[vmem, vmem],
        out_specs=(vmem, vmem),
        scratch_shapes=[
            pltpu.VMEM(rows.shape, rows.dtype),
            pltpu.VMEM(long_shape, longs.dtype),
            pltpu.SemaphoreType.DMA((2,)),
            pltpu.SemaphoreType.DMA((count,)),
            pltpu.SemaphoreType.DMA((count,)),
            pltpu.SemaphoreType.DMA((count * groups,)),
            pltpu.SemaphoreType.DMA((count * groups,)),
        ],
        compiler_params=pltpu.CompilerParams(collective_id=collective_id, has_side_effects=True),
    )(rows, longs)


def fused_kernel(
    grad_ref, rev_ref, in_ref, taps_ref, rows_out,
    hankel, toeplitz, grad_buf, rows_buf, ch_in, rows_in, local_sems,
    rows_send, rows_recv, ch_send, ch_recv,
):
    count = rows_buf.shape[0]
    chans, _, block_len = grad_ref.shape
    block_count = count
    sources, lags, _ = rev_ref.shape
    tap_count = taps_ref.shape[0]
    groups = lax.axis_size("ch")
    me = lax.axis_index("ctx")
    mine = lax.axis_index("ch")
    mesh_id = pl.DeviceIdType.MESH
    peers = [(c, 0) for c in range(1, count)] + [(0, h) for h in range(1, groups)]
    barrier = pltpu.get_barrier_semaphore()
    for step_c, step_h in peers:
        peer, other = lax.rem(me + step_c, count), lax.rem(mine + step_h, groups)
        pl.semaphore_signal(barrier, 1, device_id=(peer, other), device_id_type=mesh_id)

    def fill_hankel(lag, carry):
        col = pl.multiple_of(lag * block_len, block_len)
        for g in range(chans):
            hankel[g, :, pl.ds(col, block_len)] = grad_ref[g, pl.ds(lag, block_count), :].astype(
                hankel.dtype
            )
        return carry

    lax.fori_loop(0, lags, fill_hankel, 0)

    def fill_toeplitz(picked):
        def fill(lag, carry):
            row = pl.multiple_of(lag * block_len, block_len)
            for s in picked:
                line = rev_ref[s, pl.ds(lag, 1), :]
                tiled = jnp.broadcast_to(line, (block_len, 2 * block_len))
                skewed = pltpu.roll(tiled, block_len + 1, 1, stride=1, stride_axis=0)
                toeplitz[s, pl.ds(row, block_len), :] = skewed[:, :block_len].astype(
                    toeplitz.dtype
                )
            return carry

        lax.fori_loop(0, lags, fill, 0)

    fill_toeplitz(range(1, sources))

    acc = jnp.dot(hankel[0], toeplitz[1], preferred_element_type=jnp.float32)
    for g in range(1, chans):
        acc = acc + jnp.dot(hankel[g], toeplitz[1 + g], preferred_element_type=jnp.float32)
    ch_in[mine] = acc
    pl.semaphore_wait(barrier, len(peers))
    partials = []
    for step in range(1, groups):
        other = lax.rem(mine + step, groups)
        copy = pltpu.make_async_remote_copy(
            src_ref=ch_in.at[mine],
            dst_ref=ch_in.at[mine],
            send_sem=ch_send.at[other],
            recv_sem=ch_recv.at[mine],
            device_id=(me, other),
            device_id_type=mesh_id,
        )
        copy.start()
        partials.append(copy)
    fill_toeplitz(range(1))

    lane = lax.broadcasted_iota(jnp.int32, (block_count, block_len), 1)
    short_row = jnp.zeros((block_count, block_len), jnp.float32)
    grad_buf[...] = jnp.zeros_like(grad_buf)
    for g in range(chans):
        hidden_grad = jnp.dot(hankel[g], toeplitz[0], preferred_element_type=jnp.float32)
        grad_buf[g, pl.ds(0, block_count), :] = hidden_grad
        following = grad_buf[g, pl.ds(1, block_count), :]
        total = taps_ref[0, g] * hidden_grad
        for offset in range(1, tap_count):
            here = pltpu.roll(hidden_grad, block_len - offset, 1)
            there = pltpu.roll(following, block_len - offset, 1)
            total = total + taps_ref[offset, g] * jnp.where(
                lane >= block_len - offset, there, here
            )
        rows_buf[:, g, :] = total.astype(jnp.bfloat16).astype(jnp.float32)
        current = in_ref[g, pl.ds(1, block_count), :]
        previous = in_ref[g, pl.ds(0, block_count), :]
        for offset in range(tap_count):
            if offset == 0:
                delayed_in = current
            else:
                delayed_in = jnp.where(
                    lane < offset,
                    pltpu.roll(previous, offset, 1),
                    pltpu.roll(current, offset, 1),
                )
            value = jnp.sum(hidden_grad * delayed_in)
            short_row = jnp.where(lane == offset * chans + g, value, short_row)
    rows_buf[:, chans, :] = short_row

    for copy in partials:
        copy.wait_send()
    for step in range(1, groups):
        source = lax.rem(mine + step, groups)
        pltpu.make_async_remote_copy(
            src_ref=ch_in.at[source],
            dst_ref=ch_in.at[source],
            send_sem=ch_send.at[source],
            recv_sem=ch_recv.at[source],
            device_id=(me, source),
            device_id_type=mesh_id,
        ).wait_recv()
    summed = ch_in[0]
    for h in range(1, groups):
        summed = summed + ch_in[h]
    rows_buf[:, chans + 1, :] = summed

    local_rows = pltpu.make_async_copy(rows_buf.at[me], rows_in.at[me], local_sems.at[0])
    local_rows.start()
    copies = []
    for step in range(1, count):
        peer = lax.rem(me + step, count)
        copy = pltpu.make_async_remote_copy(
            src_ref=rows_buf.at[peer],
            dst_ref=rows_in.at[me],
            send_sem=rows_send.at[peer],
            recv_sem=rows_recv.at[me],
            device_id=(peer, mine),
            device_id_type=mesh_id,
        )
        copy.start()
        copies.append(copy)
    local_rows.wait()
    for copy in copies:
        copy.wait_send()
    for step in range(1, count):
        source = lax.rem(me + step, count)
        pltpu.make_async_remote_copy(
            src_ref=rows_buf.at[source],
            dst_ref=rows_in.at[source],
            send_sem=rows_send.at[source],
            recv_sem=rows_recv.at[source],
            device_id=(source, mine),
            device_id_type=mesh_id,
        ).wait_recv()
    rows_out[...] = rows_in[...]


def fused(grad_seq, sources, in_seq, taps, groups, block_len, collective_id):
    chans, total_len = grad_seq.shape
    count = sources.shape[0]
    block_count = total_len // block_len
    grad_pad = jnp.pad(
        grad_seq.astype(jnp.float32).reshape(chans, block_count, block_len),
        ((0, 0), (0, block_count), (0, 0)),
    )
    blocks = sources.reshape(count, block_count, block_len)
    padded = jnp.pad(blocks, ((0, 0), (1, 1), (0, 0)))
    pairs = jnp.concatenate([padded[:, :-1], padded[:, 1:]], axis=2)
    rev = pairs[..., ::-1].astype(jnp.float32)
    in_pad = jnp.pad(in_seq.reshape(chans, block_count, block_len), ((0, 0), (1, 0), (0, 0)))
    lags = block_count + 1
    rows_shape = (block_count, chans + 2, block_len)
    vmem = pl.BlockSpec(memory_space=pltpu.VMEM)
    return pl.pallas_call(
        fused_kernel,
        out_shape=jax.ShapeDtypeStruct(rows_shape, jnp.float32),
        in_specs=[vmem, vmem, vmem, pl.BlockSpec(memory_space=pltpu.SMEM)],
        out_specs=vmem,
        scratch_shapes=[
            pltpu.VMEM((chans, block_count, lags * block_len), jnp.bfloat16),
            pltpu.VMEM((count, lags * block_len, block_len), jnp.bfloat16),
            pltpu.VMEM((chans, block_count + 8, block_len), jnp.float32),
            pltpu.VMEM(rows_shape, jnp.float32),
            pltpu.VMEM((groups, block_count, block_len), jnp.float32),
            pltpu.VMEM(rows_shape, jnp.float32),
            pltpu.SemaphoreType.DMA((1,)),
            pltpu.SemaphoreType.DMA((block_count,)),
            pltpu.SemaphoreType.DMA((block_count,)),
            pltpu.SemaphoreType.DMA((groups,)),
            pltpu.SemaphoreType.DMA((groups,)),
        ],
        compiler_params=pltpu.CompilerParams(
            collective_id=collective_id,
            has_side_effects=True,
            vmem_limit_bytes=48 * 1024 * 1024,
        ),
    )(grad_pad, rev, in_pad, taps)


def relay_kernel(send_ref, out_ref, middle, landed, local_sems, first_send, first_recv, second_send, second_recv):
    firsts, seconds = send_ref.shape[0], send_ref.shape[1]
    me = lax.axis_index("ctx")
    mine = lax.axis_index("ch")
    first, second = me // seconds, lax.rem(me, seconds)
    mesh_id = pl.DeviceIdType.MESH

    def place(f, s):
        return f * seconds + s

    barrier = pltpu.get_barrier_semaphore()
    for step in range(1, firsts):
        peer = place(lax.rem(first + step, firsts), second)
        pl.semaphore_signal(barrier, 1, device_id=(peer, mine), device_id_type=mesh_id)
    for step in range(1, seconds):
        peer = place(first, lax.rem(second + step, seconds))
        pl.semaphore_signal(barrier, 1, device_id=(peer, mine), device_id_type=mesh_id)
    pl.semaphore_wait(barrier, firsts - 1 + seconds - 1)
    local = pltpu.make_async_copy(send_ref.at[first], middle.at[:, first], local_sems.at[0])
    local.start()
    copies = []
    for step in range(1, firsts):
        target = lax.rem(first + step, firsts)
        copy = pltpu.make_async_remote_copy(
            src_ref=send_ref.at[target],
            dst_ref=middle.at[:, first],
            send_sem=first_send.at[target],
            recv_sem=first_recv.at[first],
            device_id=(place(target, second), mine),
            device_id_type=mesh_id,
        )
        copy.start()
        copies.append(copy)
    local.wait()
    for copy in copies:
        copy.wait_send()
    for step in range(1, firsts):
        source = lax.rem(first + step, firsts)
        pltpu.make_async_remote_copy(
            src_ref=send_ref.at[source],
            dst_ref=middle.at[:, source],
            send_sem=first_send.at[source],
            recv_sem=first_recv.at[source],
            device_id=(place(source, second), mine),
            device_id_type=mesh_id,
        ).wait_recv()
    local = pltpu.make_async_copy(middle.at[second], landed.at[second], local_sems.at[1])
    local.start()
    copies = []
    for step in range(1, seconds):
        target = lax.rem(second + step, seconds)
        copy = pltpu.make_async_remote_copy(
            src_ref=middle.at[target],
            dst_ref=landed.at[second],
            send_sem=second_send.at[target],
            recv_sem=second_recv.at[second],
            device_id=(place(first, target), mine),
            device_id_type=mesh_id,
        )
        copy.start()
        copies.append(copy)
    local.wait()
    for copy in copies:
        copy.wait_send()
    for step in range(1, seconds):
        source = lax.rem(second + step, seconds)
        pltpu.make_async_remote_copy(
            src_ref=middle.at[source],
            dst_ref=landed.at[source],
            send_sem=second_send.at[source],
            recv_sem=second_recv.at[source],
            device_id=(place(first, source), mine),
            device_id_type=mesh_id,
        ).wait_recv()
    out_ref[...] = landed[...]


def relay(chunks, inner, collective_id):
    count = chunks.shape[0]
    outer = count // inner
    rest = chunks.shape[1:]
    by_first = chunks.reshape((outer, inner) + rest)
    first_shape = (outer, inner) + rest
    second_shape = (inner, outer) + rest
    landed = pl.pallas_call(
        relay_kernel,
        out_shape=jax.ShapeDtypeStruct(second_shape, chunks.dtype),
        in_specs=[pl.BlockSpec(memory_space=pltpu.VMEM)],
        out_specs=pl.BlockSpec(memory_space=pltpu.VMEM),
        scratch_shapes=[
            pltpu.VMEM(second_shape, chunks.dtype),
            pltpu.VMEM(second_shape, chunks.dtype),
            pltpu.SemaphoreType.DMA((2,)),
            pltpu.SemaphoreType.DMA((outer,)),
            pltpu.SemaphoreType.DMA((outer,)),
            pltpu.SemaphoreType.DMA((inner,)),
            pltpu.SemaphoreType.DMA((inner,)),
        ],
        compiler_params=pltpu.CompilerParams(collective_id=collective_id, has_side_effects=True),
    )(by_first)
    return landed.swapaxes(0, 1).reshape(chunks.shape)


def per_device(inputs, short_filter, long_filter, grad_out):
    tap_count = short_filter.shape[0]
    filter_count, chan_count, shard_len = inputs.shape
    ctx_count = lax.axis_size("ctx")
    my_index = lax.axis_index("ctx")
    total_len = shard_len * ctx_count
    per_dev = filter_count * chan_count // ctx_count
    per_filter = chan_count // per_dev
    block_len = 128
    block_count = total_len // block_len

    send = jnp.concatenate(
        [
            grad_out.reshape(ctx_count, per_dev, shard_len),
            inputs.reshape(ctx_count, per_dev, shard_len),
            jnp.repeat(long_filter, per_filter, axis=0)[:, None, :],
        ],
        axis=1,
    )
    recv = relay(send, 8, 0)
    seqs = recv.transpose(1, 0, 2).reshape(2 * per_dev + 1, total_len)
    grad_seq = seqs[:per_dev]
    in_seq = seqs[per_dev : 2 * per_dev].astype(jnp.float32)
    filt_seq = seqs[2 * per_dev :]
    taps = short_filter.reshape(tap_count, ctx_count, per_dev)
    taps = lax.dynamic_index_in_dim(taps, my_index, axis=1, keepdims=False)

    hidden = sum(
        (taps[offset][:, None] * delayed(in_seq, offset, total_len) for offset in range(tap_count))
    )
    hidden = hidden.astype(jnp.bfloat16)

    groups = lax.axis_size("ch")
    got = fused(
        grad_seq,
        jnp.concatenate([filt_seq, hidden], axis=0),
        in_seq,
        taps,
        groups,
        block_len,
        1,
    )
    grad_in_out = got[:, :per_dev].reshape(filter_count, chan_count, shard_len)
    grad_in_out = grad_in_out.astype(jnp.bfloat16)
    grad_long_out = got[:, per_dev + 1].reshape(filter_count, per_filter, shard_len).sum(axis=1)
    short_all = got[:, per_dev, : tap_count * per_dev].reshape(ctx_count, tap_count, per_dev)
    grad_short_out = short_all.transpose(1, 0, 2).reshape(tap_count, filter_count, chan_count)
    return (grad_in_out, grad_long_out, grad_short_out)


def solution(mesh):
    in_specs = (P(None, "ch", "ctx"), P(None, None, "ch"), P(None, "ctx"), P(None, "ch", "ctx"))
    out_specs = (P(None, "ch", "ctx"), P(None, "ctx"), P(None, None, "ch"))
    return jax.shard_map(
        per_device, mesh=mesh, in_specs=in_specs, out_specs=out_specs, check_vma=False
    )
```

```python
import jax
import jax.numpy as jnp
from jax import lax
from jax.experimental import pallas as pl
from jax.experimental.pallas import tpu as pltpu
from jax.sharding import PartitionSpec as P


def delayed(values, by, length):
    return jnp.pad(values, ((0, 0), (by, 0)))[:, :length]


def conv_kernel(grad_ref, rev_ref, hidden_ref, long_ref, hankel, toeplitz):
    chans, _, block_len = grad_ref.shape
    block_count = hidden_ref.shape[1]
    sources, lags, _ = rev_ref.shape

    def fill_hankel(lag, carry):
        col = pl.multiple_of(lag * block_len, block_len)
        for g in range(chans):
            hankel[g, :, pl.ds(col, block_len)] = grad_ref[g, pl.ds(lag, block_count), :].astype(
                hankel.dtype
            )
        return carry

    lax.fori_loop(0, lags, fill_hankel, 0)

    def fill_toeplitz(lag, carry):
        row = pl.multiple_of(lag * block_len, block_len)
        for s in range(sources):
            line = rev_ref[s, pl.ds(lag, 1), :]
            tiled = jnp.broadcast_to(line, (block_len, 2 * block_len))
            skewed = pltpu.roll(tiled, block_len + 1, 1, stride=1, stride_axis=0)
            toeplitz[s, pl.ds(row, block_len), :] = skewed[:, :block_len].astype(toeplitz.dtype)
        return carry

    lax.fori_loop(0, lags, fill_toeplitz, 0)

    for g in range(chans):
        hidden_ref[g] = jnp.dot(hankel[g], toeplitz[0], preferred_element_type=jnp.float32)
    acc = jnp.dot(hankel[0], toeplitz[1], preferred_element_type=jnp.float32)
    for g in range(1, chans):
        acc = acc + jnp.dot(hankel[g], toeplitz[1 + g], preferred_element_type=jnp.float32)
    long_ref[...] = acc


def correlate_all(grad_seq, sources, block_len):
    chans, total_len = grad_seq.shape
    count = sources.shape[0]
    block_count = total_len // block_len
    grad_pad = jnp.pad(
        grad_seq.astype(jnp.float32).reshape(chans, block_count, block_len),
        ((0, 0), (0, block_count), (0, 0)),
    )
    blocks = sources.reshape(count, block_count, block_len)
    padded = jnp.pad(blocks, ((0, 0), (1, 1), (0, 0)))
    pairs = jnp.concatenate([padded[:, :-1], padded[:, 1:]], axis=2)
    rev = pairs[..., ::-1].astype(jnp.float32)
    lags = block_count + 1
    hidden, long = pl.pallas_call(
        conv_kernel,
        out_shape=(
            jax.ShapeDtypeStruct((chans, block_count, block_len), jnp.float32),
            jax.ShapeDtypeStruct((block_count, block_len), jnp.float32),
        ),
        scratch_shapes=[
            pltpu.VMEM((chans, block_count, lags * block_len), jnp.bfloat16),
            pltpu.VMEM((count, lags * block_len, block_len), jnp.bfloat16),
        ],
        compiler_params=pltpu.CompilerParams(vmem_limit_bytes=48 * 1024 * 1024),
    )(grad_pad, rev)
    return hidden.reshape(chans, total_len), long.reshape(total_len)


def swap_kernel(send_ref, out_ref, landed, local_sem, send_sem, recv_sem):
    count = send_ref.shape[0]
    me = lax.axis_index("ctx")
    mine = lax.axis_index("ch")
    barrier = pltpu.get_barrier_semaphore()
    for step in range(1, count):
        peer = lax.rem(me + step, count)
        pl.semaphore_signal(
            barrier, 1, device_id=(peer, mine), device_id_type=pl.DeviceIdType.MESH
        )
    pl.semaphore_wait(barrier, count - 1)
    local = pltpu.make_async_copy(send_ref.at[me], landed.at[me], local_sem)
    local.start()
    copies = []
    for step in range(1, count):
        peer = lax.rem(me + step, count)
        copy = pltpu.make_async_remote_copy(
            src_ref=send_ref.at[peer],
            dst_ref=landed.at[me],
            send_sem=send_sem.at[peer],
            recv_sem=recv_sem.at[me],
            device_id=(peer, mine),
            device_id_type=pl.DeviceIdType.MESH,
        )
        copy.start()
        copies.append(copy)
    local.wait()
    for copy in copies:
        copy.wait_send()
    for step in range(1, count):
        source = lax.rem(me + step, count)
        pltpu.make_async_remote_copy(
            src_ref=send_ref.at[source],
            dst_ref=landed.at[source],
            send_sem=send_sem.at[source],
            recv_sem=recv_sem.at[source],
            device_id=(source, mine),
            device_id_type=pl.DeviceIdType.MESH,
        ).wait_recv()
    out_ref[...] = landed[...]


def swap(chunks, collective_id):
    return pl.pallas_call(
        swap_kernel,
        out_shape=jax.ShapeDtypeStruct(chunks.shape, chunks.dtype),
        in_specs=[pl.BlockSpec(memory_space=pltpu.VMEM)],
        out_specs=pl.BlockSpec(memory_space=pltpu.VMEM),
        scratch_shapes=[
            pltpu.VMEM(chunks.shape, chunks.dtype),
            pltpu.SemaphoreType.DMA,
            pltpu.SemaphoreType.DMA((chunks.shape[0],)),
            pltpu.SemaphoreType.DMA((chunks.shape[0],)),
        ],
        compiler_params=pltpu.CompilerParams(collective_id=collective_id, has_side_effects=True),
    )(chunks)


def gather_kernel(
    rows_ref, long_ref, rows_out, long_out, rows_in, long_in, local_sems,
    rows_send, rows_recv, long_send, long_recv,
):
    count = rows_ref.shape[0]
    groups = lax.axis_size("ch")
    me = lax.axis_index("ctx")
    mine = lax.axis_index("ch")
    mesh_id = pl.DeviceIdType.MESH
    peers = [(c, h) for c in range(count) for h in range(groups) if (c, h) != (0, 0)]
    barrier = pltpu.get_barrier_semaphore()
    for step_c, step_h in peers:
        peer, other = lax.rem(me + step_c, count), lax.rem(mine + step_h, groups)
        pl.semaphore_signal(barrier, 1, device_id=(peer, other), device_id_type=mesh_id)
    pl.semaphore_wait(barrier, len(peers))
    local_rows = pltpu.make_async_copy(rows_ref.at[me], rows_in.at[me], local_sems.at[0])
    local_long = pltpu.make_async_copy(long_ref.at[me], long_in.at[me, mine], local_sems.at[1])
    local_rows.start()
    local_long.start()
    copies = []
    for step in range(1, count):
        peer = lax.rem(me + step, count)
        copy = pltpu.make_async_remote_copy(
            src_ref=rows_ref.at[peer],
            dst_ref=rows_in.at[me],
            send_sem=rows_send.at[peer],
            recv_sem=rows_recv.at[me],
            device_id=(peer, mine),
            device_id_type=mesh_id,
        )
        copy.start()
        copies.append(copy)
    for step_c, step_h in peers:
        peer, other = lax.rem(me + step_c, count), lax.rem(mine + step_h, groups)
        copy = pltpu.make_async_remote_copy(
            src_ref=long_ref.at[peer],
            dst_ref=long_in.at[me, mine],
            send_sem=long_send.at[peer * groups + other],
            recv_sem=long_recv.at[me * groups + mine],
            device_id=(peer, other),
            device_id_type=mesh_id,
        )
        copy.start()
        copies.append(copy)
    local_rows.wait()
    local_long.wait()
    for copy in copies:
        copy.wait_send()
    for step in range(1, count):
        source = lax.rem(me + step, count)
        pltpu.make_async_remote_copy(
            src_ref=rows_ref.at[source],
            dst_ref=rows_in.at[source],
            send_sem=rows_send.at[source],
            recv_sem=rows_recv.at[source],
            device_id=(source, mine),
            device_id_type=mesh_id,
        ).wait_recv()
    for step_c, step_h in peers:
        source, other = lax.rem(me + step_c, count), lax.rem(mine + step_h, groups)
        pltpu.make_async_remote_copy(
            src_ref=long_ref.at[source],
            dst_ref=long_in.at[source, other],
            send_sem=long_send.at[source * groups + other],
            recv_sem=long_recv.at[source * groups + other],
            device_id=(source, other),
            device_id_type=mesh_id,
        ).wait_recv()
    rows_out[...] = rows_in[...]
    long_out[...] = long_in[...]


def gather(rows, longs, groups, collective_id):
    count = rows.shape[0]
    long_shape = (count, groups) + longs.shape[1:]
    vmem = pl.BlockSpec(memory_space=pltpu.VMEM)
    return pl.pallas_call(
        gather_kernel,
        out_shape=(
            jax.ShapeDtypeStruct(rows.shape, rows.dtype),
            jax.ShapeDtypeStruct(long_shape, longs.dtype),
        ),
        in_specs=[vmem, vmem],
        out_specs=(vmem, vmem),
        scratch_shapes=[
            pltpu.VMEM(rows.shape, rows.dtype),
            pltpu.VMEM(long_shape, longs.dtype),
            pltpu.SemaphoreType.DMA((2,)),
            pltpu.SemaphoreType.DMA((count,)),
            pltpu.SemaphoreType.DMA((count,)),
            pltpu.SemaphoreType.DMA((count * groups,)),
            pltpu.SemaphoreType.DMA((count * groups,)),
        ],
        compiler_params=pltpu.CompilerParams(collective_id=collective_id, has_side_effects=True),
    )(rows, longs)


def fused_kernel(
    grad_ref, rev_ref, in_ref, taps_ref, rows_out,
    hankel, toeplitz, grad_buf, rows_buf, ch_in, rows_in, local_sems,
    rows_send, rows_recv, ch_send, ch_recv,
):
    count = rows_buf.shape[0]
    chans, _, block_len = grad_ref.shape
    block_count = count
    sources, lags, _ = rev_ref.shape
    tap_count = taps_ref.shape[0]
    groups = lax.axis_size("ch")
    me = lax.axis_index("ctx")
    mine = lax.axis_index("ch")
    mesh_id = pl.DeviceIdType.MESH
    peers = [(c, 0) for c in range(1, count)] + [(0, h) for h in range(1, groups)]
    barrier = pltpu.get_barrier_semaphore()
    for step_c, step_h in peers:
        peer, other = lax.rem(me + step_c, count), lax.rem(mine + step_h, groups)
        pl.semaphore_signal(barrier, 1, device_id=(peer, other), device_id_type=mesh_id)

    def fill_hankel(lag, carry):
        col = pl.multiple_of(lag * block_len, block_len)
        for g in range(chans):
            hankel[g, :, pl.ds(col, block_len)] = grad_ref[g, pl.ds(lag, block_count), :].astype(
                hankel.dtype
            )
        return carry

    lax.fori_loop(0, lags, fill_hankel, 0)

    def fill_toeplitz(picked):
        def fill(lag, carry):
            row = pl.multiple_of(lag * block_len, block_len)
            for s in picked:
                line = rev_ref[s, pl.ds(lag, 1), :]
                tiled = jnp.broadcast_to(line, (block_len, 2 * block_len))
                skewed = pltpu.roll(tiled, block_len + 1, 1, stride=1, stride_axis=0)
                toeplitz[s, pl.ds(row, block_len), :] = skewed[:, :block_len].astype(
                    toeplitz.dtype
                )
            return carry

        lax.fori_loop(0, lags, fill, 0)

    fill_toeplitz(range(1, sources))

    acc = jnp.dot(hankel[0], toeplitz[1], preferred_element_type=jnp.float32)
    for g in range(1, chans):
        acc = acc + jnp.dot(hankel[g], toeplitz[1 + g], preferred_element_type=jnp.float32)
    ch_in[mine] = acc
    pl.semaphore_wait(barrier, len(peers))
    partials = []
    for step in range(1, groups):
        other = lax.rem(mine + step, groups)
        copy = pltpu.make_async_remote_copy(
            src_ref=ch_in.at[mine],
            dst_ref=ch_in.at[mine],
            send_sem=ch_send.at[other],
            recv_sem=ch_recv.at[mine],
            device_id=(me, other),
            device_id_type=mesh_id,
        )
        copy.start()
        partials.append(copy)
    fill_toeplitz(range(1))

    lane = lax.broadcasted_iota(jnp.int32, (block_count, block_len), 1)
    short_row = jnp.zeros((block_count, block_len), jnp.float32)
    grad_buf[...] = jnp.zeros_like(grad_buf)
    for g in range(chans):
        hidden_grad = jnp.dot(hankel[g], toeplitz[0], preferred_element_type=jnp.float32)
        grad_buf[g, pl.ds(0, block_count), :] = hidden_grad
        following = grad_buf[g, pl.ds(1, block_count), :]
        total = taps_ref[0, g] * hidden_grad
        for offset in range(1, tap_count):
            here = pltpu.roll(hidden_grad, block_len - offset, 1)
            there = pltpu.roll(following, block_len - offset, 1)
            total = total + taps_ref[offset, g] * jnp.where(
                lane >= block_len - offset, there, here
            )
        rows_buf[:, g, :] = total.astype(jnp.bfloat16).astype(jnp.float32)
        current = in_ref[g, pl.ds(1, block_count), :]
        previous = in_ref[g, pl.ds(0, block_count), :]
        for offset in range(tap_count):
            if offset == 0:
                delayed_in = current
            else:
                delayed_in = jnp.where(
                    lane < offset,
                    pltpu.roll(previous, offset, 1),
                    pltpu.roll(current, offset, 1),
                )
            value = jnp.sum(hidden_grad * delayed_in)
            short_row = jnp.where(lane == offset * chans + g, value, short_row)
    rows_buf[:, chans, :] = short_row

    for copy in partials:
        copy.wait_send()
    for step in range(1, groups):
        source = lax.rem(mine + step, groups)
        pltpu.make_async_remote_copy(
            src_ref=ch_in.at[source],
            dst_ref=ch_in.at[source],
            send_sem=ch_send.at[source],
            recv_sem=ch_recv.at[source],
            device_id=(me, source),
            device_id_type=mesh_id,
        ).wait_recv()
    summed = ch_in[0]
    for h in range(1, groups):
        summed = summed + ch_in[h]
    rows_buf[:, chans + 1, :] = summed

    local_rows = pltpu.make_async_copy(rows_buf.at[me], rows_in.at[me], local_sems.at[0])
    local_rows.start()
    copies = []
    for step in range(1, count):
        peer = lax.rem(me + step, count)
        copy = pltpu.make_async_remote_copy(
            src_ref=rows_buf.at[peer],
            dst_ref=rows_in.at[me],
            send_sem=rows_send.at[peer],
            recv_sem=rows_recv.at[me],
            device_id=(peer, mine),
            device_id_type=mesh_id,
        )
        copy.start()
        copies.append(copy)
    local_rows.wait()
    for copy in copies:
        copy.wait_send()
    for step in range(1, count):
        source = lax.rem(me + step, count)
        pltpu.make_async_remote_copy(
            src_ref=rows_buf.at[source],
            dst_ref=rows_in.at[source],
            send_sem=rows_send.at[source],
            recv_sem=rows_recv.at[source],
            device_id=(source, mine),
            device_id_type=mesh_id,
        ).wait_recv()
    rows_out[...] = rows_in[...]


def fused(grad_seq, sources, in_seq, taps, groups, block_len, collective_id):
    chans, total_len = grad_seq.shape
    count = sources.shape[0]
    block_count = total_len // block_len
    grad_pad = jnp.pad(
        grad_seq.astype(jnp.float32).reshape(chans, block_count, block_len),
        ((0, 0), (0, block_count), (0, 0)),
    )
    blocks = sources.reshape(count, block_count, block_len)
    padded = jnp.pad(blocks, ((0, 0), (1, 1), (0, 0)))
    pairs = jnp.concatenate([padded[:, :-1], padded[:, 1:]], axis=2)
    rev = pairs[..., ::-1].astype(jnp.float32)
    in_pad = jnp.pad(in_seq.reshape(chans, block_count, block_len), ((0, 0), (1, 0), (0, 0)))
    lags = block_count + 1
    rows_shape = (block_count, chans + 2, block_len)
    vmem = pl.BlockSpec(memory_space=pltpu.VMEM)
    return pl.pallas_call(
        fused_kernel,
        out_shape=jax.ShapeDtypeStruct(rows_shape, jnp.float32),
        in_specs=[vmem, vmem, vmem, pl.BlockSpec(memory_space=pltpu.SMEM)],
        out_specs=vmem,
        scratch_shapes=[
            pltpu.VMEM((chans, block_count, lags * block_len), jnp.bfloat16),
            pltpu.VMEM((count, lags * block_len, block_len), jnp.bfloat16),
            pltpu.VMEM((chans, block_count + 8, block_len), jnp.float32),
            pltpu.VMEM(rows_shape, jnp.float32),
            pltpu.VMEM((groups, block_count, block_len), jnp.float32),
            pltpu.VMEM(rows_shape, jnp.float32),
            pltpu.SemaphoreType.DMA((1,)),
            pltpu.SemaphoreType.DMA((block_count,)),
            pltpu.SemaphoreType.DMA((block_count,)),
            pltpu.SemaphoreType.DMA((groups,)),
            pltpu.SemaphoreType.DMA((groups,)),
        ],
        compiler_params=pltpu.CompilerParams(
            collective_id=collective_id,
            has_side_effects=True,
            vmem_limit_bytes=48 * 1024 * 1024,
        ),
    )(grad_pad, rev, in_pad, taps)


def relay_kernel(send_ref, out_ref, middle, landed, local_sems, first_send, first_recv, second_send, second_recv):
    firsts, seconds = send_ref.shape[0], send_ref.shape[1]
    me = lax.axis_index("ctx")
    mine = lax.axis_index("ch")
    first, second = me // seconds, lax.rem(me, seconds)
    mesh_id = pl.DeviceIdType.MESH

    def place(f, s):
        return f * seconds + s

    barrier = pltpu.get_barrier_semaphore()
    for step in range(1, firsts):
        peer = place(lax.rem(first + step, firsts), second)
        pl.semaphore_signal(barrier, 1, device_id=(peer, mine), device_id_type=mesh_id)
    for step in range(1, seconds):
        peer = place(first, lax.rem(second + step, seconds))
        pl.semaphore_signal(barrier, 1, device_id=(peer, mine), device_id_type=mesh_id)
    pl.semaphore_wait(barrier, firsts - 1 + seconds - 1)
    local = pltpu.make_async_copy(send_ref.at[first], middle.at[:, first], local_sems.at[0])
    local.start()
    copies = []
    for step in range(1, firsts):
        target = lax.rem(first + step, firsts)
        copy = pltpu.make_async_remote_copy(
            src_ref=send_ref.at[target],
            dst_ref=middle.at[:, first],
            send_sem=first_send.at[target],
            recv_sem=first_recv.at[first],
            device_id=(place(target, second), mine),
            device_id_type=mesh_id,
        )
        copy.start()
        copies.append(copy)
    local.wait()
    for copy in copies:
        copy.wait_send()
    for step in range(1, firsts):
        source = lax.rem(first + step, firsts)
        pltpu.make_async_remote_copy(
            src_ref=send_ref.at[source],
            dst_ref=middle.at[:, source],
            send_sem=first_send.at[source],
            recv_sem=first_recv.at[source],
            device_id=(place(source, second), mine),
            device_id_type=mesh_id,
        ).wait_recv()
    local = pltpu.make_async_copy(middle.at[second], landed.at[second], local_sems.at[1])
    local.start()
    copies = []
    for step in range(1, seconds):
        target = lax.rem(second + step, seconds)
        copy = pltpu.make_async_remote_copy(
            src_ref=middle.at[target],
            dst_ref=landed.at[second],
            send_sem=second_send.at[target],
            recv_sem=second_recv.at[second],
            device_id=(place(first, target), mine),
            device_id_type=mesh_id,
        )
        copy.start()
        copies.append(copy)
    local.wait()
    for copy in copies:
        copy.wait_send()
    for step in range(1, seconds):
        source = lax.rem(second + step, seconds)
        pltpu.make_async_remote_copy(
            src_ref=middle.at[source],
            dst_ref=landed.at[source],
            send_sem=second_send.at[source],
            recv_sem=second_recv.at[source],
            device_id=(place(first, source), mine),
            device_id_type=mesh_id,
        ).wait_recv()
    out_ref[...] = landed[...]


def relay(chunks, inner, collective_id):
    count = chunks.shape[0]
    outer = count // inner
    rest = chunks.shape[1:]
    by_first = chunks.reshape((outer, inner) + rest)
    first_shape = (outer, inner) + rest
    second_shape = (inner, outer) + rest
    landed = pl.pallas_call(
        relay_kernel,
        out_shape=jax.ShapeDtypeStruct(second_shape, chunks.dtype),
        in_specs=[pl.BlockSpec(memory_space=pltpu.VMEM)],
        out_specs=pl.BlockSpec(memory_space=pltpu.VMEM),
        scratch_shapes=[
            pltpu.VMEM(second_shape, chunks.dtype),
            pltpu.VMEM(second_shape, chunks.dtype),
            pltpu.SemaphoreType.DMA((2,)),
            pltpu.SemaphoreType.DMA((outer,)),
            pltpu.SemaphoreType.DMA((outer,)),
            pltpu.SemaphoreType.DMA((inner,)),
            pltpu.SemaphoreType.DMA((inner,)),
        ],
        compiler_params=pltpu.CompilerParams(collective_id=collective_id, has_side_effects=True),
    )(by_first)
    return landed.swapaxes(0, 1).reshape(chunks.shape)


def per_device(inputs, short_filter, long_filter, grad_out):
    tap_count = short_filter.shape[0]
    filter_count, chan_count, shard_len = inputs.shape
    ctx_count = lax.axis_size("ctx")
    my_index = lax.axis_index("ctx")
    total_len = shard_len * ctx_count
    per_dev = filter_count * chan_count // ctx_count
    per_filter = chan_count // per_dev
    block_len = 128
    block_count = total_len // block_len

    send = jnp.concatenate(
        [
            grad_out.reshape(ctx_count, per_dev, shard_len),
            inputs.reshape(ctx_count, per_dev, shard_len),
            jnp.repeat(long_filter, per_filter, axis=0)[:, None, :],
        ],
        axis=1,
    )
    recv = relay(send, 16, 0)
    seqs = recv.transpose(1, 0, 2).reshape(2 * per_dev + 1, total_len)
    grad_seq = seqs[:per_dev]
    in_seq = seqs[per_dev : 2 * per_dev].astype(jnp.float32)
    filt_seq = seqs[2 * per_dev :]
    taps = short_filter.reshape(tap_count, ctx_count, per_dev)
    taps = lax.dynamic_index_in_dim(taps, my_index, axis=1, keepdims=False)

    hidden = sum(
        (taps[offset][:, None] * delayed(in_seq, offset, total_len) for offset in range(tap_count))
    )
    hidden = hidden.astype(jnp.bfloat16)

    groups = lax.axis_size("ch")
    got = fused(
        grad_seq,
        jnp.concatenate([filt_seq, hidden], axis=0),
        in_seq,
        taps,
        groups,
        block_len,
        1,
    )
    grad_in_out = got[:, :per_dev].reshape(filter_count, chan_count, shard_len)
    grad_in_out = grad_in_out.astype(jnp.bfloat16)
    grad_long_out = got[:, per_dev + 1].reshape(filter_count, per_filter, shard_len).sum(axis=1)
    short_all = got[:, per_dev, : tap_count * per_dev].reshape(ctx_count, tap_count, per_dev)
    grad_short_out = short_all.transpose(1, 0, 2).reshape(tap_count, filter_count, chan_count)
    return (grad_in_out, grad_long_out, grad_short_out)


def solution(mesh):
    in_specs = (P(None, "ch", "ctx"), P(None, None, "ch"), P(None, "ctx"), P(None, "ch", "ctx"))
    out_specs = (P(None, "ch", "ctx"), P(None, "ctx"), P(None, None, "ch"))
    return jax.shard_map(
        per_device, mesh=mesh, in_specs=in_specs, out_specs=out_specs, check_vma=False
    )
```

```python
import jax
import jax.numpy as jnp
from jax import lax
from jax.experimental import pallas as pl
from jax.experimental.pallas import tpu as pltpu
from jax.sharding import PartitionSpec as P


def delayed(values, by, length):
    return jnp.pad(values, ((0, 0), (by, 0)))[:, :length]


def conv_kernel(grad_ref, rev_ref, hidden_ref, long_ref, hankel, toeplitz):
    chans, _, block_len = grad_ref.shape
    block_count = hidden_ref.shape[1]
    sources, lags, _ = rev_ref.shape

    def fill_hankel(lag, carry):
        col = pl.multiple_of(lag * block_len, block_len)
        for g in range(chans):
            hankel[g, :, pl.ds(col, block_len)] = grad_ref[g, pl.ds(lag, block_count), :].astype(
                hankel.dtype
            )
        return carry

    lax.fori_loop(0, lags, fill_hankel, 0)

    def fill_toeplitz(lag, carry):
        row = pl.multiple_of(lag * block_len, block_len)
        for s in range(sources):
            line = rev_ref[s, pl.ds(lag, 1), :]
            tiled = jnp.broadcast_to(line, (block_len, 2 * block_len))
            skewed = pltpu.roll(tiled, block_len + 1, 1, stride=1, stride_axis=0)
            toeplitz[s, pl.ds(row, block_len), :] = skewed[:, :block_len].astype(toeplitz.dtype)
        return carry

    lax.fori_loop(0, lags, fill_toeplitz, 0)

    for g in range(chans):
        hidden_ref[g] = jnp.dot(hankel[g], toeplitz[0], preferred_element_type=jnp.float32)
    acc = jnp.dot(hankel[0], toeplitz[1], preferred_element_type=jnp.float32)
    for g in range(1, chans):
        acc = acc + jnp.dot(hankel[g], toeplitz[1 + g], preferred_element_type=jnp.float32)
    long_ref[...] = acc


def correlate_all(grad_seq, sources, block_len):
    chans, total_len = grad_seq.shape
    count = sources.shape[0]
    block_count = total_len // block_len
    grad_pad = jnp.pad(
        grad_seq.astype(jnp.float32).reshape(chans, block_count, block_len),
        ((0, 0), (0, block_count), (0, 0)),
    )
    blocks = sources.reshape(count, block_count, block_len)
    padded = jnp.pad(blocks, ((0, 0), (1, 1), (0, 0)))
    pairs = jnp.concatenate([padded[:, :-1], padded[:, 1:]], axis=2)
    rev = pairs[..., ::-1].astype(jnp.float32)
    lags = block_count + 1
    hidden, long = pl.pallas_call(
        conv_kernel,
        out_shape=(
            jax.ShapeDtypeStruct((chans, block_count, block_len), jnp.float32),
            jax.ShapeDtypeStruct((block_count, block_len), jnp.float32),
        ),
        scratch_shapes=[
            pltpu.VMEM((chans, block_count, lags * block_len), jnp.bfloat16),
            pltpu.VMEM((count, lags * block_len, block_len), jnp.bfloat16),
        ],
        compiler_params=pltpu.CompilerParams(vmem_limit_bytes=48 * 1024 * 1024),
    )(grad_pad, rev)
    return hidden.reshape(chans, total_len), long.reshape(total_len)


def swap_kernel(send_ref, out_ref, landed, local_sem, send_sem, recv_sem):
    count = send_ref.shape[0]
    me = lax.axis_index("ctx")
    mine = lax.axis_index("ch")
    barrier = pltpu.get_barrier_semaphore()
    for step in range(1, count):
        peer = lax.rem(me + step, count)
        pl.semaphore_signal(
            barrier, 1, device_id=(peer, mine), device_id_type=pl.DeviceIdType.MESH
        )
    pl.semaphore_wait(barrier, count - 1)
    local = pltpu.make_async_copy(send_ref.at[me], landed.at[me], local_sem)
    local.start()
    copies = []
    for step in range(1, count):
        peer = lax.rem(me + step, count)
        copy = pltpu.make_async_remote_copy(
            src_ref=send_ref.at[peer],
            dst_ref=landed.at[me],
            send_sem=send_sem.at[peer],
            recv_sem=recv_sem.at[me],
            device_id=(peer, mine),
            device_id_type=pl.DeviceIdType.MESH,
        )
        copy.start()
        copies.append(copy)
    local.wait()
    for copy in copies:
        copy.wait_send()
    for step in range(1, count):
        source = lax.rem(me + step, count)
        pltpu.make_async_remote_copy(
            src_ref=send_ref.at[source],
            dst_ref=landed.at[source],
            send_sem=send_sem.at[source],
            recv_sem=recv_sem.at[source],
            device_id=(source, mine),
            device_id_type=pl.DeviceIdType.MESH,
        ).wait_recv()
    out_ref[...] = landed[...]


def swap(chunks, collective_id):
    return pl.pallas_call(
        swap_kernel,
        out_shape=jax.ShapeDtypeStruct(chunks.shape, chunks.dtype),
        in_specs=[pl.BlockSpec(memory_space=pltpu.VMEM)],
        out_specs=pl.BlockSpec(memory_space=pltpu.VMEM),
        scratch_shapes=[
            pltpu.VMEM(chunks.shape, chunks.dtype),
            pltpu.SemaphoreType.DMA,
            pltpu.SemaphoreType.DMA((chunks.shape[0],)),
            pltpu.SemaphoreType.DMA((chunks.shape[0],)),
        ],
        compiler_params=pltpu.CompilerParams(collective_id=collective_id, has_side_effects=True),
    )(chunks)


def gather_kernel(
    rows_ref, long_ref, rows_out, long_out, rows_in, long_in, local_sems,
    rows_send, rows_recv, long_send, long_recv,
):
    count = rows_ref.shape[0]
    groups = lax.axis_size("ch")
    me = lax.axis_index("ctx")
    mine = lax.axis_index("ch")
    mesh_id = pl.DeviceIdType.MESH
    peers = [(c, h) for c in range(count) for h in range(groups) if (c, h) != (0, 0)]
    barrier = pltpu.get_barrier_semaphore()
    for step_c, step_h in peers:
        peer, other = lax.rem(me + step_c, count), lax.rem(mine + step_h, groups)
        pl.semaphore_signal(barrier, 1, device_id=(peer, other), device_id_type=mesh_id)
    pl.semaphore_wait(barrier, len(peers))
    local_rows = pltpu.make_async_copy(rows_ref.at[me], rows_in.at[me], local_sems.at[0])
    local_long = pltpu.make_async_copy(long_ref.at[me], long_in.at[me, mine], local_sems.at[1])
    local_rows.start()
    local_long.start()
    copies = []
    for step in range(1, count):
        peer = lax.rem(me + step, count)
        copy = pltpu.make_async_remote_copy(
            src_ref=rows_ref.at[peer],
            dst_ref=rows_in.at[me],
            send_sem=rows_send.at[peer],
            recv_sem=rows_recv.at[me],
            device_id=(peer, mine),
            device_id_type=mesh_id,
        )
        copy.start()
        copies.append(copy)
    for step_c, step_h in peers:
        peer, other = lax.rem(me + step_c, count), lax.rem(mine + step_h, groups)
        copy = pltpu.make_async_remote_copy(
            src_ref=long_ref.at[peer],
            dst_ref=long_in.at[me, mine],
            send_sem=long_send.at[peer * groups + other],
            recv_sem=long_recv.at[me * groups + mine],
            device_id=(peer, other),
            device_id_type=mesh_id,
        )
        copy.start()
        copies.append(copy)
    local_rows.wait()
    local_long.wait()
    for copy in copies:
        copy.wait_send()
    for step in range(1, count):
        source = lax.rem(me + step, count)
        pltpu.make_async_remote_copy(
            src_ref=rows_ref.at[source],
            dst_ref=rows_in.at[source],
            send_sem=rows_send.at[source],
            recv_sem=rows_recv.at[source],
            device_id=(source, mine),
            device_id_type=mesh_id,
        ).wait_recv()
    for step_c, step_h in peers:
        source, other = lax.rem(me + step_c, count), lax.rem(mine + step_h, groups)
        pltpu.make_async_remote_copy(
            src_ref=long_ref.at[source],
            dst_ref=long_in.at[source, other],
            send_sem=long_send.at[source * groups + other],
            recv_sem=long_recv.at[source * groups + other],
            device_id=(source, other),
            device_id_type=mesh_id,
        ).wait_recv()
    rows_out[...] = rows_in[...]
    long_out[...] = long_in[...]


def gather(rows, longs, groups, collective_id):
    count = rows.shape[0]
    long_shape = (count, groups) + longs.shape[1:]
    vmem = pl.BlockSpec(memory_space=pltpu.VMEM)
    return pl.pallas_call(
        gather_kernel,
        out_shape=(
            jax.ShapeDtypeStruct(rows.shape, rows.dtype),
            jax.ShapeDtypeStruct(long_shape, longs.dtype),
        ),
        in_specs=[vmem, vmem],
        out_specs=(vmem, vmem),
        scratch_shapes=[
            pltpu.VMEM(rows.shape, rows.dtype),
            pltpu.VMEM(long_shape, longs.dtype),
            pltpu.SemaphoreType.DMA((2,)),
            pltpu.SemaphoreType.DMA((count,)),
            pltpu.SemaphoreType.DMA((count,)),
            pltpu.SemaphoreType.DMA((count * groups,)),
            pltpu.SemaphoreType.DMA((count * groups,)),
        ],
        compiler_params=pltpu.CompilerParams(collective_id=collective_id, has_side_effects=True),
    )(rows, longs)


def fused_kernel(
    grad_ref, rev_ref, in_ref, taps_ref, short_out, grad_in_out, long_out,
    hankel, toeplitz, grad_buf, rows_buf, ch_in, rows_in, local_sems,
    rows_send, rows_recv, ch_send, ch_recv,
):
    count = rows_buf.shape[0]
    chans, _, block_len = grad_ref.shape
    block_count = count
    sources, lags, _ = rev_ref.shape
    tap_count = taps_ref.shape[0]
    groups = lax.axis_size("ch")
    me = lax.axis_index("ctx")
    mine = lax.axis_index("ch")
    mesh_id = pl.DeviceIdType.MESH
    peers = [(c, 0) for c in range(1, count)] + [(0, h) for h in range(1, groups)]
    barrier = pltpu.get_barrier_semaphore()
    for step_c, step_h in peers:
        peer, other = lax.rem(me + step_c, count), lax.rem(mine + step_h, groups)
        pl.semaphore_signal(barrier, 1, device_id=(peer, other), device_id_type=mesh_id)

    def fill_hankel(lag, carry):
        col = pl.multiple_of(lag * block_len, block_len)
        for g in range(chans):
            hankel[g, :, pl.ds(col, block_len)] = grad_ref[g, pl.ds(lag, block_count), :].astype(
                hankel.dtype
            )
        return carry

    lax.fori_loop(0, lags, fill_hankel, 0)

    def fill_toeplitz(picked):
        def fill(lag, carry):
            row = pl.multiple_of(lag * block_len, block_len)
            for s in picked:
                line = rev_ref[s, pl.ds(lag, 1), :]
                tiled = jnp.broadcast_to(line, (block_len, 2 * block_len))
                skewed = pltpu.roll(tiled, block_len + 1, 1, stride=1, stride_axis=0)
                toeplitz[s, pl.ds(row, block_len), :] = skewed[:, :block_len].astype(
                    toeplitz.dtype
                )
            return carry

        lax.fori_loop(0, lags, fill, 0)

    fill_toeplitz(range(1, sources))

    acc = jnp.dot(hankel[0], toeplitz[1], preferred_element_type=jnp.float32)
    for g in range(1, chans):
        acc = acc + jnp.dot(hankel[g], toeplitz[1 + g], preferred_element_type=jnp.float32)
    ch_in[mine] = acc
    pl.semaphore_wait(barrier, len(peers))
    partials = []
    for step in range(1, groups):
        other = lax.rem(mine + step, groups)
        copy = pltpu.make_async_remote_copy(
            src_ref=ch_in.at[mine],
            dst_ref=ch_in.at[mine],
            send_sem=ch_send.at[other],
            recv_sem=ch_recv.at[mine],
            device_id=(me, other),
            device_id_type=mesh_id,
        )
        copy.start()
        partials.append(copy)
    fill_toeplitz(range(1))

    lane = lax.broadcasted_iota(jnp.int32, (block_count, block_len), 1)
    short_row = jnp.zeros((block_count, block_len), jnp.float32)
    grad_buf[...] = jnp.zeros_like(grad_buf)
    for g in range(chans):
        hidden_grad = jnp.dot(hankel[g], toeplitz[0], preferred_element_type=jnp.float32)
        grad_buf[g, pl.ds(0, block_count), :] = hidden_grad
        following = grad_buf[g, pl.ds(1, block_count), :]
        total = taps_ref[0, g] * hidden_grad
        for offset in range(1, tap_count):
            here = pltpu.roll(hidden_grad, block_len - offset, 1)
            there = pltpu.roll(following, block_len - offset, 1)
            total = total + taps_ref[offset, g] * jnp.where(
                lane >= block_len - offset, there, here
            )
        rows_buf[:, g, :] = total.astype(jnp.bfloat16).astype(jnp.float32)
        current = in_ref[g, pl.ds(1, block_count), :]
        previous = in_ref[g, pl.ds(0, block_count), :]
        for offset in range(tap_count):
            if offset == 0:
                delayed_in = current
            else:
                delayed_in = jnp.where(
                    lane < offset,
                    pltpu.roll(previous, offset, 1),
                    pltpu.roll(current, offset, 1),
                )
            value = jnp.sum(hidden_grad * delayed_in)
            short_row = jnp.where(lane == offset * chans + g, value, short_row)
    rows_buf[:, chans, :] = short_row

    for copy in partials:
        copy.wait_send()
    for step in range(1, groups):
        source = lax.rem(mine + step, groups)
        pltpu.make_async_remote_copy(
            src_ref=ch_in.at[source],
            dst_ref=ch_in.at[source],
            send_sem=ch_send.at[source],
            recv_sem=ch_recv.at[source],
            device_id=(me, source),
            device_id_type=mesh_id,
        ).wait_recv()
    summed = ch_in[0]
    for h in range(1, groups):
        summed = summed + ch_in[h]
    rows_buf[:, chans + 1, :] = summed

    pairs = rows_in.shape[1]

    def landing(index):
        return rows_in.at[index // pairs, lax.rem(index, pairs)]

    local_rows = pltpu.make_async_copy(rows_buf.at[me], landing(me), local_sems.at[0])
    local_rows.start()
    copies = []
    for step in range(1, count):
        peer = lax.rem(me + step, count)
        copy = pltpu.make_async_remote_copy(
            src_ref=rows_buf.at[peer],
            dst_ref=landing(me),
            send_sem=rows_send.at[peer],
            recv_sem=rows_recv.at[me],
            device_id=(peer, mine),
            device_id_type=mesh_id,
        )
        copy.start()
        copies.append(copy)
    local_rows.wait()
    for copy in copies:
        copy.wait_send()
    for step in range(1, count):
        source = lax.rem(me + step, count)
        pltpu.make_async_remote_copy(
            src_ref=rows_buf.at[source],
            dst_ref=landing(source),
            send_sem=rows_send.at[source],
            recv_sem=rows_recv.at[source],
            device_id=(source, mine),
            device_id_type=mesh_id,
        ).wait_recv()
    for pair in range(pairs):
        short_out[:, pair, :] = rows_in[:, pair, chans, :]
        for g in range(chans):
            grad_in_out[:, pair * chans + g, :] = rows_in[:, pair, g, :].astype(grad_in_out.dtype)
    total = rows_in[:, 0, chans + 1, :]
    for pair in range(1, pairs):
        total = total + rows_in[:, pair, chans + 1, :]
    long_out[...] = total


def fused(grad_seq, sources, in_seq, taps, groups, filter_count, block_len, collective_id):
    chans, total_len = grad_seq.shape
    count = sources.shape[0]
    block_count = total_len // block_len
    grad_pad = jnp.pad(
        grad_seq.astype(jnp.float32).reshape(chans, block_count, block_len),
        ((0, 0), (0, block_count), (0, 0)),
    )
    blocks = sources.reshape(count, block_count, block_len)
    padded = jnp.pad(blocks, ((0, 0), (1, 1), (0, 0)))
    pairs = jnp.concatenate([padded[:, :-1], padded[:, 1:]], axis=2)
    rev = pairs[..., ::-1].astype(jnp.float32)
    in_pad = jnp.pad(in_seq.reshape(chans, block_count, block_len), ((0, 0), (1, 0), (0, 0)))
    lags = block_count + 1
    rows_shape = (block_count, chans + 2, block_len)
    pairs = block_count // filter_count
    landed_shape = (filter_count, pairs, chans + 2, block_len)
    vmem = pl.BlockSpec(memory_space=pltpu.VMEM)
    return pl.pallas_call(
        fused_kernel,
        out_shape=(
            jax.ShapeDtypeStruct((filter_count, pairs, block_len), jnp.float32),
            jax.ShapeDtypeStruct((filter_count, pairs * chans, block_len), jnp.bfloat16),
            jax.ShapeDtypeStruct((filter_count, block_len), jnp.float32),
        ),
        in_specs=[vmem, vmem, vmem, pl.BlockSpec(memory_space=pltpu.SMEM)],
        out_specs=(vmem, vmem, vmem),
        scratch_shapes=[
            pltpu.VMEM((chans, block_count, lags * block_len), jnp.bfloat16),
            pltpu.VMEM((count, lags * block_len, block_len), jnp.bfloat16),
            pltpu.VMEM((chans, block_count + 8, block_len), jnp.float32),
            pltpu.VMEM(rows_shape, jnp.float32),
            pltpu.VMEM((groups, block_count, block_len), jnp.float32),
            pltpu.VMEM(landed_shape, jnp.float32),
            pltpu.SemaphoreType.DMA((1,)),
            pltpu.SemaphoreType.DMA((block_count,)),
            pltpu.SemaphoreType.DMA((block_count,)),
            pltpu.SemaphoreType.DMA((groups,)),
            pltpu.SemaphoreType.DMA((groups,)),
        ],
        compiler_params=pltpu.CompilerParams(
            collective_id=collective_id,
            has_side_effects=True,
            vmem_limit_bytes=48 * 1024 * 1024,
        ),
    )(grad_pad, rev, in_pad, taps)


def relay_kernel(send_ref, out_ref, middle, landed, local_sems, first_send, first_recv, second_send, second_recv):
    firsts, seconds = send_ref.shape[0], send_ref.shape[1]
    me = lax.axis_index("ctx")
    mine = lax.axis_index("ch")
    first, second = me // seconds, lax.rem(me, seconds)
    mesh_id = pl.DeviceIdType.MESH

    def place(f, s):
        return f * seconds + s

    barrier = pltpu.get_barrier_semaphore()
    for step in range(1, firsts):
        peer = place(lax.rem(first + step, firsts), second)
        pl.semaphore_signal(barrier, 1, device_id=(peer, mine), device_id_type=mesh_id)
    for step in range(1, seconds):
        peer = place(first, lax.rem(second + step, seconds))
        pl.semaphore_signal(barrier, 1, device_id=(peer, mine), device_id_type=mesh_id)
    pl.semaphore_wait(barrier, firsts - 1 + seconds - 1)
    local = pltpu.make_async_copy(send_ref.at[first], middle.at[:, first], local_sems.at[0])
    local.start()
    copies = []
    for step in range(1, firsts):
        target = lax.rem(first + step, firsts)
        copy = pltpu.make_async_remote_copy(
            src_ref=send_ref.at[target],
            dst_ref=middle.at[:, first],
            send_sem=first_send.at[target],
            recv_sem=first_recv.at[first],
            device_id=(place(target, second), mine),
            device_id_type=mesh_id,
        )
        copy.start()
        copies.append(copy)
    local.wait()
    for copy in copies:
        copy.wait_send()
    for step in range(1, firsts):
        source = lax.rem(first + step, firsts)
        pltpu.make_async_remote_copy(
            src_ref=send_ref.at[source],
            dst_ref=middle.at[:, source],
            send_sem=first_send.at[source],
            recv_sem=first_recv.at[source],
            device_id=(place(source, second), mine),
            device_id_type=mesh_id,
        ).wait_recv()
    local = pltpu.make_async_copy(middle.at[second], landed.at[second], local_sems.at[1])
    local.start()
    copies = []
    for step in range(1, seconds):
        target = lax.rem(second + step, seconds)
        copy = pltpu.make_async_remote_copy(
            src_ref=middle.at[target],
            dst_ref=landed.at[second],
            send_sem=second_send.at[target],
            recv_sem=second_recv.at[second],
            device_id=(place(first, target), mine),
            device_id_type=mesh_id,
        )
        copy.start()
        copies.append(copy)
    local.wait()
    for copy in copies:
        copy.wait_send()
    for step in range(1, seconds):
        source = lax.rem(second + step, seconds)
        pltpu.make_async_remote_copy(
            src_ref=middle.at[source],
            dst_ref=landed.at[source],
            send_sem=second_send.at[source],
            recv_sem=second_recv.at[source],
            device_id=(place(first, source), mine),
            device_id_type=mesh_id,
        ).wait_recv()
    out_ref[...] = landed[...]


def relay(chunks, inner, collective_id):
    count = chunks.shape[0]
    outer = count // inner
    rest = chunks.shape[1:]
    by_first = chunks.reshape((outer, inner) + rest)
    first_shape = (outer, inner) + rest
    second_shape = (inner, outer) + rest
    landed = pl.pallas_call(
        relay_kernel,
        out_shape=jax.ShapeDtypeStruct(second_shape, chunks.dtype),
        in_specs=[pl.BlockSpec(memory_space=pltpu.VMEM)],
        out_specs=pl.BlockSpec(memory_space=pltpu.VMEM),
        scratch_shapes=[
            pltpu.VMEM(second_shape, chunks.dtype),
            pltpu.VMEM(second_shape, chunks.dtype),
            pltpu.SemaphoreType.DMA((2,)),
            pltpu.SemaphoreType.DMA((outer,)),
            pltpu.SemaphoreType.DMA((outer,)),
            pltpu.SemaphoreType.DMA((inner,)),
            pltpu.SemaphoreType.DMA((inner,)),
        ],
        compiler_params=pltpu.CompilerParams(collective_id=collective_id, has_side_effects=True),
    )(by_first)
    return landed.swapaxes(0, 1).reshape(chunks.shape)


def per_device(inputs, short_filter, long_filter, grad_out):
    tap_count = short_filter.shape[0]
    filter_count, chan_count, shard_len = inputs.shape
    ctx_count = lax.axis_size("ctx")
    my_index = lax.axis_index("ctx")
    total_len = shard_len * ctx_count
    per_dev = filter_count * chan_count // ctx_count
    per_filter = chan_count // per_dev
    block_len = 128
    block_count = total_len // block_len

    send = jnp.concatenate(
        [
            grad_out.reshape(ctx_count, per_dev, shard_len),
            inputs.reshape(ctx_count, per_dev, shard_len),
            jnp.repeat(long_filter, per_filter, axis=0)[:, None, :],
        ],
        axis=1,
    )
    recv = relay(send, 8, 0)
    seqs = recv.transpose(1, 0, 2).reshape(2 * per_dev + 1, total_len)
    grad_seq = seqs[:per_dev]
    in_seq = seqs[per_dev : 2 * per_dev].astype(jnp.float32)
    filt_seq = seqs[2 * per_dev :]
    taps = short_filter.reshape(tap_count, ctx_count, per_dev)
    taps = lax.dynamic_index_in_dim(taps, my_index, axis=1, keepdims=False)

    hidden = sum(
        (taps[offset][:, None] * delayed(in_seq, offset, total_len) for offset in range(tap_count))
    )
    hidden = hidden.astype(jnp.bfloat16)

    groups = lax.axis_size("ch")
    short_rows, grad_in_out, grad_long_out = fused(
        grad_seq,
        jnp.concatenate([filt_seq, hidden], axis=0),
        in_seq,
        taps,
        groups,
        filter_count,
        block_len,
        1,
    )
    short_all = short_rows.reshape(ctx_count, shard_len)[:, : tap_count * per_dev]
    short_all = short_all.reshape(ctx_count, tap_count, per_dev)
    grad_short_out = short_all.transpose(1, 0, 2).reshape(tap_count, filter_count, chan_count)
    return (grad_in_out, grad_long_out, grad_short_out)


def solution(mesh):
    in_specs = (P(None, "ch", "ctx"), P(None, None, "ch"), P(None, "ctx"), P(None, "ch", "ctx"))
    out_specs = (P(None, "ch", "ctx"), P(None, "ctx"), P(None, None, "ch"))
    return jax.shard_map(
        per_device, mesh=mesh, in_specs=in_specs, out_specs=out_specs, check_vma=False
    )
```

```python
import jax
import jax.numpy as jnp
from jax import lax
from jax.experimental import pallas as pl
from jax.experimental.pallas import tpu as pltpu
from jax.sharding import PartitionSpec as P


def delayed(values, by, length):
    return jnp.pad(values, ((0, 0), (by, 0)))[:, :length]


def conv_kernel(grad_ref, rev_ref, hidden_ref, long_ref, hankel, toeplitz):
    chans, _, block_len = grad_ref.shape
    block_count = hidden_ref.shape[1]
    sources, lags, _ = rev_ref.shape

    def fill_hankel(lag, carry):
        col = pl.multiple_of(lag * block_len, block_len)
        for g in range(chans):
            hankel[g, :, pl.ds(col, block_len)] = grad_ref[g, pl.ds(lag, block_count), :].astype(
                hankel.dtype
            )
        return carry

    lax.fori_loop(0, lags, fill_hankel, 0)

    def fill_toeplitz(lag, carry):
        row = pl.multiple_of(lag * block_len, block_len)
        for s in range(sources):
            line = rev_ref[s, pl.ds(lag, 1), :]
            tiled = jnp.broadcast_to(line, (block_len, 2 * block_len))
            skewed = pltpu.roll(tiled, block_len + 1, 1, stride=1, stride_axis=0)
            toeplitz[s, pl.ds(row, block_len), :] = skewed[:, :block_len].astype(toeplitz.dtype)
        return carry

    lax.fori_loop(0, lags, fill_toeplitz, 0)

    for g in range(chans):
        hidden_ref[g] = jnp.dot(hankel[g], toeplitz[0], preferred_element_type=jnp.float32)
    acc = jnp.dot(hankel[0], toeplitz[1], preferred_element_type=jnp.float32)
    for g in range(1, chans):
        acc = acc + jnp.dot(hankel[g], toeplitz[1 + g], preferred_element_type=jnp.float32)
    long_ref[...] = acc


def correlate_all(grad_seq, sources, block_len):
    chans, total_len = grad_seq.shape
    count = sources.shape[0]
    block_count = total_len // block_len
    grad_pad = jnp.pad(
        grad_seq.astype(jnp.float32).reshape(chans, block_count, block_len),
        ((0, 0), (0, block_count), (0, 0)),
    )
    blocks = sources.reshape(count, block_count, block_len)
    padded = jnp.pad(blocks, ((0, 0), (1, 1), (0, 0)))
    pairs = jnp.concatenate([padded[:, :-1], padded[:, 1:]], axis=2)
    rev = pairs[..., ::-1].astype(jnp.float32)
    lags = block_count + 1
    hidden, long = pl.pallas_call(
        conv_kernel,
        out_shape=(
            jax.ShapeDtypeStruct((chans, block_count, block_len), jnp.float32),
            jax.ShapeDtypeStruct((block_count, block_len), jnp.float32),
        ),
        scratch_shapes=[
            pltpu.VMEM((chans, block_count, lags * block_len), jnp.bfloat16),
            pltpu.VMEM((count, lags * block_len, block_len), jnp.bfloat16),
        ],
        compiler_params=pltpu.CompilerParams(vmem_limit_bytes=48 * 1024 * 1024),
    )(grad_pad, rev)
    return hidden.reshape(chans, total_len), long.reshape(total_len)


def swap_kernel(send_ref, out_ref, landed, local_sem, send_sem, recv_sem):
    count = send_ref.shape[0]
    me = lax.axis_index("ctx")
    mine = lax.axis_index("ch")
    barrier = pltpu.get_barrier_semaphore()
    for step in range(1, count):
        peer = lax.rem(me + step, count)
        pl.semaphore_signal(
            barrier, 1, device_id=(peer, mine), device_id_type=pl.DeviceIdType.MESH
        )
    pl.semaphore_wait(barrier, count - 1)
    local = pltpu.make_async_copy(send_ref.at[me], landed.at[me], local_sem)
    local.start()
    copies = []
    for step in range(1, count):
        peer = lax.rem(me + step, count)
        copy = pltpu.make_async_remote_copy(
            src_ref=send_ref.at[peer],
            dst_ref=landed.at[me],
            send_sem=send_sem.at[peer],
            recv_sem=recv_sem.at[me],
            device_id=(peer, mine),
            device_id_type=pl.DeviceIdType.MESH,
        )
        copy.start()
        copies.append(copy)
    local.wait()
    for copy in copies:
        copy.wait_send()
    for step in range(1, count):
        source = lax.rem(me + step, count)
        pltpu.make_async_remote_copy(
            src_ref=send_ref.at[source],
            dst_ref=landed.at[source],
            send_sem=send_sem.at[source],
            recv_sem=recv_sem.at[source],
            device_id=(source, mine),
            device_id_type=pl.DeviceIdType.MESH,
        ).wait_recv()
    out_ref[...] = landed[...]


def swap(chunks, collective_id):
    return pl.pallas_call(
        swap_kernel,
        out_shape=jax.ShapeDtypeStruct(chunks.shape, chunks.dtype),
        in_specs=[pl.BlockSpec(memory_space=pltpu.VMEM)],
        out_specs=pl.BlockSpec(memory_space=pltpu.VMEM),
        scratch_shapes=[
            pltpu.VMEM(chunks.shape, chunks.dtype),
            pltpu.SemaphoreType.DMA,
            pltpu.SemaphoreType.DMA((chunks.shape[0],)),
            pltpu.SemaphoreType.DMA((chunks.shape[0],)),
        ],
        compiler_params=pltpu.CompilerParams(collective_id=collective_id, has_side_effects=True),
    )(chunks)


def gather_kernel(
    rows_ref, long_ref, rows_out, long_out, rows_in, long_in, local_sems,
    rows_send, rows_recv, long_send, long_recv,
):
    count = rows_ref.shape[0]
    groups = lax.axis_size("ch")
    me = lax.axis_index("ctx")
    mine = lax.axis_index("ch")
    mesh_id = pl.DeviceIdType.MESH
    peers = [(c, h) for c in range(count) for h in range(groups) if (c, h) != (0, 0)]
    barrier = pltpu.get_barrier_semaphore()
    for step_c, step_h in peers:
        peer, other = lax.rem(me + step_c, count), lax.rem(mine + step_h, groups)
        pl.semaphore_signal(barrier, 1, device_id=(peer, other), device_id_type=mesh_id)
    pl.semaphore_wait(barrier, len(peers))
    local_rows = pltpu.make_async_copy(rows_ref.at[me], rows_in.at[me], local_sems.at[0])
    local_long = pltpu.make_async_copy(long_ref.at[me], long_in.at[me, mine], local_sems.at[1])
    local_rows.start()
    local_long.start()
    copies = []
    for step in range(1, count):
        peer = lax.rem(me + step, count)
        copy = pltpu.make_async_remote_copy(
            src_ref=rows_ref.at[peer],
            dst_ref=rows_in.at[me],
            send_sem=rows_send.at[peer],
            recv_sem=rows_recv.at[me],
            device_id=(peer, mine),
            device_id_type=mesh_id,
        )
        copy.start()
        copies.append(copy)
    for step_c, step_h in peers:
        peer, other = lax.rem(me + step_c, count), lax.rem(mine + step_h, groups)
        copy = pltpu.make_async_remote_copy(
            src_ref=long_ref.at[peer],
            dst_ref=long_in.at[me, mine],
            send_sem=long_send.at[peer * groups + other],
            recv_sem=long_recv.at[me * groups + mine],
            device_id=(peer, other),
            device_id_type=mesh_id,
        )
        copy.start()
        copies.append(copy)
    local_rows.wait()
    local_long.wait()
    for copy in copies:
        copy.wait_send()
    for step in range(1, count):
        source = lax.rem(me + step, count)
        pltpu.make_async_remote_copy(
            src_ref=rows_ref.at[source],
            dst_ref=rows_in.at[source],
            send_sem=rows_send.at[source],
            recv_sem=rows_recv.at[source],
            device_id=(source, mine),
            device_id_type=mesh_id,
        ).wait_recv()
    for step_c, step_h in peers:
        source, other = lax.rem(me + step_c, count), lax.rem(mine + step_h, groups)
        pltpu.make_async_remote_copy(
            src_ref=long_ref.at[source],
            dst_ref=long_in.at[source, other],
            send_sem=long_send.at[source * groups + other],
            recv_sem=long_recv.at[source * groups + other],
            device_id=(source, other),
            device_id_type=mesh_id,
        ).wait_recv()
    rows_out[...] = rows_in[...]
    long_out[...] = long_in[...]


def gather(rows, longs, groups, collective_id):
    count = rows.shape[0]
    long_shape = (count, groups) + longs.shape[1:]
    vmem = pl.BlockSpec(memory_space=pltpu.VMEM)
    return pl.pallas_call(
        gather_kernel,
        out_shape=(
            jax.ShapeDtypeStruct(rows.shape, rows.dtype),
            jax.ShapeDtypeStruct(long_shape, longs.dtype),
        ),
        in_specs=[vmem, vmem],
        out_specs=(vmem, vmem),
        scratch_shapes=[
            pltpu.VMEM(rows.shape, rows.dtype),
            pltpu.VMEM(long_shape, longs.dtype),
            pltpu.SemaphoreType.DMA((2,)),
            pltpu.SemaphoreType.DMA((count,)),
            pltpu.SemaphoreType.DMA((count,)),
            pltpu.SemaphoreType.DMA((count * groups,)),
            pltpu.SemaphoreType.DMA((count * groups,)),
        ],
        compiler_params=pltpu.CompilerParams(collective_id=collective_id, has_side_effects=True),
    )(rows, longs)


def fused_kernel(
    grad_ref, rev_ref, in_ref, taps_ref, short_out, grad_in_out, long_out,
    hankel, toeplitz, grad_buf, rows_buf, ch_in, rows_in, local_sems,
    rows_send, rows_recv, ch_send, ch_recv,
):
    count = rows_buf.shape[0]
    chans, _, block_len = grad_ref.shape
    block_count = count
    sources, lags, _ = rev_ref.shape
    tap_count = taps_ref.shape[0]
    groups = lax.axis_size("ch")
    me = lax.axis_index("ctx")
    mine = lax.axis_index("ch")
    mesh_id = pl.DeviceIdType.MESH
    peers = [(c, 0) for c in range(1, count)] + [(0, h) for h in range(1, groups)]
    barrier = pltpu.get_barrier_semaphore()
    for step_c, step_h in peers:
        peer, other = lax.rem(me + step_c, count), lax.rem(mine + step_h, groups)
        pl.semaphore_signal(barrier, 1, device_id=(peer, other), device_id_type=mesh_id)

    def fill_hankel(lag, carry):
        col = pl.multiple_of(lag * block_len, block_len)
        for g in range(chans):
            hankel[g, :, pl.ds(col, block_len)] = grad_ref[g, pl.ds(lag, block_count), :].astype(
                hankel.dtype
            )
        return carry

    lax.fori_loop(0, lags, fill_hankel, 0)

    def fill_toeplitz(picked):
        def fill(lag, carry):
            row = pl.multiple_of(lag * block_len, block_len)
            for s in picked:
                line = rev_ref[s, pl.ds(lag, 1), :]
                tiled = jnp.broadcast_to(line, (block_len, 2 * block_len))
                skewed = pltpu.roll(tiled, block_len + 1, 1, stride=1, stride_axis=0)
                toeplitz[s, pl.ds(row, block_len), :] = skewed[:, :block_len].astype(
                    toeplitz.dtype
                )
            return carry

        lax.fori_loop(0, lags, fill, 0)

    fill_toeplitz(range(1, sources))

    acc = jnp.dot(hankel[0], toeplitz[1], preferred_element_type=jnp.float32)
    for g in range(1, chans):
        acc = acc + jnp.dot(hankel[g], toeplitz[1 + g], preferred_element_type=jnp.float32)
    ch_in[mine] = acc
    pl.semaphore_wait(barrier, len(peers))
    partials = []
    for step in range(1, groups):
        other = lax.rem(mine + step, groups)
        copy = pltpu.make_async_remote_copy(
            src_ref=ch_in.at[mine],
            dst_ref=ch_in.at[mine],
            send_sem=ch_send.at[other],
            recv_sem=ch_recv.at[mine],
            device_id=(me, other),
            device_id_type=mesh_id,
        )
        copy.start()
        partials.append(copy)
    fill_toeplitz(range(1))

    lane = lax.broadcasted_iota(jnp.int32, (block_count, block_len), 1)
    short_row = jnp.zeros((block_count, block_len), jnp.float32)
    grad_buf[...] = jnp.zeros_like(grad_buf)
    window = hankel.shape[2]
    hidden_all = jnp.dot(
        hankel[...].reshape(chans * block_count, window),
        toeplitz[0],
        preferred_element_type=jnp.float32,
    )
    for g in range(chans):
        hidden_grad = hidden_all[g * block_count : (g + 1) * block_count]
        grad_buf[g, pl.ds(0, block_count), :] = hidden_grad
        following = grad_buf[g, pl.ds(1, block_count), :]
        total = taps_ref[0, g] * hidden_grad
        for offset in range(1, tap_count):
            here = pltpu.roll(hidden_grad, block_len - offset, 1)
            there = pltpu.roll(following, block_len - offset, 1)
            total = total + taps_ref[offset, g] * jnp.where(
                lane >= block_len - offset, there, here
            )
        rows_buf[:, g, :] = total.astype(jnp.bfloat16).astype(jnp.float32)
        current = in_ref[g, pl.ds(1, block_count), :]
        previous = in_ref[g, pl.ds(0, block_count), :]
        for offset in range(tap_count):
            if offset == 0:
                delayed_in = current
            else:
                delayed_in = jnp.where(
                    lane < offset,
                    pltpu.roll(previous, offset, 1),
                    pltpu.roll(current, offset, 1),
                )
            value = jnp.sum(hidden_grad * delayed_in)
            short_row = jnp.where(lane == offset * chans + g, value, short_row)
    rows_buf[:, chans, :] = short_row

    for copy in partials:
        copy.wait_send()
    for step in range(1, groups):
        source = lax.rem(mine + step, groups)
        pltpu.make_async_remote_copy(
            src_ref=ch_in.at[source],
            dst_ref=ch_in.at[source],
            send_sem=ch_send.at[source],
            recv_sem=ch_recv.at[source],
            device_id=(me, source),
            device_id_type=mesh_id,
        ).wait_recv()
    summed = ch_in[0]
    for h in range(1, groups):
        summed = summed + ch_in[h]
    rows_buf[:, chans + 1, :] = summed

    pairs = rows_in.shape[1]

    def landing(index):
        return rows_in.at[index // pairs, lax.rem(index, pairs)]

    local_rows = pltpu.make_async_copy(rows_buf.at[me], landing(me), local_sems.at[0])
    local_rows.start()
    copies = []
    for step in range(1, count):
        peer = lax.rem(me + step, count)
        copy = pltpu.make_async_remote_copy(
            src_ref=rows_buf.at[peer],
            dst_ref=landing(me),
            send_sem=rows_send.at[peer],
            recv_sem=rows_recv.at[me],
            device_id=(peer, mine),
            device_id_type=mesh_id,
        )
        copy.start()
        copies.append(copy)
    local_rows.wait()
    for copy in copies:
        copy.wait_send()
    for step in range(1, count):
        source = lax.rem(me + step, count)
        pltpu.make_async_remote_copy(
            src_ref=rows_buf.at[source],
            dst_ref=landing(source),
            send_sem=rows_send.at[source],
            recv_sem=rows_recv.at[source],
            device_id=(source, mine),
            device_id_type=mesh_id,
        ).wait_recv()
    for pair in range(pairs):
        short_out[:, pair, :] = rows_in[:, pair, chans, :]
        for g in range(chans):
            grad_in_out[:, pair * chans + g, :] = rows_in[:, pair, g, :].astype(grad_in_out.dtype)
    total = rows_in[:, 0, chans + 1, :]
    for pair in range(1, pairs):
        total = total + rows_in[:, pair, chans + 1, :]
    long_out[...] = total


def fused(grad_seq, sources, in_seq, taps, groups, filter_count, block_len, collective_id):
    chans, total_len = grad_seq.shape
    count = sources.shape[0]
    block_count = total_len // block_len
    grad_pad = jnp.pad(
        grad_seq.astype(jnp.float32).reshape(chans, block_count, block_len),
        ((0, 0), (0, block_count), (0, 0)),
    )
    blocks = sources.reshape(count, block_count, block_len)
    padded = jnp.pad(blocks, ((0, 0), (1, 1), (0, 0)))
    pairs = jnp.concatenate([padded[:, :-1], padded[:, 1:]], axis=2)
    rev = pairs[..., ::-1].astype(jnp.float32)
    in_pad = jnp.pad(in_seq.reshape(chans, block_count, block_len), ((0, 0), (1, 0), (0, 0)))
    lags = block_count + 1
    rows_shape = (block_count, chans + 2, block_len)
    pairs = block_count // filter_count
    landed_shape = (filter_count, pairs, chans + 2, block_len)
    vmem = pl.BlockSpec(memory_space=pltpu.VMEM)
    return pl.pallas_call(
        fused_kernel,
        out_shape=(
            jax.ShapeDtypeStruct((filter_count, pairs, block_len), jnp.float32),
            jax.ShapeDtypeStruct((filter_count, pairs * chans, block_len), jnp.bfloat16),
            jax.ShapeDtypeStruct((filter_count, block_len), jnp.float32),
        ),
        in_specs=[vmem, vmem, vmem, pl.BlockSpec(memory_space=pltpu.SMEM)],
        out_specs=(vmem, vmem, vmem),
        scratch_shapes=[
            pltpu.VMEM((chans, block_count, lags * block_len), jnp.bfloat16),
            pltpu.VMEM((count, lags * block_len, block_len), jnp.bfloat16),
            pltpu.VMEM((chans, block_count + 8, block_len), jnp.float32),
            pltpu.VMEM(rows_shape, jnp.float32),
            pltpu.VMEM((groups, block_count, block_len), jnp.float32),
            pltpu.VMEM(landed_shape, jnp.float32),
            pltpu.SemaphoreType.DMA((1,)),
            pltpu.SemaphoreType.DMA((block_count,)),
            pltpu.SemaphoreType.DMA((block_count,)),
            pltpu.SemaphoreType.DMA((groups,)),
            pltpu.SemaphoreType.DMA((groups,)),
        ],
        compiler_params=pltpu.CompilerParams(
            collective_id=collective_id,
            has_side_effects=True,
            vmem_limit_bytes=48 * 1024 * 1024,
        ),
    )(grad_pad, rev, in_pad, taps)


def relay_kernel(send_ref, out_ref, middle, landed, local_sems, first_send, first_recv, second_send, second_recv):
    firsts, seconds = send_ref.shape[0], send_ref.shape[1]
    me = lax.axis_index("ctx")
    mine = lax.axis_index("ch")
    first, second = me // seconds, lax.rem(me, seconds)
    mesh_id = pl.DeviceIdType.MESH

    def place(f, s):
        return f * seconds + s

    barrier = pltpu.get_barrier_semaphore()
    for step in range(1, firsts):
        peer = place(lax.rem(first + step, firsts), second)
        pl.semaphore_signal(barrier, 1, device_id=(peer, mine), device_id_type=mesh_id)
    for step in range(1, seconds):
        peer = place(first, lax.rem(second + step, seconds))
        pl.semaphore_signal(barrier, 1, device_id=(peer, mine), device_id_type=mesh_id)
    pl.semaphore_wait(barrier, firsts - 1 + seconds - 1)
    local = pltpu.make_async_copy(send_ref.at[first], middle.at[:, first], local_sems.at[0])
    local.start()
    copies = []
    for step in range(1, firsts):
        target = lax.rem(first + step, firsts)
        copy = pltpu.make_async_remote_copy(
            src_ref=send_ref.at[target],
            dst_ref=middle.at[:, first],
            send_sem=first_send.at[target],
            recv_sem=first_recv.at[first],
            device_id=(place(target, second), mine),
            device_id_type=mesh_id,
        )
        copy.start()
        copies.append(copy)
    local.wait()
    for copy in copies:
        copy.wait_send()
    for step in range(1, firsts):
        source = lax.rem(first + step, firsts)
        pltpu.make_async_remote_copy(
            src_ref=send_ref.at[source],
            dst_ref=middle.at[:, source],
            send_sem=first_send.at[source],
            recv_sem=first_recv.at[source],
            device_id=(place(source, second), mine),
            device_id_type=mesh_id,
        ).wait_recv()
    local = pltpu.make_async_copy(middle.at[second], landed.at[second], local_sems.at[1])
    local.start()
    copies = []
    for step in range(1, seconds):
        target = lax.rem(second + step, seconds)
        copy = pltpu.make_async_remote_copy(
            src_ref=middle.at[target],
            dst_ref=landed.at[second],
            send_sem=second_send.at[target],
            recv_sem=second_recv.at[second],
            device_id=(place(first, target), mine),
            device_id_type=mesh_id,
        )
        copy.start()
        copies.append(copy)
    local.wait()
    for copy in copies:
        copy.wait_send()
    for step in range(1, seconds):
        source = lax.rem(second + step, seconds)
        pltpu.make_async_remote_copy(
            src_ref=middle.at[source],
            dst_ref=landed.at[source],
            send_sem=second_send.at[source],
            recv_sem=second_recv.at[source],
            device_id=(place(first, source), mine),
            device_id_type=mesh_id,
        ).wait_recv()
    out_ref[...] = landed[...]


def relay(chunks, inner, collective_id):
    count = chunks.shape[0]
    outer = count // inner
    rest = chunks.shape[1:]
    by_first = chunks.reshape((outer, inner) + rest)
    first_shape = (outer, inner) + rest
    second_shape = (inner, outer) + rest
    landed = pl.pallas_call(
        relay_kernel,
        out_shape=jax.ShapeDtypeStruct(second_shape, chunks.dtype),
        in_specs=[pl.BlockSpec(memory_space=pltpu.VMEM)],
        out_specs=pl.BlockSpec(memory_space=pltpu.VMEM),
        scratch_shapes=[
            pltpu.VMEM(second_shape, chunks.dtype),
            pltpu.VMEM(second_shape, chunks.dtype),
            pltpu.SemaphoreType.DMA((2,)),
            pltpu.SemaphoreType.DMA((outer,)),
            pltpu.SemaphoreType.DMA((outer,)),
            pltpu.SemaphoreType.DMA((inner,)),
            pltpu.SemaphoreType.DMA((inner,)),
        ],
        compiler_params=pltpu.CompilerParams(collective_id=collective_id, has_side_effects=True),
    )(by_first)
    return landed.swapaxes(0, 1).reshape(chunks.shape)


def per_device(inputs, short_filter, long_filter, grad_out):
    tap_count = short_filter.shape[0]
    filter_count, chan_count, shard_len = inputs.shape
    ctx_count = lax.axis_size("ctx")
    my_index = lax.axis_index("ctx")
    total_len = shard_len * ctx_count
    per_dev = filter_count * chan_count // ctx_count
    per_filter = chan_count // per_dev
    block_len = 128
    block_count = total_len // block_len

    send = jnp.concatenate(
        [
            grad_out.reshape(ctx_count, per_dev, shard_len),
            inputs.reshape(ctx_count, per_dev, shard_len),
            jnp.repeat(long_filter, per_filter, axis=0)[:, None, :],
        ],
        axis=1,
    )
    recv = relay(send, 8, 0)
    seqs = recv.transpose(1, 0, 2).reshape(2 * per_dev + 1, total_len)
    grad_seq = seqs[:per_dev]
    in_seq = seqs[per_dev : 2 * per_dev].astype(jnp.float32)
    filt_seq = seqs[2 * per_dev :]
    taps = short_filter.reshape(tap_count, ctx_count, per_dev)
    taps = lax.dynamic_index_in_dim(taps, my_index, axis=1, keepdims=False)

    hidden = sum(
        (taps[offset][:, None] * delayed(in_seq, offset, total_len) for offset in range(tap_count))
    )
    hidden = hidden.astype(jnp.bfloat16)

    groups = lax.axis_size("ch")
    short_rows, grad_in_out, grad_long_out = fused(
        grad_seq,
        jnp.concatenate([filt_seq, hidden], axis=0),
        in_seq,
        taps,
        groups,
        filter_count,
        block_len,
        1,
    )
    short_all = short_rows.reshape(ctx_count, shard_len)[:, : tap_count * per_dev]
    short_all = short_all.reshape(ctx_count, tap_count, per_dev)
    grad_short_out = short_all.transpose(1, 0, 2).reshape(tap_count, filter_count, chan_count)
    return (grad_in_out, grad_long_out, grad_short_out)


def solution(mesh):
    in_specs = (P(None, "ch", "ctx"), P(None, None, "ch"), P(None, "ctx"), P(None, "ch", "ctx"))
    out_specs = (P(None, "ch", "ctx"), P(None, "ctx"), P(None, None, "ch"))
    return jax.shard_map(
        per_device, mesh=mesh, in_specs=in_specs, out_specs=out_specs, check_vma=False
    )
```

```python
import jax
import jax.numpy as jnp
from jax import lax
from jax.experimental import pallas as pl
from jax.experimental.pallas import tpu as pltpu
from jax.sharding import PartitionSpec as P


def delayed(values, by, length):
    return jnp.pad(values, ((0, 0), (by, 0)))[:, :length]


def conv_kernel(grad_ref, rev_ref, hidden_ref, long_ref, hankel, toeplitz):
    chans, _, block_len = grad_ref.shape
    block_count = hidden_ref.shape[1]
    sources, lags, _ = rev_ref.shape

    def fill_hankel(lag, carry):
        col = pl.multiple_of(lag * block_len, block_len)
        for g in range(chans):
            hankel[g, :, pl.ds(col, block_len)] = grad_ref[g, pl.ds(lag, block_count), :].astype(
                hankel.dtype
            )
        return carry

    lax.fori_loop(0, lags, fill_hankel, 0)

    def fill_toeplitz(lag, carry):
        row = pl.multiple_of(lag * block_len, block_len)
        for s in range(sources):
            line = rev_ref[s, pl.ds(lag, 1), :]
            tiled = jnp.broadcast_to(line, (block_len, 2 * block_len))
            skewed = pltpu.roll(tiled, block_len + 1, 1, stride=1, stride_axis=0)
            toeplitz[s, pl.ds(row, block_len), :] = skewed[:, :block_len].astype(toeplitz.dtype)
        return carry

    lax.fori_loop(0, lags, fill_toeplitz, 0)

    for g in range(chans):
        hidden_ref[g] = jnp.dot(hankel[g], toeplitz[0], preferred_element_type=jnp.float32)
    acc = jnp.dot(hankel[0], toeplitz[1], preferred_element_type=jnp.float32)
    for g in range(1, chans):
        acc = acc + jnp.dot(hankel[g], toeplitz[1 + g], preferred_element_type=jnp.float32)
    long_ref[...] = acc


def correlate_all(grad_seq, sources, block_len):
    chans, total_len = grad_seq.shape
    count = sources.shape[0]
    block_count = total_len // block_len
    grad_pad = jnp.pad(
        grad_seq.astype(jnp.float32).reshape(chans, block_count, block_len),
        ((0, 0), (0, block_count), (0, 0)),
    )
    blocks = sources.reshape(count, block_count, block_len)
    padded = jnp.pad(blocks, ((0, 0), (1, 1), (0, 0)))
    pairs = jnp.concatenate([padded[:, :-1], padded[:, 1:]], axis=2)
    rev = pairs[..., ::-1].astype(jnp.float32)
    lags = block_count + 1
    hidden, long = pl.pallas_call(
        conv_kernel,
        out_shape=(
            jax.ShapeDtypeStruct((chans, block_count, block_len), jnp.float32),
            jax.ShapeDtypeStruct((block_count, block_len), jnp.float32),
        ),
        scratch_shapes=[
            pltpu.VMEM((chans, block_count, lags * block_len), jnp.bfloat16),
            pltpu.VMEM((count, lags * block_len, block_len), jnp.bfloat16),
        ],
        compiler_params=pltpu.CompilerParams(vmem_limit_bytes=48 * 1024 * 1024),
    )(grad_pad, rev)
    return hidden.reshape(chans, total_len), long.reshape(total_len)


def swap_kernel(send_ref, out_ref, landed, local_sem, send_sem, recv_sem):
    count = send_ref.shape[0]
    me = lax.axis_index("ctx")
    mine = lax.axis_index("ch")
    barrier = pltpu.get_barrier_semaphore()
    for step in range(1, count):
        peer = lax.rem(me + step, count)
        pl.semaphore_signal(
            barrier, 1, device_id=(peer, mine), device_id_type=pl.DeviceIdType.MESH
        )
    pl.semaphore_wait(barrier, count - 1)
    local = pltpu.make_async_copy(send_ref.at[me], landed.at[me], local_sem)
    local.start()
    copies = []
    for step in range(1, count):
        peer = lax.rem(me + step, count)
        copy = pltpu.make_async_remote_copy(
            src_ref=send_ref.at[peer],
            dst_ref=landed.at[me],
            send_sem=send_sem.at[peer],
            recv_sem=recv_sem.at[me],
            device_id=(peer, mine),
            device_id_type=pl.DeviceIdType.MESH,
        )
        copy.start()
        copies.append(copy)
    local.wait()
    for copy in copies:
        copy.wait_send()
    for step in range(1, count):
        source = lax.rem(me + step, count)
        pltpu.make_async_remote_copy(
            src_ref=send_ref.at[source],
            dst_ref=landed.at[source],
            send_sem=send_sem.at[source],
            recv_sem=recv_sem.at[source],
            device_id=(source, mine),
            device_id_type=pl.DeviceIdType.MESH,
        ).wait_recv()
    out_ref[...] = landed[...]


def swap(chunks, collective_id):
    return pl.pallas_call(
        swap_kernel,
        out_shape=jax.ShapeDtypeStruct(chunks.shape, chunks.dtype),
        in_specs=[pl.BlockSpec(memory_space=pltpu.VMEM)],
        out_specs=pl.BlockSpec(memory_space=pltpu.VMEM),
        scratch_shapes=[
            pltpu.VMEM(chunks.shape, chunks.dtype),
            pltpu.SemaphoreType.DMA,
            pltpu.SemaphoreType.DMA((chunks.shape[0],)),
            pltpu.SemaphoreType.DMA((chunks.shape[0],)),
        ],
        compiler_params=pltpu.CompilerParams(collective_id=collective_id, has_side_effects=True),
    )(chunks)


def gather_kernel(
    rows_ref, long_ref, rows_out, long_out, rows_in, long_in, local_sems,
    rows_send, rows_recv, long_send, long_recv,
):
    count = rows_ref.shape[0]
    groups = lax.axis_size("ch")
    me = lax.axis_index("ctx")
    mine = lax.axis_index("ch")
    mesh_id = pl.DeviceIdType.MESH
    peers = [(c, h) for c in range(count) for h in range(groups) if (c, h) != (0, 0)]
    barrier = pltpu.get_barrier_semaphore()
    for step_c, step_h in peers:
        peer, other = lax.rem(me + step_c, count), lax.rem(mine + step_h, groups)
        pl.semaphore_signal(barrier, 1, device_id=(peer, other), device_id_type=mesh_id)
    pl.semaphore_wait(barrier, len(peers))
    local_rows = pltpu.make_async_copy(rows_ref.at[me], rows_in.at[me], local_sems.at[0])
    local_long = pltpu.make_async_copy(long_ref.at[me], long_in.at[me, mine], local_sems.at[1])
    local_rows.start()
    local_long.start()
    copies = []
    for step in range(1, count):
        peer = lax.rem(me + step, count)
        copy = pltpu.make_async_remote_copy(
            src_ref=rows_ref.at[peer],
            dst_ref=rows_in.at[me],
            send_sem=rows_send.at[peer],
            recv_sem=rows_recv.at[me],
            device_id=(peer, mine),
            device_id_type=mesh_id,
        )
        copy.start()
        copies.append(copy)
    for step_c, step_h in peers:
        peer, other = lax.rem(me + step_c, count), lax.rem(mine + step_h, groups)
        copy = pltpu.make_async_remote_copy(
            src_ref=long_ref.at[peer],
            dst_ref=long_in.at[me, mine],
            send_sem=long_send.at[peer * groups + other],
            recv_sem=long_recv.at[me * groups + mine],
            device_id=(peer, other),
            device_id_type=mesh_id,
        )
        copy.start()
        copies.append(copy)
    local_rows.wait()
    local_long.wait()
    for copy in copies:
        copy.wait_send()
    for step in range(1, count):
        source = lax.rem(me + step, count)
        pltpu.make_async_remote_copy(
            src_ref=rows_ref.at[source],
            dst_ref=rows_in.at[source],
            send_sem=rows_send.at[source],
            recv_sem=rows_recv.at[source],
            device_id=(source, mine),
            device_id_type=mesh_id,
        ).wait_recv()
    for step_c, step_h in peers:
        source, other = lax.rem(me + step_c, count), lax.rem(mine + step_h, groups)
        pltpu.make_async_remote_copy(
            src_ref=long_ref.at[source],
            dst_ref=long_in.at[source, other],
            send_sem=long_send.at[source * groups + other],
            recv_sem=long_recv.at[source * groups + other],
            device_id=(source, other),
            device_id_type=mesh_id,
        ).wait_recv()
    rows_out[...] = rows_in[...]
    long_out[...] = long_in[...]


def gather(rows, longs, groups, collective_id):
    count = rows.shape[0]
    long_shape = (count, groups) + longs.shape[1:]
    vmem = pl.BlockSpec(memory_space=pltpu.VMEM)
    return pl.pallas_call(
        gather_kernel,
        out_shape=(
            jax.ShapeDtypeStruct(rows.shape, rows.dtype),
            jax.ShapeDtypeStruct(long_shape, longs.dtype),
        ),
        in_specs=[vmem, vmem],
        out_specs=(vmem, vmem),
        scratch_shapes=[
            pltpu.VMEM(rows.shape, rows.dtype),
            pltpu.VMEM(long_shape, longs.dtype),
            pltpu.SemaphoreType.DMA((2,)),
            pltpu.SemaphoreType.DMA((count,)),
            pltpu.SemaphoreType.DMA((count,)),
            pltpu.SemaphoreType.DMA((count * groups,)),
            pltpu.SemaphoreType.DMA((count * groups,)),
        ],
        compiler_params=pltpu.CompilerParams(collective_id=collective_id, has_side_effects=True),
    )(rows, longs)


def fused_kernel(
    grad_ref, rev_ref, in_ref, taps_ref, short_out, grad_in_out, long_out,
    hankel, toeplitz, grad_buf, rows_buf, ch_in, rows_in, local_sems,
    rows_send, rows_recv, ch_send, ch_recv,
):
    count = rows_buf.shape[0]
    chans, _, block_len = grad_ref.shape
    block_count = count
    sources, lags, _ = rev_ref.shape
    tap_count = taps_ref.shape[0]
    groups = lax.axis_size("ch")
    me = lax.axis_index("ctx")
    mine = lax.axis_index("ch")
    mesh_id = pl.DeviceIdType.MESH
    peers = [(c, 0) for c in range(1, count)] + [(0, h) for h in range(1, groups)]
    barrier = pltpu.get_barrier_semaphore()
    for step_c, step_h in peers:
        peer, other = lax.rem(me + step_c, count), lax.rem(mine + step_h, groups)
        pl.semaphore_signal(barrier, 1, device_id=(peer, other), device_id_type=mesh_id)

    def fill_hankel(lag, carry):
        col = pl.multiple_of(lag * block_len, block_len)
        for g in range(chans):
            hankel[g, :, pl.ds(col, block_len)] = grad_ref[g, pl.ds(lag, block_count), :].astype(
                hankel.dtype
            )
        return carry

    lax.fori_loop(0, lags, fill_hankel, 0)

    def fill_toeplitz(picked):
        def fill(lag, carry):
            row = pl.multiple_of(lag * block_len, block_len)
            for s in picked:
                line = rev_ref[s, pl.ds(lag, 1), :]
                tiled = jnp.broadcast_to(line, (block_len, 2 * block_len))
                skewed = pltpu.roll(tiled, block_len + 1, 1, stride=1, stride_axis=0)
                toeplitz[pl.ds(row, block_len), pl.ds(s * block_len, block_len)] = skewed[
                    :, :block_len
                ].astype(toeplitz.dtype)
            return carry

        lax.fori_loop(0, lags, fill, 0)

    fill_toeplitz(range(1, sources))

    window = hankel.shape[2]
    both = jnp.dot(
        hankel[...].reshape(chans * block_count, window),
        toeplitz[:, block_len:],
        preferred_element_type=jnp.float32,
    )
    acc = both[:block_count, :block_len]
    for g in range(1, chans):
        acc = acc + both[g * block_count : (g + 1) * block_count, g * block_len : (g + 1) * block_len]
    ch_in[mine] = acc
    pl.semaphore_wait(barrier, len(peers))
    partials = []
    for step in range(1, groups):
        other = lax.rem(mine + step, groups)
        copy = pltpu.make_async_remote_copy(
            src_ref=ch_in.at[mine],
            dst_ref=ch_in.at[mine],
            send_sem=ch_send.at[other],
            recv_sem=ch_recv.at[mine],
            device_id=(me, other),
            device_id_type=mesh_id,
        )
        copy.start()
        partials.append(copy)
    fill_toeplitz(range(1))

    lane = lax.broadcasted_iota(jnp.int32, (block_count, block_len), 1)
    short_row = jnp.zeros((block_count, block_len), jnp.float32)
    grad_buf[...] = jnp.zeros_like(grad_buf)
    hidden_all = jnp.dot(
        hankel[...].reshape(chans * block_count, window),
        toeplitz[:, :block_len],
        preferred_element_type=jnp.float32,
    )
    for g in range(chans):
        hidden_grad = hidden_all[g * block_count : (g + 1) * block_count]
        grad_buf[g, pl.ds(0, block_count), :] = hidden_grad
        following = grad_buf[g, pl.ds(1, block_count), :]
        total = taps_ref[0, g] * hidden_grad
        for offset in range(1, tap_count):
            here = pltpu.roll(hidden_grad, block_len - offset, 1)
            there = pltpu.roll(following, block_len - offset, 1)
            total = total + taps_ref[offset, g] * jnp.where(
                lane >= block_len - offset, there, here
            )
        rows_buf[:, g, :] = total.astype(jnp.bfloat16).astype(jnp.float32)
        current = in_ref[g, pl.ds(1, block_count), :]
        previous = in_ref[g, pl.ds(0, block_count), :]
        for offset in range(tap_count):
            if offset == 0:
                delayed_in = current
            else:
                delayed_in = jnp.where(
                    lane < offset,
                    pltpu.roll(previous, offset, 1),
                    pltpu.roll(current, offset, 1),
                )
            value = jnp.sum(hidden_grad * delayed_in)
            short_row = jnp.where(lane == offset * chans + g, value, short_row)
    rows_buf[:, chans, :] = short_row

    for copy in partials:
        copy.wait_send()
    for step in range(1, groups):
        source = lax.rem(mine + step, groups)
        pltpu.make_async_remote_copy(
            src_ref=ch_in.at[source],
            dst_ref=ch_in.at[source],
            send_sem=ch_send.at[source],
            recv_sem=ch_recv.at[source],
            device_id=(me, source),
            device_id_type=mesh_id,
        ).wait_recv()
    summed = ch_in[0]
    for h in range(1, groups):
        summed = summed + ch_in[h]
    rows_buf[:, chans + 1, :] = summed

    pairs = rows_in.shape[1]

    def landing(index):
        return rows_in.at[index // pairs, lax.rem(index, pairs)]

    local_rows = pltpu.make_async_copy(rows_buf.at[me], landing(me), local_sems.at[0])
    local_rows.start()
    copies = []
    for step in range(1, count):
        peer = lax.rem(me + step, count)
        copy = pltpu.make_async_remote_copy(
            src_ref=rows_buf.at[peer],
            dst_ref=landing(me),
            send_sem=rows_send.at[peer],
            recv_sem=rows_recv.at[me],
            device_id=(peer, mine),
            device_id_type=mesh_id,
        )
        copy.start()
        copies.append(copy)
    local_rows.wait()
    for copy in copies:
        copy.wait_send()
    for step in range(1, count):
        source = lax.rem(me + step, count)
        pltpu.make_async_remote_copy(
            src_ref=rows_buf.at[source],
            dst_ref=landing(source),
            send_sem=rows_send.at[source],
            recv_sem=rows_recv.at[source],
            device_id=(source, mine),
            device_id_type=mesh_id,
        ).wait_recv()
    for pair in range(pairs):
        short_out[:, pair, :] = rows_in[:, pair, chans, :]
        for g in range(chans):
            grad_in_out[:, pair * chans + g, :] = rows_in[:, pair, g, :].astype(grad_in_out.dtype)
    total = rows_in[:, 0, chans + 1, :]
    for pair in range(1, pairs):
        total = total + rows_in[:, pair, chans + 1, :]
    long_out[...] = total


def fused(grad_seq, sources, in_seq, taps, groups, filter_count, block_len, collective_id):
    chans, total_len = grad_seq.shape
    count = sources.shape[0]
    block_count = total_len // block_len
    grad_pad = jnp.pad(
        grad_seq.astype(jnp.float32).reshape(chans, block_count, block_len),
        ((0, 0), (0, block_count), (0, 0)),
    )
    blocks = sources.reshape(count, block_count, block_len)
    padded = jnp.pad(blocks, ((0, 0), (1, 1), (0, 0)))
    pairs = jnp.concatenate([padded[:, :-1], padded[:, 1:]], axis=2)
    rev = pairs[..., ::-1].astype(jnp.float32)
    in_pad = jnp.pad(in_seq.reshape(chans, block_count, block_len), ((0, 0), (1, 0), (0, 0)))
    lags = block_count + 1
    rows_shape = (block_count, chans + 2, block_len)
    pairs = block_count // filter_count
    landed_shape = (filter_count, pairs, chans + 2, block_len)
    vmem = pl.BlockSpec(memory_space=pltpu.VMEM)
    return pl.pallas_call(
        fused_kernel,
        out_shape=(
            jax.ShapeDtypeStruct((filter_count, pairs, block_len), jnp.float32),
            jax.ShapeDtypeStruct((filter_count, pairs * chans, block_len), jnp.bfloat16),
            jax.ShapeDtypeStruct((filter_count, block_len), jnp.float32),
        ),
        in_specs=[vmem, vmem, vmem, pl.BlockSpec(memory_space=pltpu.SMEM)],
        out_specs=(vmem, vmem, vmem),
        scratch_shapes=[
            pltpu.VMEM((chans, block_count, lags * block_len), jnp.bfloat16),
            pltpu.VMEM((lags * block_len, count * block_len), jnp.bfloat16),
            pltpu.VMEM((chans, block_count + 8, block_len), jnp.float32),
            pltpu.VMEM(rows_shape, jnp.float32),
            pltpu.VMEM((groups, block_count, block_len), jnp.float32),
            pltpu.VMEM(landed_shape, jnp.float32),
            pltpu.SemaphoreType.DMA((1,)),
            pltpu.SemaphoreType.DMA((block_count,)),
            pltpu.SemaphoreType.DMA((block_count,)),
            pltpu.SemaphoreType.DMA((groups,)),
            pltpu.SemaphoreType.DMA((groups,)),
        ],
        compiler_params=pltpu.CompilerParams(
            collective_id=collective_id,
            has_side_effects=True,
            vmem_limit_bytes=48 * 1024 * 1024,
        ),
    )(grad_pad, rev, in_pad, taps)


def relay_kernel(send_ref, out_ref, middle, landed, local_sems, first_send, first_recv, second_send, second_recv):
    firsts, seconds = send_ref.shape[0], send_ref.shape[1]
    me = lax.axis_index("ctx")
    mine = lax.axis_index("ch")
    first, second = me // seconds, lax.rem(me, seconds)
    mesh_id = pl.DeviceIdType.MESH

    def place(f, s):
        return f * seconds + s

    barrier = pltpu.get_barrier_semaphore()
    for step in range(1, firsts):
        peer = place(lax.rem(first + step, firsts), second)
        pl.semaphore_signal(barrier, 1, device_id=(peer, mine), device_id_type=mesh_id)
    for step in range(1, seconds):
        peer = place(first, lax.rem(second + step, seconds))
        pl.semaphore_signal(barrier, 1, device_id=(peer, mine), device_id_type=mesh_id)
    pl.semaphore_wait(barrier, firsts - 1 + seconds - 1)
    local = pltpu.make_async_copy(send_ref.at[first], middle.at[:, first], local_sems.at[0])
    local.start()
    copies = []
    for step in range(1, firsts):
        target = lax.rem(first + step, firsts)
        copy = pltpu.make_async_remote_copy(
            src_ref=send_ref.at[target],
            dst_ref=middle.at[:, first],
            send_sem=first_send.at[target],
            recv_sem=first_recv.at[first],
            device_id=(place(target, second), mine),
            device_id_type=mesh_id,
        )
        copy.start()
        copies.append(copy)
    local.wait()
    for copy in copies:
        copy.wait_send()
    for step in range(1, firsts):
        source = lax.rem(first + step, firsts)
        pltpu.make_async_remote_copy(
            src_ref=send_ref.at[source],
            dst_ref=middle.at[:, source],
            send_sem=first_send.at[source],
            recv_sem=first_recv.at[source],
            device_id=(place(source, second), mine),
            device_id_type=mesh_id,
        ).wait_recv()
    local = pltpu.make_async_copy(middle.at[second], landed.at[second], local_sems.at[1])
    local.start()
    copies = []
    for step in range(1, seconds):
        target = lax.rem(second + step, seconds)
        copy = pltpu.make_async_remote_copy(
            src_ref=middle.at[target],
            dst_ref=landed.at[second],
            send_sem=second_send.at[target],
            recv_sem=second_recv.at[second],
            device_id=(place(first, target), mine),
            device_id_type=mesh_id,
        )
        copy.start()
        copies.append(copy)
    local.wait()
    for copy in copies:
        copy.wait_send()
    for step in range(1, seconds):
        source = lax.rem(second + step, seconds)
        pltpu.make_async_remote_copy(
            src_ref=middle.at[source],
            dst_ref=landed.at[source],
            send_sem=second_send.at[source],
            recv_sem=second_recv.at[source],
            device_id=(place(first, source), mine),
            device_id_type=mesh_id,
        ).wait_recv()
    out_ref[...] = landed[...]


def relay(chunks, inner, collective_id):
    count = chunks.shape[0]
    outer = count // inner
    rest = chunks.shape[1:]
    by_first = chunks.reshape((outer, inner) + rest)
    first_shape = (outer, inner) + rest
    second_shape = (inner, outer) + rest
    landed = pl.pallas_call(
        relay_kernel,
        out_shape=jax.ShapeDtypeStruct(second_shape, chunks.dtype),
        in_specs=[pl.BlockSpec(memory_space=pltpu.VMEM)],
        out_specs=pl.BlockSpec(memory_space=pltpu.VMEM),
        scratch_shapes=[
            pltpu.VMEM(second_shape, chunks.dtype),
            pltpu.VMEM(second_shape, chunks.dtype),
            pltpu.SemaphoreType.DMA((2,)),
            pltpu.SemaphoreType.DMA((outer,)),
            pltpu.SemaphoreType.DMA((outer,)),
            pltpu.SemaphoreType.DMA((inner,)),
            pltpu.SemaphoreType.DMA((inner,)),
        ],
        compiler_params=pltpu.CompilerParams(collective_id=collective_id, has_side_effects=True),
    )(by_first)
    return landed.swapaxes(0, 1).reshape(chunks.shape)


def per_device(inputs, short_filter, long_filter, grad_out):
    tap_count = short_filter.shape[0]
    filter_count, chan_count, shard_len = inputs.shape
    ctx_count = lax.axis_size("ctx")
    my_index = lax.axis_index("ctx")
    total_len = shard_len * ctx_count
    per_dev = filter_count * chan_count // ctx_count
    per_filter = chan_count // per_dev
    block_len = 128
    block_count = total_len // block_len

    send = jnp.concatenate(
        [
            grad_out.reshape(ctx_count, per_dev, shard_len),
            inputs.reshape(ctx_count, per_dev, shard_len),
            jnp.repeat(long_filter, per_filter, axis=0)[:, None, :],
        ],
        axis=1,
    )
    recv = relay(send, 8, 0)
    seqs = recv.transpose(1, 0, 2).reshape(2 * per_dev + 1, total_len)
    grad_seq = seqs[:per_dev]
    in_seq = seqs[per_dev : 2 * per_dev].astype(jnp.float32)
    filt_seq = seqs[2 * per_dev :]
    taps = short_filter.reshape(tap_count, ctx_count, per_dev)
    taps = lax.dynamic_index_in_dim(taps, my_index, axis=1, keepdims=False)

    hidden = sum(
        (taps[offset][:, None] * delayed(in_seq, offset, total_len) for offset in range(tap_count))
    )
    hidden = hidden.astype(jnp.bfloat16)

    groups = lax.axis_size("ch")
    short_rows, grad_in_out, grad_long_out = fused(
        grad_seq,
        jnp.concatenate([filt_seq, hidden], axis=0),
        in_seq,
        taps,
        groups,
        filter_count,
        block_len,
        1,
    )
    short_all = short_rows.reshape(ctx_count, shard_len)[:, : tap_count * per_dev]
    short_all = short_all.reshape(ctx_count, tap_count, per_dev)
    grad_short_out = short_all.transpose(1, 0, 2).reshape(tap_count, filter_count, chan_count)
    return (grad_in_out, grad_long_out, grad_short_out)


def solution(mesh):
    in_specs = (P(None, "ch", "ctx"), P(None, None, "ch"), P(None, "ctx"), P(None, "ch", "ctx"))
    out_specs = (P(None, "ch", "ctx"), P(None, "ctx"), P(None, None, "ch"))
    return jax.shard_map(
        per_device, mesh=mesh, in_specs=in_specs, out_specs=out_specs, check_vma=False
    )
```

```python
import jax
import jax.numpy as jnp
from jax import lax
from jax.experimental import pallas as pl
from jax.experimental.pallas import tpu as pltpu
from jax.sharding import PartitionSpec as P


def delayed(values, by, length):
    return jnp.pad(values, ((0, 0), (by, 0)))[:, :length]


def conv_kernel(grad_ref, rev_ref, hidden_ref, long_ref, hankel, toeplitz):
    chans, _, block_len = grad_ref.shape
    block_count = hidden_ref.shape[1]
    sources, lags, _ = rev_ref.shape

    def fill_hankel(lag, carry):
        col = pl.multiple_of(lag * block_len, block_len)
        for g in range(chans):
            hankel[g, :, pl.ds(col, block_len)] = grad_ref[g, pl.ds(lag, block_count), :].astype(
                hankel.dtype
            )
        return carry

    lax.fori_loop(0, lags, fill_hankel, 0)

    def fill_toeplitz(lag, carry):
        row = pl.multiple_of(lag * block_len, block_len)
        for s in range(sources):
            line = rev_ref[s, pl.ds(lag, 1), :]
            tiled = jnp.broadcast_to(line, (block_len, 2 * block_len))
            skewed = pltpu.roll(tiled, block_len + 1, 1, stride=1, stride_axis=0)
            toeplitz[s, pl.ds(row, block_len), :] = skewed[:, :block_len].astype(toeplitz.dtype)
        return carry

    lax.fori_loop(0, lags, fill_toeplitz, 0)

    for g in range(chans):
        hidden_ref[g] = jnp.dot(hankel[g], toeplitz[0], preferred_element_type=jnp.float32)
    acc = jnp.dot(hankel[0], toeplitz[1], preferred_element_type=jnp.float32)
    for g in range(1, chans):
        acc = acc + jnp.dot(hankel[g], toeplitz[1 + g], preferred_element_type=jnp.float32)
    long_ref[...] = acc


def correlate_all(grad_seq, sources, block_len):
    chans, total_len = grad_seq.shape
    count = sources.shape[0]
    block_count = total_len // block_len
    grad_pad = jnp.pad(
        grad_seq.astype(jnp.float32).reshape(chans, block_count, block_len),
        ((0, 0), (0, block_count), (0, 0)),
    )
    blocks = sources.reshape(count, block_count, block_len)
    padded = jnp.pad(blocks, ((0, 0), (1, 1), (0, 0)))
    pairs = jnp.concatenate([padded[:, :-1], padded[:, 1:]], axis=2)
    rev = pairs[..., ::-1].astype(jnp.float32)
    lags = block_count + 1
    hidden, long = pl.pallas_call(
        conv_kernel,
        out_shape=(
            jax.ShapeDtypeStruct((chans, block_count, block_len), jnp.float32),
            jax.ShapeDtypeStruct((block_count, block_len), jnp.float32),
        ),
        scratch_shapes=[
            pltpu.VMEM((chans, block_count, lags * block_len), jnp.bfloat16),
            pltpu.VMEM((count, lags * block_len, block_len), jnp.bfloat16),
        ],
        compiler_params=pltpu.CompilerParams(vmem_limit_bytes=48 * 1024 * 1024),
    )(grad_pad, rev)
    return hidden.reshape(chans, total_len), long.reshape(total_len)


def swap_kernel(send_ref, out_ref, landed, local_sem, send_sem, recv_sem):
    count = send_ref.shape[0]
    me = lax.axis_index("ctx")
    mine = lax.axis_index("ch")
    barrier = pltpu.get_barrier_semaphore()
    for step in range(1, count):
        peer = lax.rem(me + step, count)
        pl.semaphore_signal(
            barrier, 1, device_id=(peer, mine), device_id_type=pl.DeviceIdType.MESH
        )
    pl.semaphore_wait(barrier, count - 1)
    local = pltpu.make_async_copy(send_ref.at[me], landed.at[me], local_sem)
    local.start()
    copies = []
    for step in range(1, count):
        peer = lax.rem(me + step, count)
        copy = pltpu.make_async_remote_copy(
            src_ref=send_ref.at[peer],
            dst_ref=landed.at[me],
            send_sem=send_sem.at[peer],
            recv_sem=recv_sem.at[me],
            device_id=(peer, mine),
            device_id_type=pl.DeviceIdType.MESH,
        )
        copy.start()
        copies.append(copy)
    local.wait()
    for copy in copies:
        copy.wait_send()
    for step in range(1, count):
        source = lax.rem(me + step, count)
        pltpu.make_async_remote_copy(
            src_ref=send_ref.at[source],
            dst_ref=landed.at[source],
            send_sem=send_sem.at[source],
            recv_sem=recv_sem.at[source],
            device_id=(source, mine),
            device_id_type=pl.DeviceIdType.MESH,
        ).wait_recv()
    out_ref[...] = landed[...]


def swap(chunks, collective_id):
    return pl.pallas_call(
        swap_kernel,
        out_shape=jax.ShapeDtypeStruct(chunks.shape, chunks.dtype),
        in_specs=[pl.BlockSpec(memory_space=pltpu.VMEM)],
        out_specs=pl.BlockSpec(memory_space=pltpu.VMEM),
        scratch_shapes=[
            pltpu.VMEM(chunks.shape, chunks.dtype),
            pltpu.SemaphoreType.DMA,
            pltpu.SemaphoreType.DMA((chunks.shape[0],)),
            pltpu.SemaphoreType.DMA((chunks.shape[0],)),
        ],
        compiler_params=pltpu.CompilerParams(collective_id=collective_id, has_side_effects=True),
    )(chunks)


def gather_kernel(
    rows_ref, long_ref, rows_out, long_out, rows_in, long_in, local_sems,
    rows_send, rows_recv, long_send, long_recv,
):
    count = rows_ref.shape[0]
    groups = lax.axis_size("ch")
    me = lax.axis_index("ctx")
    mine = lax.axis_index("ch")
    mesh_id = pl.DeviceIdType.MESH
    peers = [(c, h) for c in range(count) for h in range(groups) if (c, h) != (0, 0)]
    barrier = pltpu.get_barrier_semaphore()
    for step_c, step_h in peers:
        peer, other = lax.rem(me + step_c, count), lax.rem(mine + step_h, groups)
        pl.semaphore_signal(barrier, 1, device_id=(peer, other), device_id_type=mesh_id)
    pl.semaphore_wait(barrier, len(peers))
    local_rows = pltpu.make_async_copy(rows_ref.at[me], rows_in.at[me], local_sems.at[0])
    local_long = pltpu.make_async_copy(long_ref.at[me], long_in.at[me, mine], local_sems.at[1])
    local_rows.start()
    local_long.start()
    copies = []
    for step in range(1, count):
        peer = lax.rem(me + step, count)
        copy = pltpu.make_async_remote_copy(
            src_ref=rows_ref.at[peer],
            dst_ref=rows_in.at[me],
            send_sem=rows_send.at[peer],
            recv_sem=rows_recv.at[me],
            device_id=(peer, mine),
            device_id_type=mesh_id,
        )
        copy.start()
        copies.append(copy)
    for step_c, step_h in peers:
        peer, other = lax.rem(me + step_c, count), lax.rem(mine + step_h, groups)
        copy = pltpu.make_async_remote_copy(
            src_ref=long_ref.at[peer],
            dst_ref=long_in.at[me, mine],
            send_sem=long_send.at[peer * groups + other],
            recv_sem=long_recv.at[me * groups + mine],
            device_id=(peer, other),
            device_id_type=mesh_id,
        )
        copy.start()
        copies.append(copy)
    local_rows.wait()
    local_long.wait()
    for copy in copies:
        copy.wait_send()
    for step in range(1, count):
        source = lax.rem(me + step, count)
        pltpu.make_async_remote_copy(
            src_ref=rows_ref.at[source],
            dst_ref=rows_in.at[source],
            send_sem=rows_send.at[source],
            recv_sem=rows_recv.at[source],
            device_id=(source, mine),
            device_id_type=mesh_id,
        ).wait_recv()
    for step_c, step_h in peers:
        source, other = lax.rem(me + step_c, count), lax.rem(mine + step_h, groups)
        pltpu.make_async_remote_copy(
            src_ref=long_ref.at[source],
            dst_ref=long_in.at[source, other],
            send_sem=long_send.at[source * groups + other],
            recv_sem=long_recv.at[source * groups + other],
            device_id=(source, other),
            device_id_type=mesh_id,
        ).wait_recv()
    rows_out[...] = rows_in[...]
    long_out[...] = long_in[...]


def gather(rows, longs, groups, collective_id):
    count = rows.shape[0]
    long_shape = (count, groups) + longs.shape[1:]
    vmem = pl.BlockSpec(memory_space=pltpu.VMEM)
    return pl.pallas_call(
        gather_kernel,
        out_shape=(
            jax.ShapeDtypeStruct(rows.shape, rows.dtype),
            jax.ShapeDtypeStruct(long_shape, longs.dtype),
        ),
        in_specs=[vmem, vmem],
        out_specs=(vmem, vmem),
        scratch_shapes=[
            pltpu.VMEM(rows.shape, rows.dtype),
            pltpu.VMEM(long_shape, longs.dtype),
            pltpu.SemaphoreType.DMA((2,)),
            pltpu.SemaphoreType.DMA((count,)),
            pltpu.SemaphoreType.DMA((count,)),
            pltpu.SemaphoreType.DMA((count * groups,)),
            pltpu.SemaphoreType.DMA((count * groups,)),
        ],
        compiler_params=pltpu.CompilerParams(collective_id=collective_id, has_side_effects=True),
    )(rows, longs)


def fused_kernel(
    grad_ref, rev_ref, in_ref, taps_ref, short_out, grad_in_out, long_out,
    hankel, toeplitz, grad_buf, rows_buf, ch_in, rows_in, local_sems,
    rows_send, rows_recv, ch_send, ch_recv,
):
    count = rows_buf.shape[0]
    chans, _, block_len = grad_ref.shape
    block_count = count
    sources, lags, _ = rev_ref.shape
    tap_count = taps_ref.shape[0]
    groups = lax.axis_size("ch")
    me = lax.axis_index("ctx")
    mine = lax.axis_index("ch")
    mesh_id = pl.DeviceIdType.MESH
    peers = [(c, 0) for c in range(1, count)] + [(0, h) for h in range(1, groups)]
    barrier = pltpu.get_barrier_semaphore()
    for step_c, step_h in peers:
        peer, other = lax.rem(me + step_c, count), lax.rem(mine + step_h, groups)
        pl.semaphore_signal(barrier, 1, device_id=(peer, other), device_id_type=mesh_id)

    def fill_hankel(lag, carry):
        col = pl.multiple_of(lag * block_len, block_len)
        for g in range(chans):
            hankel[g, :, pl.ds(col, block_len)] = grad_ref[g, pl.ds(lag, block_count), :].astype(
                hankel.dtype
            )
        return carry

    lax.fori_loop(0, lags, fill_hankel, 0)

    def fill_toeplitz(picked):
        def fill(lag, carry):
            row = pl.multiple_of(lag * block_len, block_len)
            for s in picked:
                line = rev_ref[s, pl.ds(lag, 1), :]
                tiled = jnp.broadcast_to(line, (block_len, 2 * block_len))
                skewed = pltpu.roll(tiled, block_len + 1, 1, stride=1, stride_axis=0)
                toeplitz[s, pl.ds(row, block_len), :] = skewed[:, :block_len].astype(
                    toeplitz.dtype
                )
            return carry

        lax.fori_loop(0, lags, fill, 0)

    fill_toeplitz(range(1, sources))

    acc = jnp.dot(hankel[0], toeplitz[1], preferred_element_type=jnp.float32)
    for g in range(1, chans):
        acc = acc + jnp.dot(hankel[g], toeplitz[1 + g], preferred_element_type=jnp.float32)
    ch_in[mine] = acc
    pl.semaphore_wait(barrier, len(peers))
    partials = []
    for step in range(1, groups):
        other = lax.rem(mine + step, groups)
        copy = pltpu.make_async_remote_copy(
            src_ref=ch_in.at[mine],
            dst_ref=ch_in.at[mine],
            send_sem=ch_send.at[other],
            recv_sem=ch_recv.at[mine],
            device_id=(me, other),
            device_id_type=mesh_id,
        )
        copy.start()
        partials.append(copy)
    fill_toeplitz(range(1))

    lane = lax.broadcasted_iota(jnp.int32, (block_count, block_len), 1)
    short_row = jnp.zeros((block_count, block_len), jnp.float32)
    grad_buf[...] = jnp.zeros_like(grad_buf)
    window = hankel.shape[2]
    hidden_all = jnp.dot(
        hankel[...].reshape(chans * block_count, window),
        toeplitz[0],
        preferred_element_type=jnp.float32,
    )
    for g in range(chans):
        hidden_grad = hidden_all[g * block_count : (g + 1) * block_count]
        grad_buf[g, pl.ds(0, block_count), :] = hidden_grad
        following = grad_buf[g, pl.ds(1, block_count), :]
        total = taps_ref[0, g] * hidden_grad
        for offset in range(1, tap_count):
            here = pltpu.roll(hidden_grad, block_len - offset, 1)
            there = pltpu.roll(following, block_len - offset, 1)
            total = total + taps_ref[offset, g] * jnp.where(
                lane >= block_len - offset, there, here
            )
        rows_buf[:, g, :] = total.astype(jnp.bfloat16).astype(jnp.float32)
        current = in_ref[g, pl.ds(1, block_count), :]
        previous = in_ref[g, pl.ds(0, block_count), :]
        for offset in range(tap_count):
            if offset == 0:
                delayed_in = current
            else:
                delayed_in = jnp.where(
                    lane < offset,
                    pltpu.roll(previous, offset, 1),
                    pltpu.roll(current, offset, 1),
                )
            value = jnp.sum(hidden_grad * delayed_in)
            short_row = jnp.where(lane == offset * chans + g, value, short_row)
    rows_buf[:, chans, :] = short_row

    for copy in partials:
        copy.wait_send()
    for step in range(1, groups):
        source = lax.rem(mine + step, groups)
        pltpu.make_async_remote_copy(
            src_ref=ch_in.at[source],
            dst_ref=ch_in.at[source],
            send_sem=ch_send.at[source],
            recv_sem=ch_recv.at[source],
            device_id=(me, source),
            device_id_type=mesh_id,
        ).wait_recv()
    summed = ch_in[0]
    for h in range(1, groups):
        summed = summed + ch_in[h]
    rows_buf[:, chans + 1, :] = summed

    pairs = rows_in.shape[1]

    def landing(index):
        return rows_in.at[index // pairs, lax.rem(index, pairs)]

    local_rows = pltpu.make_async_copy(rows_buf.at[me], landing(me), local_sems.at[0])
    local_rows.start()
    copies = []
    for step in range(1, count):
        peer = lax.rem(me + step, count)
        copy = pltpu.make_async_remote_copy(
            src_ref=rows_buf.at[peer],
            dst_ref=landing(me),
            send_sem=rows_send.at[peer],
            recv_sem=rows_recv.at[me],
            device_id=(peer, mine),
            device_id_type=mesh_id,
        )
        copy.start()
        copies.append(copy)
    local_rows.wait()
    for copy in copies:
        copy.wait_send()
    for step in range(1, count):
        source = lax.rem(me + step, count)
        pltpu.make_async_remote_copy(
            src_ref=rows_buf.at[source],
            dst_ref=landing(source),
            send_sem=rows_send.at[source],
            recv_sem=rows_recv.at[source],
            device_id=(source, mine),
            device_id_type=mesh_id,
        ).wait_recv()
    for pair in range(pairs):
        short_out[:, pair, :] = rows_in[:, pair, chans, :]
        for g in range(chans):
            grad_in_out[:, pair * chans + g, :] = rows_in[:, pair, g, :].astype(grad_in_out.dtype)
    total = rows_in[:, 0, chans + 1, :]
    for pair in range(1, pairs):
        total = total + rows_in[:, pair, chans + 1, :]
    long_out[...] = total


def fused(grad_seq, sources, in_seq, taps, groups, filter_count, block_len, collective_id):
    chans, total_len = grad_seq.shape
    count = sources.shape[0]
    block_count = total_len // block_len
    grad_pad = jnp.pad(
        grad_seq.astype(jnp.float32).reshape(chans, block_count, block_len),
        ((0, 0), (0, block_count), (0, 0)),
    )
    blocks = sources.reshape(count, block_count, block_len)
    padded = jnp.pad(blocks, ((0, 0), (1, 1), (0, 0)))
    pairs = jnp.concatenate([padded[:, :-1], padded[:, 1:]], axis=2)
    rev = pairs[..., ::-1].astype(jnp.float32)
    in_pad = jnp.pad(in_seq.reshape(chans, block_count, block_len), ((0, 0), (1, 0), (0, 0)))
    lags = block_count + 1
    rows_shape = (block_count, chans + 2, block_len)
    pairs = block_count // filter_count
    landed_shape = (filter_count, pairs, chans + 2, block_len)
    vmem = pl.BlockSpec(memory_space=pltpu.VMEM)
    return pl.pallas_call(
        fused_kernel,
        out_shape=(
            jax.ShapeDtypeStruct((filter_count, pairs, block_len), jnp.float32),
            jax.ShapeDtypeStruct((filter_count, pairs * chans, block_len), jnp.bfloat16),
            jax.ShapeDtypeStruct((filter_count, block_len), jnp.float32),
        ),
        in_specs=[vmem, vmem, vmem, pl.BlockSpec(memory_space=pltpu.SMEM)],
        out_specs=(vmem, vmem, vmem),
        scratch_shapes=[
            pltpu.VMEM((chans, block_count, lags * block_len), jnp.bfloat16),
            pltpu.VMEM((count, lags * block_len, block_len), jnp.bfloat16),
            pltpu.VMEM((chans, block_count + 8, block_len), jnp.float32),
            pltpu.VMEM(rows_shape, jnp.float32),
            pltpu.VMEM((groups, block_count, block_len), jnp.float32),
            pltpu.VMEM(landed_shape, jnp.float32),
            pltpu.SemaphoreType.DMA((1,)),
            pltpu.SemaphoreType.DMA((block_count,)),
            pltpu.SemaphoreType.DMA((block_count,)),
            pltpu.SemaphoreType.DMA((groups,)),
            pltpu.SemaphoreType.DMA((groups,)),
        ],
        compiler_params=pltpu.CompilerParams(
            collective_id=collective_id,
            has_side_effects=True,
            vmem_limit_bytes=48 * 1024 * 1024,
        ),
    )(grad_pad, rev, in_pad, taps)


def relay_kernel(send_ref, out_ref, middle, landed, local_sems, first_send, first_recv, second_send, second_recv):
    firsts, seconds = send_ref.shape[0], send_ref.shape[1]
    me = lax.axis_index("ctx")
    mine = lax.axis_index("ch")
    first, second = me // seconds, lax.rem(me, seconds)
    mesh_id = pl.DeviceIdType.MESH

    def place(f, s):
        return f * seconds + s

    barrier = pltpu.get_barrier_semaphore()
    for step in range(1, firsts):
        peer = place(lax.rem(first + step, firsts), second)
        pl.semaphore_signal(barrier, 1, device_id=(peer, mine), device_id_type=mesh_id)
    for step in range(1, seconds):
        peer = place(first, lax.rem(second + step, seconds))
        pl.semaphore_signal(barrier, 1, device_id=(peer, mine), device_id_type=mesh_id)
    pl.semaphore_wait(barrier, firsts - 1 + seconds - 1)
    local = pltpu.make_async_copy(send_ref.at[first], middle.at[:, first], local_sems.at[0])
    local.start()
    copies = []
    for step in range(1, firsts):
        target = lax.rem(first + step, firsts)
        copy = pltpu.make_async_remote_copy(
            src_ref=send_ref.at[target],
            dst_ref=middle.at[:, first],
            send_sem=first_send.at[target],
            recv_sem=first_recv.at[first],
            device_id=(place(target, second), mine),
            device_id_type=mesh_id,
        )
        copy.start()
        copies.append(copy)
    local.wait()
    for copy in copies:
        copy.wait_send()
    for step in range(1, firsts):
        source = lax.rem(first + step, firsts)
        pltpu.make_async_remote_copy(
            src_ref=send_ref.at[source],
            dst_ref=middle.at[:, source],
            send_sem=first_send.at[source],
            recv_sem=first_recv.at[source],
            device_id=(place(source, second), mine),
            device_id_type=mesh_id,
        ).wait_recv()
    local = pltpu.make_async_copy(middle.at[second], landed.at[second], local_sems.at[1])
    local.start()
    copies = []
    for step in range(1, seconds):
        target = lax.rem(second + step, seconds)
        copy = pltpu.make_async_remote_copy(
            src_ref=middle.at[target],
            dst_ref=landed.at[second],
            send_sem=second_send.at[target],
            recv_sem=second_recv.at[second],
            device_id=(place(first, target), mine),
            device_id_type=mesh_id,
        )
        copy.start()
        copies.append(copy)
    local.wait()
    for copy in copies:
        copy.wait_send()
    for step in range(1, seconds):
        source = lax.rem(second + step, seconds)
        pltpu.make_async_remote_copy(
            src_ref=middle.at[source],
            dst_ref=landed.at[source],
            send_sem=second_send.at[source],
            recv_sem=second_recv.at[source],
            device_id=(place(first, source), mine),
            device_id_type=mesh_id,
        ).wait_recv()
    for r in range(send_ref.shape[2]):
        for f in range(firsts):
            out_ref[r, pl.ds(f * seconds, seconds), :] = landed[:, f, r, :]


def relay(chunks, inner, collective_id):
    count = chunks.shape[0]
    outer = count // inner
    rest = chunks.shape[1:]
    by_first = chunks.reshape((outer, inner) + rest)
    first_shape = (outer, inner) + rest
    second_shape = (inner, outer) + rest
    landed = pl.pallas_call(
        relay_kernel,
        out_shape=jax.ShapeDtypeStruct((rest[0], count) + rest[1:], chunks.dtype),
        in_specs=[pl.BlockSpec(memory_space=pltpu.VMEM)],
        out_specs=pl.BlockSpec(memory_space=pltpu.VMEM),
        scratch_shapes=[
            pltpu.VMEM(second_shape, chunks.dtype),
            pltpu.VMEM(second_shape, chunks.dtype),
            pltpu.SemaphoreType.DMA((2,)),
            pltpu.SemaphoreType.DMA((outer,)),
            pltpu.SemaphoreType.DMA((outer,)),
            pltpu.SemaphoreType.DMA((inner,)),
            pltpu.SemaphoreType.DMA((inner,)),
        ],
        compiler_params=pltpu.CompilerParams(collective_id=collective_id, has_side_effects=True),
    )(by_first)
    return landed


def per_device(inputs, short_filter, long_filter, grad_out):
    tap_count = short_filter.shape[0]
    filter_count, chan_count, shard_len = inputs.shape
    ctx_count = lax.axis_size("ctx")
    my_index = lax.axis_index("ctx")
    total_len = shard_len * ctx_count
    per_dev = filter_count * chan_count // ctx_count
    per_filter = chan_count // per_dev
    block_len = 128
    block_count = total_len // block_len

    send = jnp.concatenate(
        [
            grad_out.reshape(ctx_count, per_dev, shard_len),
            inputs.reshape(ctx_count, per_dev, shard_len),
            jnp.repeat(long_filter, per_filter, axis=0)[:, None, :],
        ],
        axis=1,
    )
    recv = relay(send.astype(jnp.float32), 8, 0)
    seqs = recv.reshape(2 * per_dev + 1, total_len)
    grad_seq = seqs[:per_dev]
    in_seq = seqs[per_dev : 2 * per_dev]
    filt_seq = seqs[2 * per_dev :].astype(jnp.bfloat16)
    taps = short_filter.reshape(tap_count, ctx_count, per_dev)
    taps = lax.dynamic_index_in_dim(taps, my_index, axis=1, keepdims=False)

    hidden = sum(
        (taps[offset][:, None] * delayed(in_seq, offset, total_len) for offset in range(tap_count))
    )
    hidden = hidden.astype(jnp.bfloat16)

    groups = lax.axis_size("ch")
    short_rows, grad_in_out, grad_long_out = fused(
        grad_seq,
        jnp.concatenate([filt_seq, hidden], axis=0),
        in_seq,
        taps,
        groups,
        filter_count,
        block_len,
        1,
    )
    short_all = short_rows.reshape(ctx_count, shard_len)[:, : tap_count * per_dev]
    short_all = short_all.reshape(ctx_count, tap_count, per_dev)
    grad_short_out = short_all.transpose(1, 0, 2).reshape(tap_count, filter_count, chan_count)
    return (grad_in_out, grad_long_out, grad_short_out)


def solution(mesh):
    in_specs = (P(None, "ch", "ctx"), P(None, None, "ch"), P(None, "ctx"), P(None, "ch", "ctx"))
    out_specs = (P(None, "ch", "ctx"), P(None, "ctx"), P(None, None, "ch"))
    return jax.shard_map(
        per_device, mesh=mesh, in_specs=in_specs, out_specs=out_specs, check_vma=False
    )
```

```python
import jax
import jax.numpy as jnp
from jax import lax
from jax.experimental import pallas as pl
from jax.experimental.pallas import tpu as pltpu
from jax.sharding import PartitionSpec as P


def delayed(values, by, length):
    return jnp.pad(values, ((0, 0), (by, 0)))[:, :length]


def conv_kernel(grad_ref, rev_ref, hidden_ref, long_ref, hankel, toeplitz):
    chans, _, block_len = grad_ref.shape
    block_count = hidden_ref.shape[1]
    sources, lags, _ = rev_ref.shape

    def fill_hankel(lag, carry):
        col = pl.multiple_of(lag * block_len, block_len)
        for g in range(chans):
            hankel[g, :, pl.ds(col, block_len)] = grad_ref[g, pl.ds(lag, block_count), :].astype(
                hankel.dtype
            )
        return carry

    lax.fori_loop(0, lags, fill_hankel, 0)

    def fill_toeplitz(lag, carry):
        row = pl.multiple_of(lag * block_len, block_len)
        for s in range(sources):
            line = rev_ref[s, pl.ds(lag, 1), :]
            tiled = jnp.broadcast_to(line, (block_len, 2 * block_len))
            skewed = pltpu.roll(tiled, block_len + 1, 1, stride=1, stride_axis=0)
            toeplitz[s, pl.ds(row, block_len), :] = skewed[:, :block_len].astype(toeplitz.dtype)
        return carry

    lax.fori_loop(0, lags, fill_toeplitz, 0)

    for g in range(chans):
        hidden_ref[g] = jnp.dot(hankel[g], toeplitz[0], preferred_element_type=jnp.float32)
    acc = jnp.dot(hankel[0], toeplitz[1], preferred_element_type=jnp.float32)
    for g in range(1, chans):
        acc = acc + jnp.dot(hankel[g], toeplitz[1 + g], preferred_element_type=jnp.float32)
    long_ref[...] = acc


def correlate_all(grad_seq, sources, block_len):
    chans, total_len = grad_seq.shape
    count = sources.shape[0]
    block_count = total_len // block_len
    grad_pad = jnp.pad(
        grad_seq.astype(jnp.float32).reshape(chans, block_count, block_len),
        ((0, 0), (0, block_count), (0, 0)),
    )
    blocks = sources.reshape(count, block_count, block_len)
    padded = jnp.pad(blocks, ((0, 0), (1, 1), (0, 0)))
    pairs = jnp.concatenate([padded[:, :-1], padded[:, 1:]], axis=2)
    rev = pairs[..., ::-1].astype(jnp.float32)
    lags = block_count + 1
    hidden, long = pl.pallas_call(
        conv_kernel,
        out_shape=(
            jax.ShapeDtypeStruct((chans, block_count, block_len), jnp.float32),
            jax.ShapeDtypeStruct((block_count, block_len), jnp.float32),
        ),
        scratch_shapes=[
            pltpu.VMEM((chans, block_count, lags * block_len), jnp.bfloat16),
            pltpu.VMEM((count, lags * block_len, block_len), jnp.bfloat16),
        ],
        compiler_params=pltpu.CompilerParams(vmem_limit_bytes=48 * 1024 * 1024),
    )(grad_pad, rev)
    return hidden.reshape(chans, total_len), long.reshape(total_len)


def swap_kernel(send_ref, out_ref, landed, local_sem, send_sem, recv_sem):
    count = send_ref.shape[0]
    me = lax.axis_index("ctx")
    mine = lax.axis_index("ch")
    barrier = pltpu.get_barrier_semaphore()
    for step in range(1, count):
        peer = lax.rem(me + step, count)
        pl.semaphore_signal(
            barrier, 1, device_id=(peer, mine), device_id_type=pl.DeviceIdType.MESH
        )
    pl.semaphore_wait(barrier, count - 1)
    local = pltpu.make_async_copy(send_ref.at[me], landed.at[me], local_sem)
    local.start()
    copies = []
    for step in range(1, count):
        peer = lax.rem(me + step, count)
        copy = pltpu.make_async_remote_copy(
            src_ref=send_ref.at[peer],
            dst_ref=landed.at[me],
            send_sem=send_sem.at[peer],
            recv_sem=recv_sem.at[me],
            device_id=(peer, mine),
            device_id_type=pl.DeviceIdType.MESH,
        )
        copy.start()
        copies.append(copy)
    local.wait()
    for copy in copies:
        copy.wait_send()
    for step in range(1, count):
        source = lax.rem(me + step, count)
        pltpu.make_async_remote_copy(
            src_ref=send_ref.at[source],
            dst_ref=landed.at[source],
            send_sem=send_sem.at[source],
            recv_sem=recv_sem.at[source],
            device_id=(source, mine),
            device_id_type=pl.DeviceIdType.MESH,
        ).wait_recv()
    out_ref[...] = landed[...]


def swap(chunks, collective_id):
    return pl.pallas_call(
        swap_kernel,
        out_shape=jax.ShapeDtypeStruct(chunks.shape, chunks.dtype),
        in_specs=[pl.BlockSpec(memory_space=pltpu.VMEM)],
        out_specs=pl.BlockSpec(memory_space=pltpu.VMEM),
        scratch_shapes=[
            pltpu.VMEM(chunks.shape, chunks.dtype),
            pltpu.SemaphoreType.DMA,
            pltpu.SemaphoreType.DMA((chunks.shape[0],)),
            pltpu.SemaphoreType.DMA((chunks.shape[0],)),
        ],
        compiler_params=pltpu.CompilerParams(collective_id=collective_id, has_side_effects=True),
    )(chunks)


def gather_kernel(
    rows_ref, long_ref, rows_out, long_out, rows_in, long_in, local_sems,
    rows_send, rows_recv, long_send, long_recv,
):
    count = rows_ref.shape[0]
    groups = lax.axis_size("ch")
    me = lax.axis_index("ctx")
    mine = lax.axis_index("ch")
    mesh_id = pl.DeviceIdType.MESH
    peers = [(c, h) for c in range(count) for h in range(groups) if (c, h) != (0, 0)]
    barrier = pltpu.get_barrier_semaphore()
    for step_c, step_h in peers:
        peer, other = lax.rem(me + step_c, count), lax.rem(mine + step_h, groups)
        pl.semaphore_signal(barrier, 1, device_id=(peer, other), device_id_type=mesh_id)
    pl.semaphore_wait(barrier, len(peers))
    local_rows = pltpu.make_async_copy(rows_ref.at[me], rows_in.at[me], local_sems.at[0])
    local_long = pltpu.make_async_copy(long_ref.at[me], long_in.at[me, mine], local_sems.at[1])
    local_rows.start()
    local_long.start()
    copies = []
    for step in range(1, count):
        peer = lax.rem(me + step, count)
        copy = pltpu.make_async_remote_copy(
            src_ref=rows_ref.at[peer],
            dst_ref=rows_in.at[me],
            send_sem=rows_send.at[peer],
            recv_sem=rows_recv.at[me],
            device_id=(peer, mine),
            device_id_type=mesh_id,
        )
        copy.start()
        copies.append(copy)
    for step_c, step_h in peers:
        peer, other = lax.rem(me + step_c, count), lax.rem(mine + step_h, groups)
        copy = pltpu.make_async_remote_copy(
            src_ref=long_ref.at[peer],
            dst_ref=long_in.at[me, mine],
            send_sem=long_send.at[peer * groups + other],
            recv_sem=long_recv.at[me * groups + mine],
            device_id=(peer, other),
            device_id_type=mesh_id,
        )
        copy.start()
        copies.append(copy)
    local_rows.wait()
    local_long.wait()
    for copy in copies:
        copy.wait_send()
    for step in range(1, count):
        source = lax.rem(me + step, count)
        pltpu.make_async_remote_copy(
            src_ref=rows_ref.at[source],
            dst_ref=rows_in.at[source],
            send_sem=rows_send.at[source],
            recv_sem=rows_recv.at[source],
            device_id=(source, mine),
            device_id_type=mesh_id,
        ).wait_recv()
    for step_c, step_h in peers:
        source, other = lax.rem(me + step_c, count), lax.rem(mine + step_h, groups)
        pltpu.make_async_remote_copy(
            src_ref=long_ref.at[source],
            dst_ref=long_in.at[source, other],
            send_sem=long_send.at[source * groups + other],
            recv_sem=long_recv.at[source * groups + other],
            device_id=(source, other),
            device_id_type=mesh_id,
        ).wait_recv()
    rows_out[...] = rows_in[...]
    long_out[...] = long_in[...]


def gather(rows, longs, groups, collective_id):
    count = rows.shape[0]
    long_shape = (count, groups) + longs.shape[1:]
    vmem = pl.BlockSpec(memory_space=pltpu.VMEM)
    return pl.pallas_call(
        gather_kernel,
        out_shape=(
            jax.ShapeDtypeStruct(rows.shape, rows.dtype),
            jax.ShapeDtypeStruct(long_shape, longs.dtype),
        ),
        in_specs=[vmem, vmem],
        out_specs=(vmem, vmem),
        scratch_shapes=[
            pltpu.VMEM(rows.shape, rows.dtype),
            pltpu.VMEM(long_shape, longs.dtype),
            pltpu.SemaphoreType.DMA((2,)),
            pltpu.SemaphoreType.DMA((count,)),
            pltpu.SemaphoreType.DMA((count,)),
            pltpu.SemaphoreType.DMA((count * groups,)),
            pltpu.SemaphoreType.DMA((count * groups,)),
        ],
        compiler_params=pltpu.CompilerParams(collective_id=collective_id, has_side_effects=True),
    )(rows, longs)


def fused_kernel(
    grad_ref, rev_ref, in_ref, taps_ref, short_out, grad_in_out, long_out,
    hankel, toeplitz, grad_buf, rows_buf, ch_in, rows_in, local_sems,
    rows_send, rows_recv, ch_send, ch_recv,
):
    count = rows_buf.shape[0]
    chans, _, block_len = grad_ref.shape
    block_count = count
    sources, lags, _ = rev_ref.shape
    tap_count = taps_ref.shape[0]
    groups = lax.axis_size("ch")
    me = lax.axis_index("ctx")
    mine = lax.axis_index("ch")
    mesh_id = pl.DeviceIdType.MESH
    peers = [(c, 0) for c in range(1, count)] + [(0, h) for h in range(1, groups)]
    barrier = pltpu.get_barrier_semaphore()
    for step_c, step_h in peers:
        peer, other = lax.rem(me + step_c, count), lax.rem(mine + step_h, groups)
        pl.semaphore_signal(barrier, 1, device_id=(peer, other), device_id_type=mesh_id)

    def fill_hankel(lag, carry):
        col = pl.multiple_of(lag * block_len, block_len)
        for g in range(chans):
            hankel[g, :, pl.ds(col, block_len)] = grad_ref[g, pl.ds(lag, block_count), :].astype(
                hankel.dtype
            )
        return carry

    lax.fori_loop(0, lags, fill_hankel, 0)

    def fill_toeplitz(picked):
        def fill(lag, carry):
            row = pl.multiple_of(lag * block_len, block_len)
            for s in picked:
                line = rev_ref[s, pl.ds(lag, 1), :]
                tiled = jnp.broadcast_to(line, (block_len, 2 * block_len))
                skewed = pltpu.roll(tiled, block_len + 1, 1, stride=1, stride_axis=0)
                toeplitz[s, pl.ds(row, block_len), :] = skewed[:, :block_len].astype(
                    toeplitz.dtype
                )
            return carry

        lax.fori_loop(0, lags, fill, 0)

    fill_toeplitz(range(1, sources))

    acc = jnp.dot(hankel[0], toeplitz[1], preferred_element_type=jnp.float32)
    for g in range(1, chans):
        acc = acc + jnp.dot(hankel[g], toeplitz[1 + g], preferred_element_type=jnp.float32)
    ch_in[mine] = acc
    pl.semaphore_wait(barrier, len(peers))
    partials = []
    for step in range(1, groups):
        other = lax.rem(mine + step, groups)
        copy = pltpu.make_async_remote_copy(
            src_ref=ch_in.at[mine],
            dst_ref=ch_in.at[mine],
            send_sem=ch_send.at[other],
            recv_sem=ch_recv.at[mine],
            device_id=(me, other),
            device_id_type=mesh_id,
        )
        copy.start()
        partials.append(copy)
    fill_toeplitz(range(1))

    lane = lax.broadcasted_iota(jnp.int32, (block_count, block_len), 1)
    short_row = jnp.zeros((block_count, block_len), jnp.float32)
    grad_buf[...] = jnp.zeros_like(grad_buf)
    window = hankel.shape[2]
    hidden_all = jnp.dot(
        hankel[...].reshape(chans * block_count, window),
        toeplitz[0],
        preferred_element_type=jnp.float32,
    )
    for g in range(chans):
        hidden_grad = hidden_all[g * block_count : (g + 1) * block_count]
        grad_buf[g, pl.ds(0, block_count), :] = hidden_grad
        following = grad_buf[g, pl.ds(1, block_count), :]
        total = taps_ref[0, g] * hidden_grad
        for offset in range(1, tap_count):
            here = pltpu.roll(hidden_grad, block_len - offset, 1)
            there = pltpu.roll(following, block_len - offset, 1)
            total = total + taps_ref[offset, g] * jnp.where(
                lane >= block_len - offset, there, here
            )
        rows_buf[:, g, :] = total.astype(jnp.bfloat16).astype(jnp.float32)
        current = in_ref[g, pl.ds(1, block_count), :]
        previous = in_ref[g, pl.ds(0, block_count), :]
        for offset in range(tap_count):
            if offset == 0:
                delayed_in = current
            else:
                delayed_in = jnp.where(
                    lane < offset,
                    pltpu.roll(previous, offset, 1),
                    pltpu.roll(current, offset, 1),
                )
            value = jnp.sum(hidden_grad * delayed_in)
            short_row = jnp.where(lane == offset * chans + g, value, short_row)
    rows_buf[:, chans, :] = short_row

    for copy in partials:
        copy.wait_send()
    for step in range(1, groups):
        source = lax.rem(mine + step, groups)
        pltpu.make_async_remote_copy(
            src_ref=ch_in.at[source],
            dst_ref=ch_in.at[source],
            send_sem=ch_send.at[source],
            recv_sem=ch_recv.at[source],
            device_id=(me, source),
            device_id_type=mesh_id,
        ).wait_recv()
    summed = ch_in[0]
    for h in range(1, groups):
        summed = summed + ch_in[h]
    rows_buf[:, chans + 1, :] = summed

    pairs = rows_in.shape[1]

    def landing(index):
        return rows_in.at[index // pairs, lax.rem(index, pairs)]

    local_rows = pltpu.make_async_copy(rows_buf.at[me], landing(me), local_sems.at[0])
    local_rows.start()
    copies = []
    for step in range(1, count):
        peer = lax.rem(me + step, count)
        copy = pltpu.make_async_remote_copy(
            src_ref=rows_buf.at[peer],
            dst_ref=landing(me),
            send_sem=rows_send.at[peer],
            recv_sem=rows_recv.at[me],
            device_id=(peer, mine),
            device_id_type=mesh_id,
        )
        copy.start()
        copies.append(copy)
    local_rows.wait()
    for copy in copies:
        copy.wait_send()
    for step in range(1, count):
        source = lax.rem(me + step, count)
        pltpu.make_async_remote_copy(
            src_ref=rows_buf.at[source],
            dst_ref=landing(source),
            send_sem=rows_send.at[source],
            recv_sem=rows_recv.at[source],
            device_id=(source, mine),
            device_id_type=mesh_id,
        ).wait_recv()
    for pair in range(pairs):
        short_out[:, pair, :] = rows_in[:, pair, chans, :]
        for g in range(chans):
            grad_in_out[:, pair * chans + g, :] = rows_in[:, pair, g, :].astype(grad_in_out.dtype)
    total = rows_in[:, 0, chans + 1, :]
    for pair in range(1, pairs):
        total = total + rows_in[:, pair, chans + 1, :]
    long_out[...] = total


def fused(grad_seq, sources, in_seq, taps, groups, filter_count, block_len, collective_id):
    chans, total_len = grad_seq.shape
    count = sources.shape[0]
    block_count = total_len // block_len
    grad_pad = jnp.pad(
        grad_seq.astype(jnp.float32).reshape(chans, block_count, block_len),
        ((0, 0), (0, block_count), (0, 0)),
    )
    blocks = sources.reshape(count, block_count, block_len)
    padded = jnp.pad(blocks, ((0, 0), (1, 1), (0, 0)))
    pairs = jnp.concatenate([padded[:, :-1], padded[:, 1:]], axis=2)
    rev = pairs[..., ::-1].astype(jnp.float32)
    in_pad = jnp.pad(in_seq.reshape(chans, block_count, block_len), ((0, 0), (1, 0), (0, 0)))
    lags = block_count + 1
    rows_shape = (block_count, chans + 2, block_len)
    pairs = block_count // filter_count
    landed_shape = (filter_count, pairs, chans + 2, block_len)
    vmem = pl.BlockSpec(memory_space=pltpu.VMEM)
    return pl.pallas_call(
        fused_kernel,
        out_shape=(
            jax.ShapeDtypeStruct((filter_count, pairs, block_len), jnp.float32),
            jax.ShapeDtypeStruct((filter_count, pairs * chans, block_len), jnp.bfloat16),
            jax.ShapeDtypeStruct((filter_count, block_len), jnp.float32),
        ),
        in_specs=[vmem, vmem, vmem, pl.BlockSpec(memory_space=pltpu.SMEM)],
        out_specs=(vmem, vmem, vmem),
        scratch_shapes=[
            pltpu.VMEM((chans, block_count, lags * block_len), jnp.bfloat16),
            pltpu.VMEM((count, lags * block_len, block_len), jnp.bfloat16),
            pltpu.VMEM((chans, block_count + 8, block_len), jnp.float32),
            pltpu.VMEM(rows_shape, jnp.float32),
            pltpu.VMEM((groups, block_count, block_len), jnp.float32),
            pltpu.VMEM(landed_shape, jnp.float32),
            pltpu.SemaphoreType.DMA((1,)),
            pltpu.SemaphoreType.DMA((block_count,)),
            pltpu.SemaphoreType.DMA((block_count,)),
            pltpu.SemaphoreType.DMA((groups,)),
            pltpu.SemaphoreType.DMA((groups,)),
        ],
        compiler_params=pltpu.CompilerParams(
            collective_id=collective_id,
            has_side_effects=True,
            vmem_limit_bytes=48 * 1024 * 1024,
        ),
    )(grad_pad, rev, in_pad, taps)


def relay_kernel(send_ref, out_ref, middle, landed, local_sems, first_send, first_recv, second_send, second_recv):
    firsts, seconds = send_ref.shape[0], send_ref.shape[1]
    me = lax.axis_index("ctx")
    mine = lax.axis_index("ch")
    first, second = me // seconds, lax.rem(me, seconds)
    mesh_id = pl.DeviceIdType.MESH

    def place(f, s):
        return f * seconds + s

    barrier = pltpu.get_barrier_semaphore()
    for step in range(1, firsts):
        peer = place(lax.rem(first + step, firsts), second)
        pl.semaphore_signal(barrier, 1, device_id=(peer, mine), device_id_type=mesh_id)
    for step in range(1, seconds):
        peer = place(first, lax.rem(second + step, seconds))
        pl.semaphore_signal(barrier, 1, device_id=(peer, mine), device_id_type=mesh_id)
    pl.semaphore_wait(barrier, firsts - 1 + seconds - 1)
    local = pltpu.make_async_copy(send_ref.at[first], middle.at[:, first], local_sems.at[0])
    local.start()
    copies = []
    for step in range(1, firsts):
        target = lax.rem(first + step, firsts)
        copy = pltpu.make_async_remote_copy(
            src_ref=send_ref.at[target],
            dst_ref=middle.at[:, first],
            send_sem=first_send.at[target],
            recv_sem=first_recv.at[first],
            device_id=(place(target, second), mine),
            device_id_type=mesh_id,
        )
        copy.start()
        copies.append(copy)
    local.wait()
    for copy in copies:
        copy.wait_send()
    for step in range(1, firsts):
        source = lax.rem(first + step, firsts)
        pltpu.make_async_remote_copy(
            src_ref=send_ref.at[source],
            dst_ref=middle.at[:, source],
            send_sem=first_send.at[source],
            recv_sem=first_recv.at[source],
            device_id=(place(source, second), mine),
            device_id_type=mesh_id,
        ).wait_recv()
    local = pltpu.make_async_copy(middle.at[second], landed.at[second], local_sems.at[1])
    local.start()
    copies = []
    for step in range(1, seconds):
        target = lax.rem(second + step, seconds)
        copy = pltpu.make_async_remote_copy(
            src_ref=middle.at[target],
            dst_ref=landed.at[second],
            send_sem=second_send.at[target],
            recv_sem=second_recv.at[second],
            device_id=(place(first, target), mine),
            device_id_type=mesh_id,
        )
        copy.start()
        copies.append(copy)
    local.wait()
    for copy in copies:
        copy.wait_send()
    for step in range(1, seconds):
        source = lax.rem(second + step, seconds)
        pltpu.make_async_remote_copy(
            src_ref=middle.at[source],
            dst_ref=landed.at[source],
            send_sem=second_send.at[source],
            recv_sem=second_recv.at[source],
            device_id=(place(first, source), mine),
            device_id_type=mesh_id,
        ).wait_recv()
    for r in range(send_ref.shape[2]):
        for f in range(firsts):
            out_ref[r, pl.ds(f * seconds, seconds), :] = landed[:, f, r, :]


def relay(chunks, inner, collective_id):
    count = chunks.shape[0]
    outer = count // inner
    rest = chunks.shape[1:]
    by_first = chunks.reshape((outer, inner) + rest)
    first_shape = (outer, inner) + rest
    second_shape = (inner, outer) + rest
    landed = pl.pallas_call(
        relay_kernel,
        out_shape=jax.ShapeDtypeStruct((rest[0], count) + rest[1:], chunks.dtype),
        in_specs=[pl.BlockSpec(memory_space=pltpu.VMEM)],
        out_specs=pl.BlockSpec(memory_space=pltpu.VMEM),
        scratch_shapes=[
            pltpu.VMEM(second_shape, chunks.dtype),
            pltpu.VMEM(second_shape, chunks.dtype),
            pltpu.SemaphoreType.DMA((2,)),
            pltpu.SemaphoreType.DMA((outer,)),
            pltpu.SemaphoreType.DMA((outer,)),
            pltpu.SemaphoreType.DMA((inner,)),
            pltpu.SemaphoreType.DMA((inner,)),
        ],
        compiler_params=pltpu.CompilerParams(collective_id=collective_id, has_side_effects=True),
    )(by_first)
    return landed


def per_device(inputs, short_filter, long_filter, grad_out):
    tap_count = short_filter.shape[0]
    filter_count, chan_count, shard_len = inputs.shape
    ctx_count = lax.axis_size("ctx")
    my_index = lax.axis_index("ctx")
    total_len = shard_len * ctx_count
    per_dev = filter_count * chan_count // ctx_count
    per_filter = chan_count // per_dev
    block_len = 128
    block_count = total_len // block_len

    send = jnp.concatenate(
        [
            grad_out.reshape(ctx_count, per_dev, shard_len),
            inputs.reshape(ctx_count, per_dev, shard_len),
            jnp.repeat(long_filter, per_filter, axis=0)[:, None, :],
        ],
        axis=1,
    )
    recv = relay(send, 8, 0)
    seqs = recv.reshape(2 * per_dev + 1, total_len)
    grad_seq = seqs[:per_dev]
    in_seq = seqs[per_dev : 2 * per_dev].astype(jnp.float32)
    filt_seq = seqs[2 * per_dev :]
    taps = short_filter.reshape(tap_count, ctx_count, per_dev)
    taps = lax.dynamic_index_in_dim(taps, my_index, axis=1, keepdims=False)

    hidden = sum(
        (taps[offset][:, None] * delayed(in_seq, offset, total_len) for offset in range(tap_count))
    )
    hidden = hidden.astype(jnp.bfloat16)

    groups = lax.axis_size("ch")
    short_rows, grad_in_out, grad_long_out = fused(
        grad_seq,
        jnp.concatenate([filt_seq, hidden], axis=0),
        in_seq,
        taps,
        groups,
        filter_count,
        block_len,
        1,
    )
    short_all = short_rows.reshape(ctx_count, shard_len)[:, : tap_count * per_dev]
    short_all = short_all.reshape(ctx_count, tap_count, per_dev)
    grad_short_out = short_all.transpose(1, 0, 2).reshape(tap_count, filter_count, chan_count)
    return (grad_in_out, grad_long_out, grad_short_out)


def solution(mesh):
    in_specs = (P(None, "ch", "ctx"), P(None, None, "ch"), P(None, "ctx"), P(None, "ch", "ctx"))
    out_specs = (P(None, "ch", "ctx"), P(None, "ctx"), P(None, None, "ch"))
    return jax.shard_map(
        per_device, mesh=mesh, in_specs=in_specs, out_specs=out_specs, check_vma=False
    )
```

```python
import jax
import jax.numpy as jnp
from jax import lax
from jax.experimental import pallas as pl
from jax.experimental.pallas import tpu as pltpu
from jax.sharding import PartitionSpec as P


def delayed(values, by, length):
    return jnp.pad(values, ((0, 0), (by, 0)))[:, :length]


def conv_kernel(grad_ref, rev_ref, hidden_ref, long_ref, hankel, toeplitz):
    chans, _, block_len = grad_ref.shape
    block_count = hidden_ref.shape[1]
    sources, lags, _ = rev_ref.shape

    def fill_hankel(lag, carry):
        col = pl.multiple_of(lag * block_len, block_len)
        for g in range(chans):
            hankel[g, :, pl.ds(col, block_len)] = grad_ref[g, pl.ds(lag, block_count), :].astype(
                hankel.dtype
            )
        return carry

    lax.fori_loop(0, lags, fill_hankel, 0)

    def fill_toeplitz(lag, carry):
        row = pl.multiple_of(lag * block_len, block_len)
        for s in range(sources):
            line = rev_ref[s, pl.ds(lag, 1), :]
            tiled = jnp.broadcast_to(line, (block_len, 2 * block_len))
            skewed = pltpu.roll(tiled, block_len + 1, 1, stride=1, stride_axis=0)
            toeplitz[s, pl.ds(row, block_len), :] = skewed[:, :block_len].astype(toeplitz.dtype)
        return carry

    lax.fori_loop(0, lags, fill_toeplitz, 0)

    for g in range(chans):
        hidden_ref[g] = jnp.dot(hankel[g], toeplitz[0], preferred_element_type=jnp.float32)
    acc = jnp.dot(hankel[0], toeplitz[1], preferred_element_type=jnp.float32)
    for g in range(1, chans):
        acc = acc + jnp.dot(hankel[g], toeplitz[1 + g], preferred_element_type=jnp.float32)
    long_ref[...] = acc


def correlate_all(grad_seq, sources, block_len):
    chans, total_len = grad_seq.shape
    count = sources.shape[0]
    block_count = total_len // block_len
    grad_pad = jnp.pad(
        grad_seq.astype(jnp.float32).reshape(chans, block_count, block_len),
        ((0, 0), (0, block_count), (0, 0)),
    )
    blocks = sources.reshape(count, block_count, block_len)
    padded = jnp.pad(blocks, ((0, 0), (1, 1), (0, 0)))
    pairs = jnp.concatenate([padded[:, :-1], padded[:, 1:]], axis=2)
    rev = pairs[..., ::-1].astype(jnp.float32)
    lags = block_count + 1
    hidden, long = pl.pallas_call(
        conv_kernel,
        out_shape=(
            jax.ShapeDtypeStruct((chans, block_count, block_len), jnp.float32),
            jax.ShapeDtypeStruct((block_count, block_len), jnp.float32),
        ),
        scratch_shapes=[
            pltpu.VMEM((chans, block_count, lags * block_len), jnp.bfloat16),
            pltpu.VMEM((count, lags * block_len, block_len), jnp.bfloat16),
        ],
        compiler_params=pltpu.CompilerParams(vmem_limit_bytes=48 * 1024 * 1024),
    )(grad_pad, rev)
    return hidden.reshape(chans, total_len), long.reshape(total_len)


def swap_kernel(send_ref, out_ref, landed, local_sem, send_sem, recv_sem):
    count = send_ref.shape[0]
    me = lax.axis_index("ctx")
    mine = lax.axis_index("ch")
    barrier = pltpu.get_barrier_semaphore()
    for step in range(1, count):
        peer = lax.rem(me + step, count)
        pl.semaphore_signal(
            barrier, 1, device_id=(peer, mine), device_id_type=pl.DeviceIdType.MESH
        )
    pl.semaphore_wait(barrier, count - 1)
    local = pltpu.make_async_copy(send_ref.at[me], landed.at[me], local_sem)
    local.start()
    copies = []
    for step in range(1, count):
        peer = lax.rem(me + step, count)
        copy = pltpu.make_async_remote_copy(
            src_ref=send_ref.at[peer],
            dst_ref=landed.at[me],
            send_sem=send_sem.at[peer],
            recv_sem=recv_sem.at[me],
            device_id=(peer, mine),
            device_id_type=pl.DeviceIdType.MESH,
        )
        copy.start()
        copies.append(copy)
    local.wait()
    for copy in copies:
        copy.wait_send()
    for step in range(1, count):
        source = lax.rem(me + step, count)
        pltpu.make_async_remote_copy(
            src_ref=send_ref.at[source],
            dst_ref=landed.at[source],
            send_sem=send_sem.at[source],
            recv_sem=recv_sem.at[source],
            device_id=(source, mine),
            device_id_type=pl.DeviceIdType.MESH,
        ).wait_recv()
    out_ref[...] = landed[...]


def swap(chunks, collective_id):
    return pl.pallas_call(
        swap_kernel,
        out_shape=jax.ShapeDtypeStruct(chunks.shape, chunks.dtype),
        in_specs=[pl.BlockSpec(memory_space=pltpu.VMEM)],
        out_specs=pl.BlockSpec(memory_space=pltpu.VMEM),
        scratch_shapes=[
            pltpu.VMEM(chunks.shape, chunks.dtype),
            pltpu.SemaphoreType.DMA,
            pltpu.SemaphoreType.DMA((chunks.shape[0],)),
            pltpu.SemaphoreType.DMA((chunks.shape[0],)),
        ],
        compiler_params=pltpu.CompilerParams(collective_id=collective_id, has_side_effects=True),
    )(chunks)


def gather_kernel(
    rows_ref, long_ref, rows_out, long_out, rows_in, long_in, local_sems,
    rows_send, rows_recv, long_send, long_recv,
):
    count = rows_ref.shape[0]
    groups = lax.axis_size("ch")
    me = lax.axis_index("ctx")
    mine = lax.axis_index("ch")
    mesh_id = pl.DeviceIdType.MESH
    peers = [(c, h) for c in range(count) for h in range(groups) if (c, h) != (0, 0)]
    barrier = pltpu.get_barrier_semaphore()
    for step_c, step_h in peers:
        peer, other = lax.rem(me + step_c, count), lax.rem(mine + step_h, groups)
        pl.semaphore_signal(barrier, 1, device_id=(peer, other), device_id_type=mesh_id)
    pl.semaphore_wait(barrier, len(peers))
    local_rows = pltpu.make_async_copy(rows_ref.at[me], rows_in.at[me], local_sems.at[0])
    local_long = pltpu.make_async_copy(long_ref.at[me], long_in.at[me, mine], local_sems.at[1])
    local_rows.start()
    local_long.start()
    copies = []
    for step in range(1, count):
        peer = lax.rem(me + step, count)
        copy = pltpu.make_async_remote_copy(
            src_ref=rows_ref.at[peer],
            dst_ref=rows_in.at[me],
            send_sem=rows_send.at[peer],
            recv_sem=rows_recv.at[me],
            device_id=(peer, mine),
            device_id_type=mesh_id,
        )
        copy.start()
        copies.append(copy)
    for step_c, step_h in peers:
        peer, other = lax.rem(me + step_c, count), lax.rem(mine + step_h, groups)
        copy = pltpu.make_async_remote_copy(
            src_ref=long_ref.at[peer],
            dst_ref=long_in.at[me, mine],
            send_sem=long_send.at[peer * groups + other],
            recv_sem=long_recv.at[me * groups + mine],
            device_id=(peer, other),
            device_id_type=mesh_id,
        )
        copy.start()
        copies.append(copy)
    local_rows.wait()
    local_long.wait()
    for copy in copies:
        copy.wait_send()
    for step in range(1, count):
        source = lax.rem(me + step, count)
        pltpu.make_async_remote_copy(
            src_ref=rows_ref.at[source],
            dst_ref=rows_in.at[source],
            send_sem=rows_send.at[source],
            recv_sem=rows_recv.at[source],
            device_id=(source, mine),
            device_id_type=mesh_id,
        ).wait_recv()
    for step_c, step_h in peers:
        source, other = lax.rem(me + step_c, count), lax.rem(mine + step_h, groups)
        pltpu.make_async_remote_copy(
            src_ref=long_ref.at[source],
            dst_ref=long_in.at[source, other],
            send_sem=long_send.at[source * groups + other],
            recv_sem=long_recv.at[source * groups + other],
            device_id=(source, other),
            device_id_type=mesh_id,
        ).wait_recv()
    rows_out[...] = rows_in[...]
    long_out[...] = long_in[...]


def gather(rows, longs, groups, collective_id):
    count = rows.shape[0]
    long_shape = (count, groups) + longs.shape[1:]
    vmem = pl.BlockSpec(memory_space=pltpu.VMEM)
    return pl.pallas_call(
        gather_kernel,
        out_shape=(
            jax.ShapeDtypeStruct(rows.shape, rows.dtype),
            jax.ShapeDtypeStruct(long_shape, longs.dtype),
        ),
        in_specs=[vmem, vmem],
        out_specs=(vmem, vmem),
        scratch_shapes=[
            pltpu.VMEM(rows.shape, rows.dtype),
            pltpu.VMEM(long_shape, longs.dtype),
            pltpu.SemaphoreType.DMA((2,)),
            pltpu.SemaphoreType.DMA((count,)),
            pltpu.SemaphoreType.DMA((count,)),
            pltpu.SemaphoreType.DMA((count * groups,)),
            pltpu.SemaphoreType.DMA((count * groups,)),
        ],
        compiler_params=pltpu.CompilerParams(collective_id=collective_id, has_side_effects=True),
    )(rows, longs)


def fused_kernel(
    grad_ref, rev_ref, in_ref, taps_ref, short_out, grad_in_out, long_out,
    hankel, toeplitz, grad_buf, rows_buf, ch_in, rows_in, local_sems,
    rows_send, rows_recv, ch_send, ch_recv,
):
    count = rows_buf.shape[0]
    chans, _, block_len = grad_ref.shape
    block_count = count
    sources, lags, _ = rev_ref.shape
    tap_count = taps_ref.shape[0]
    groups = lax.axis_size("ch")
    me = lax.axis_index("ctx")
    mine = lax.axis_index("ch")
    mesh_id = pl.DeviceIdType.MESH
    peers = [(c, 0) for c in range(1, count)] + [(0, h) for h in range(1, groups)]
    barrier = pltpu.get_barrier_semaphore()
    for step_c, step_h in peers:
        peer, other = lax.rem(me + step_c, count), lax.rem(mine + step_h, groups)
        pl.semaphore_signal(barrier, 1, device_id=(peer, other), device_id_type=mesh_id)

    def fill_hankel(lag, carry):
        col = pl.multiple_of(lag * block_len, block_len)
        for g in range(chans):
            hankel[g, :, pl.ds(col, block_len)] = grad_ref[g, pl.ds(lag, block_count), :].astype(
                hankel.dtype
            )
        return carry

    lax.fori_loop(0, lags, fill_hankel, 0, unroll=5)

    def fill_toeplitz(picked):
        def fill(lag, carry):
            row = pl.multiple_of(lag * block_len, block_len)
            for s in picked:
                line = rev_ref[s, pl.ds(lag, 1), :]
                tiled = jnp.broadcast_to(line, (block_len, 2 * block_len))
                skewed = pltpu.roll(tiled, block_len + 1, 1, stride=1, stride_axis=0)
                toeplitz[s, pl.ds(row, block_len), :] = skewed[:, :block_len].astype(
                    toeplitz.dtype
                )
            return carry

        lax.fori_loop(0, lags, fill, 0, unroll=5)

    fill_toeplitz(range(1, sources))

    acc = jnp.dot(hankel[0], toeplitz[1], preferred_element_type=jnp.float32)
    for g in range(1, chans):
        acc = acc + jnp.dot(hankel[g], toeplitz[1 + g], preferred_element_type=jnp.float32)
    ch_in[mine] = acc
    pl.semaphore_wait(barrier, len(peers))
    partials = []
    for step in range(1, groups):
        other = lax.rem(mine + step, groups)
        copy = pltpu.make_async_remote_copy(
            src_ref=ch_in.at[mine],
            dst_ref=ch_in.at[mine],
            send_sem=ch_send.at[other],
            recv_sem=ch_recv.at[mine],
            device_id=(me, other),
            device_id_type=mesh_id,
        )
        copy.start()
        partials.append(copy)
    fill_toeplitz(range(1))

    lane = lax.broadcasted_iota(jnp.int32, (block_count, block_len), 1)
    short_row = jnp.zeros((block_count, block_len), jnp.float32)
    grad_buf[...] = jnp.zeros_like(grad_buf)
    window = hankel.shape[2]
    hidden_all = jnp.dot(
        hankel[...].reshape(chans * block_count, window),
        toeplitz[0],
        preferred_element_type=jnp.float32,
    )
    for g in range(chans):
        hidden_grad = hidden_all[g * block_count : (g + 1) * block_count]
        grad_buf[g, pl.ds(0, block_count), :] = hidden_grad
        following = grad_buf[g, pl.ds(1, block_count), :]
        total = taps_ref[0, g] * hidden_grad
        for offset in range(1, tap_count):
            here = pltpu.roll(hidden_grad, block_len - offset, 1)
            there = pltpu.roll(following, block_len - offset, 1)
            total = total + taps_ref[offset, g] * jnp.where(
                lane >= block_len - offset, there, here
            )
        rows_buf[:, g, :] = total.astype(jnp.bfloat16).astype(jnp.float32)
        current = in_ref[g, pl.ds(1, block_count), :]
        previous = in_ref[g, pl.ds(0, block_count), :]
        for offset in range(tap_count):
            if offset == 0:
                delayed_in = current
            else:
                delayed_in = jnp.where(
                    lane < offset,
                    pltpu.roll(previous, offset, 1),
                    pltpu.roll(current, offset, 1),
                )
            value = jnp.sum(hidden_grad * delayed_in)
            short_row = jnp.where(lane == offset * chans + g, value, short_row)
    rows_buf[:, chans, :] = short_row

    for copy in partials:
        copy.wait_send()
    for step in range(1, groups):
        source = lax.rem(mine + step, groups)
        pltpu.make_async_remote_copy(
            src_ref=ch_in.at[source],
            dst_ref=ch_in.at[source],
            send_sem=ch_send.at[source],
            recv_sem=ch_recv.at[source],
            device_id=(me, source),
            device_id_type=mesh_id,
        ).wait_recv()
    summed = ch_in[0]
    for h in range(1, groups):
        summed = summed + ch_in[h]
    rows_buf[:, chans + 1, :] = summed

    pairs = rows_in.shape[1]

    def landing(index):
        return rows_in.at[index // pairs, lax.rem(index, pairs)]

    local_rows = pltpu.make_async_copy(rows_buf.at[me], landing(me), local_sems.at[0])
    local_rows.start()
    copies = []
    for step in range(1, count):
        peer = lax.rem(me + step, count)
        copy = pltpu.make_async_remote_copy(
            src_ref=rows_buf.at[peer],
            dst_ref=landing(me),
            send_sem=rows_send.at[peer],
            recv_sem=rows_recv.at[me],
            device_id=(peer, mine),
            device_id_type=mesh_id,
        )
        copy.start()
        copies.append(copy)
    local_rows.wait()
    for copy in copies:
        copy.wait_send()
    for step in range(1, count):
        source = lax.rem(me + step, count)
        pltpu.make_async_remote_copy(
            src_ref=rows_buf.at[source],
            dst_ref=landing(source),
            send_sem=rows_send.at[source],
            recv_sem=rows_recv.at[source],
            device_id=(source, mine),
            device_id_type=mesh_id,
        ).wait_recv()
    for pair in range(pairs):
        short_out[:, pair, :] = rows_in[:, pair, chans, :]
        for g in range(chans):
            grad_in_out[:, pair * chans + g, :] = rows_in[:, pair, g, :].astype(grad_in_out.dtype)
    total = rows_in[:, 0, chans + 1, :]
    for pair in range(1, pairs):
        total = total + rows_in[:, pair, chans + 1, :]
    long_out[...] = total


def fused(grad_seq, sources, in_seq, taps, groups, filter_count, block_len, collective_id):
    chans, total_len = grad_seq.shape
    count = sources.shape[0]
    block_count = total_len // block_len
    grad_pad = jnp.pad(
        grad_seq.astype(jnp.float32).reshape(chans, block_count, block_len),
        ((0, 0), (0, block_count), (0, 0)),
    )
    blocks = sources.reshape(count, block_count, block_len)
    padded = jnp.pad(blocks, ((0, 0), (1, 1), (0, 0)))
    pairs = jnp.concatenate([padded[:, :-1], padded[:, 1:]], axis=2)
    rev = pairs[..., ::-1].astype(jnp.float32)
    in_pad = jnp.pad(in_seq.reshape(chans, block_count, block_len), ((0, 0), (1, 0), (0, 0)))
    lags = block_count + 1
    rows_shape = (block_count, chans + 2, block_len)
    pairs = block_count // filter_count
    landed_shape = (filter_count, pairs, chans + 2, block_len)
    vmem = pl.BlockSpec(memory_space=pltpu.VMEM)
    return pl.pallas_call(
        fused_kernel,
        out_shape=(
            jax.ShapeDtypeStruct((filter_count, pairs, block_len), jnp.float32),
            jax.ShapeDtypeStruct((filter_count, pairs * chans, block_len), jnp.bfloat16),
            jax.ShapeDtypeStruct((filter_count, block_len), jnp.float32),
        ),
        in_specs=[vmem, vmem, vmem, pl.BlockSpec(memory_space=pltpu.SMEM)],
        out_specs=(vmem, vmem, vmem),
        scratch_shapes=[
            pltpu.VMEM((chans, block_count, lags * block_len), jnp.bfloat16),
            pltpu.VMEM((count, lags * block_len, block_len), jnp.bfloat16),
            pltpu.VMEM((chans, block_count + 8, block_len), jnp.float32),
            pltpu.VMEM(rows_shape, jnp.float32),
            pltpu.VMEM((groups, block_count, block_len), jnp.float32),
            pltpu.VMEM(landed_shape, jnp.float32),
            pltpu.SemaphoreType.DMA((1,)),
            pltpu.SemaphoreType.DMA((block_count,)),
            pltpu.SemaphoreType.DMA((block_count,)),
            pltpu.SemaphoreType.DMA((groups,)),
            pltpu.SemaphoreType.DMA((groups,)),
        ],
        compiler_params=pltpu.CompilerParams(
            collective_id=collective_id,
            has_side_effects=True,
            vmem_limit_bytes=48 * 1024 * 1024,
        ),
    )(grad_pad, rev, in_pad, taps)


def relay_kernel(send_ref, out_ref, middle, landed, local_sems, first_send, first_recv, second_send, second_recv):
    firsts, seconds = send_ref.shape[0], send_ref.shape[1]
    me = lax.axis_index("ctx")
    mine = lax.axis_index("ch")
    first, second = me // seconds, lax.rem(me, seconds)
    mesh_id = pl.DeviceIdType.MESH

    def place(f, s):
        return f * seconds + s

    barrier = pltpu.get_barrier_semaphore()
    for step in range(1, firsts):
        peer = place(lax.rem(first + step, firsts), second)
        pl.semaphore_signal(barrier, 1, device_id=(peer, mine), device_id_type=mesh_id)
    for step in range(1, seconds):
        peer = place(first, lax.rem(second + step, seconds))
        pl.semaphore_signal(barrier, 1, device_id=(peer, mine), device_id_type=mesh_id)
    pl.semaphore_wait(barrier, firsts - 1 + seconds - 1)
    local = pltpu.make_async_copy(send_ref.at[first], middle.at[:, first], local_sems.at[0])
    local.start()
    copies = []
    for step in range(1, firsts):
        target = lax.rem(first + step, firsts)
        copy = pltpu.make_async_remote_copy(
            src_ref=send_ref.at[target],
            dst_ref=middle.at[:, first],
            send_sem=first_send.at[target],
            recv_sem=first_recv.at[first],
            device_id=(place(target, second), mine),
            device_id_type=mesh_id,
        )
        copy.start()
        copies.append(copy)
    local.wait()
    for copy in copies:
        copy.wait_send()
    for step in range(1, firsts):
        source = lax.rem(first + step, firsts)
        pltpu.make_async_remote_copy(
            src_ref=send_ref.at[source],
            dst_ref=middle.at[:, source],
            send_sem=first_send.at[source],
            recv_sem=first_recv.at[source],
            device_id=(place(source, second), mine),
            device_id_type=mesh_id,
        ).wait_recv()
    local = pltpu.make_async_copy(middle.at[second], landed.at[second], local_sems.at[1])
    local.start()
    copies = []
    for step in range(1, seconds):
        target = lax.rem(second + step, seconds)
        copy = pltpu.make_async_remote_copy(
            src_ref=middle.at[target],
            dst_ref=landed.at[second],
            send_sem=second_send.at[target],
            recv_sem=second_recv.at[second],
            device_id=(place(first, target), mine),
            device_id_type=mesh_id,
        )
        copy.start()
        copies.append(copy)
    local.wait()
    for copy in copies:
        copy.wait_send()
    for step in range(1, seconds):
        source = lax.rem(second + step, seconds)
        pltpu.make_async_remote_copy(
            src_ref=middle.at[source],
            dst_ref=landed.at[source],
            send_sem=second_send.at[source],
            recv_sem=second_recv.at[source],
            device_id=(place(first, source), mine),
            device_id_type=mesh_id,
        ).wait_recv()
    out_ref[...] = landed[...]


def relay(chunks, inner, collective_id):
    count = chunks.shape[0]
    outer = count // inner
    rest = chunks.shape[1:]
    by_first = chunks.reshape((outer, inner) + rest)
    first_shape = (outer, inner) + rest
    second_shape = (inner, outer) + rest
    landed = pl.pallas_call(
        relay_kernel,
        out_shape=jax.ShapeDtypeStruct(second_shape, chunks.dtype),
        in_specs=[pl.BlockSpec(memory_space=pltpu.VMEM)],
        out_specs=pl.BlockSpec(memory_space=pltpu.VMEM),
        scratch_shapes=[
            pltpu.VMEM(second_shape, chunks.dtype),
            pltpu.VMEM(second_shape, chunks.dtype),
            pltpu.SemaphoreType.DMA((2,)),
            pltpu.SemaphoreType.DMA((outer,)),
            pltpu.SemaphoreType.DMA((outer,)),
            pltpu.SemaphoreType.DMA((inner,)),
            pltpu.SemaphoreType.DMA((inner,)),
        ],
        compiler_params=pltpu.CompilerParams(collective_id=collective_id, has_side_effects=True),
    )(by_first)
    return landed.swapaxes(0, 1).reshape(chunks.shape)


def per_device(inputs, short_filter, long_filter, grad_out):
    tap_count = short_filter.shape[0]
    filter_count, chan_count, shard_len = inputs.shape
    ctx_count = lax.axis_size("ctx")
    my_index = lax.axis_index("ctx")
    total_len = shard_len * ctx_count
    per_dev = filter_count * chan_count // ctx_count
    per_filter = chan_count // per_dev
    block_len = 128
    block_count = total_len // block_len

    send = jnp.concatenate(
        [
            grad_out.reshape(ctx_count, per_dev, shard_len),
            inputs.reshape(ctx_count, per_dev, shard_len),
            jnp.repeat(long_filter, per_filter, axis=0)[:, None, :],
        ],
        axis=1,
    )
    recv = relay(send, 8, 0)
    seqs = recv.transpose(1, 0, 2).reshape(2 * per_dev + 1, total_len)
    grad_seq = seqs[:per_dev]
    in_seq = seqs[per_dev : 2 * per_dev].astype(jnp.float32)
    filt_seq = seqs[2 * per_dev :]
    taps = short_filter.reshape(tap_count, ctx_count, per_dev)
    taps = lax.dynamic_index_in_dim(taps, my_index, axis=1, keepdims=False)

    hidden = sum(
        (taps[offset][:, None] * delayed(in_seq, offset, total_len) for offset in range(tap_count))
    )
    hidden = hidden.astype(jnp.bfloat16)

    groups = lax.axis_size("ch")
    short_rows, grad_in_out, grad_long_out = fused(
        grad_seq,
        jnp.concatenate([filt_seq, hidden], axis=0),
        in_seq,
        taps,
        groups,
        filter_count,
        block_len,
        1,
    )
    short_all = short_rows.reshape(ctx_count, shard_len)[:, : tap_count * per_dev]
    short_all = short_all.reshape(ctx_count, tap_count, per_dev)
    grad_short_out = short_all.transpose(1, 0, 2).reshape(tap_count, filter_count, chan_count)
    return (grad_in_out, grad_long_out, grad_short_out)


def solution(mesh):
    in_specs = (P(None, "ch", "ctx"), P(None, None, "ch"), P(None, "ctx"), P(None, "ch", "ctx"))
    out_specs = (P(None, "ch", "ctx"), P(None, "ctx"), P(None, None, "ch"))
    return jax.shard_map(
        per_device, mesh=mesh, in_specs=in_specs, out_specs=out_specs, check_vma=False
    )
```

```python
import jax
import jax.numpy as jnp
from jax import lax
from jax.experimental import pallas as pl
from jax.experimental.pallas import tpu as pltpu
from jax.sharding import PartitionSpec as P


def delayed(values, by, length):
    return jnp.pad(values, ((0, 0), (by, 0)))[:, :length]


def conv_kernel(grad_ref, rev_ref, hidden_ref, long_ref, hankel, toeplitz):
    chans, _, block_len = grad_ref.shape
    block_count = hidden_ref.shape[1]
    sources, lags, _ = rev_ref.shape

    def fill_hankel(lag, carry):
        col = pl.multiple_of(lag * block_len, block_len)
        for g in range(chans):
            hankel[g, :, pl.ds(col, block_len)] = grad_ref[g, pl.ds(lag, block_count), :].astype(
                hankel.dtype
            )
        return carry

    lax.fori_loop(0, lags, fill_hankel, 0)

    def fill_toeplitz(lag, carry):
        row = pl.multiple_of(lag * block_len, block_len)
        for s in range(sources):
            line = rev_ref[s, pl.ds(lag, 1), :]
            tiled = jnp.broadcast_to(line, (block_len, 2 * block_len))
            skewed = pltpu.roll(tiled, block_len + 1, 1, stride=1, stride_axis=0)
            toeplitz[s, pl.ds(row, block_len), :] = skewed[:, :block_len].astype(toeplitz.dtype)
        return carry

    lax.fori_loop(0, lags, fill_toeplitz, 0)

    for g in range(chans):
        hidden_ref[g] = jnp.dot(hankel[g], toeplitz[0], preferred_element_type=jnp.float32)
    acc = jnp.dot(hankel[0], toeplitz[1], preferred_element_type=jnp.float32)
    for g in range(1, chans):
        acc = acc + jnp.dot(hankel[g], toeplitz[1 + g], preferred_element_type=jnp.float32)
    long_ref[...] = acc


def correlate_all(grad_seq, sources, block_len):
    chans, total_len = grad_seq.shape
    count = sources.shape[0]
    block_count = total_len // block_len
    grad_pad = jnp.pad(
        grad_seq.astype(jnp.float32).reshape(chans, block_count, block_len),
        ((0, 0), (0, block_count), (0, 0)),
    )
    blocks = sources.reshape(count, block_count, block_len)
    padded = jnp.pad(blocks, ((0, 0), (1, 1), (0, 0)))
    pairs = jnp.concatenate([padded[:, :-1], padded[:, 1:]], axis=2)
    rev = pairs[..., ::-1].astype(jnp.float32)
    lags = block_count + 1
    hidden, long = pl.pallas_call(
        conv_kernel,
        out_shape=(
            jax.ShapeDtypeStruct((chans, block_count, block_len), jnp.float32),
            jax.ShapeDtypeStruct((block_count, block_len), jnp.float32),
        ),
        scratch_shapes=[
            pltpu.VMEM((chans, block_count, lags * block_len), jnp.bfloat16),
            pltpu.VMEM((count, lags * block_len, block_len), jnp.bfloat16),
        ],
        compiler_params=pltpu.CompilerParams(vmem_limit_bytes=48 * 1024 * 1024),
    )(grad_pad, rev)
    return hidden.reshape(chans, total_len), long.reshape(total_len)


def swap_kernel(send_ref, out_ref, landed, local_sem, send_sem, recv_sem):
    count = send_ref.shape[0]
    me = lax.axis_index("ctx")
    mine = lax.axis_index("ch")
    barrier = pltpu.get_barrier_semaphore()
    for step in range(1, count):
        peer = lax.rem(me + step, count)
        pl.semaphore_signal(
            barrier, 1, device_id=(peer, mine), device_id_type=pl.DeviceIdType.MESH
        )
    pl.semaphore_wait(barrier, count - 1)
    local = pltpu.make_async_copy(send_ref.at[me], landed.at[me], local_sem)
    local.start()
    copies = []
    for step in range(1, count):
        peer = lax.rem(me + step, count)
        copy = pltpu.make_async_remote_copy(
            src_ref=send_ref.at[peer],
            dst_ref=landed.at[me],
            send_sem=send_sem.at[peer],
            recv_sem=recv_sem.at[me],
            device_id=(peer, mine),
            device_id_type=pl.DeviceIdType.MESH,
        )
        copy.start()
        copies.append(copy)
    local.wait()
    for copy in copies:
        copy.wait_send()
    for step in range(1, count):
        source = lax.rem(me + step, count)
        pltpu.make_async_remote_copy(
            src_ref=send_ref.at[source],
            dst_ref=landed.at[source],
            send_sem=send_sem.at[source],
            recv_sem=recv_sem.at[source],
            device_id=(source, mine),
            device_id_type=pl.DeviceIdType.MESH,
        ).wait_recv()
    out_ref[...] = landed[...]


def swap(chunks, collective_id):
    return pl.pallas_call(
        swap_kernel,
        out_shape=jax.ShapeDtypeStruct(chunks.shape, chunks.dtype),
        in_specs=[pl.BlockSpec(memory_space=pltpu.VMEM)],
        out_specs=pl.BlockSpec(memory_space=pltpu.VMEM),
        scratch_shapes=[
            pltpu.VMEM(chunks.shape, chunks.dtype),
            pltpu.SemaphoreType.DMA,
            pltpu.SemaphoreType.DMA((chunks.shape[0],)),
            pltpu.SemaphoreType.DMA((chunks.shape[0],)),
        ],
        compiler_params=pltpu.CompilerParams(collective_id=collective_id, has_side_effects=True),
    )(chunks)


def gather_kernel(
    rows_ref, long_ref, rows_out, long_out, rows_in, long_in, local_sems,
    rows_send, rows_recv, long_send, long_recv,
):
    count = rows_ref.shape[0]
    groups = lax.axis_size("ch")
    me = lax.axis_index("ctx")
    mine = lax.axis_index("ch")
    mesh_id = pl.DeviceIdType.MESH
    peers = [(c, h) for c in range(count) for h in range(groups) if (c, h) != (0, 0)]
    barrier = pltpu.get_barrier_semaphore()
    for step_c, step_h in peers:
        peer, other = lax.rem(me + step_c, count), lax.rem(mine + step_h, groups)
        pl.semaphore_signal(barrier, 1, device_id=(peer, other), device_id_type=mesh_id)
    pl.semaphore_wait(barrier, len(peers))
    local_rows = pltpu.make_async_copy(rows_ref.at[me], rows_in.at[me], local_sems.at[0])
    local_long = pltpu.make_async_copy(long_ref.at[me], long_in.at[me, mine], local_sems.at[1])
    local_rows.start()
    local_long.start()
    copies = []
    for step in range(1, count):
        peer = lax.rem(me + step, count)
        copy = pltpu.make_async_remote_copy(
            src_ref=rows_ref.at[peer],
            dst_ref=rows_in.at[me],
            send_sem=rows_send.at[peer],
            recv_sem=rows_recv.at[me],
            device_id=(peer, mine),
            device_id_type=mesh_id,
        )
        copy.start()
        copies.append(copy)
    for step_c, step_h in peers:
        peer, other = lax.rem(me + step_c, count), lax.rem(mine + step_h, groups)
        copy = pltpu.make_async_remote_copy(
            src_ref=long_ref.at[peer],
            dst_ref=long_in.at[me, mine],
            send_sem=long_send.at[peer * groups + other],
            recv_sem=long_recv.at[me * groups + mine],
            device_id=(peer, other),
            device_id_type=mesh_id,
        )
        copy.start()
        copies.append(copy)
    local_rows.wait()
    local_long.wait()
    for copy in copies:
        copy.wait_send()
    for step in range(1, count):
        source = lax.rem(me + step, count)
        pltpu.make_async_remote_copy(
            src_ref=rows_ref.at[source],
            dst_ref=rows_in.at[source],
            send_sem=rows_send.at[source],
            recv_sem=rows_recv.at[source],
            device_id=(source, mine),
            device_id_type=mesh_id,
        ).wait_recv()
    for step_c, step_h in peers:
        source, other = lax.rem(me + step_c, count), lax.rem(mine + step_h, groups)
        pltpu.make_async_remote_copy(
            src_ref=long_ref.at[source],
            dst_ref=long_in.at[source, other],
            send_sem=long_send.at[source * groups + other],
            recv_sem=long_recv.at[source * groups + other],
            device_id=(source, other),
            device_id_type=mesh_id,
        ).wait_recv()
    rows_out[...] = rows_in[...]
    long_out[...] = long_in[...]


def gather(rows, longs, groups, collective_id):
    count = rows.shape[0]
    long_shape = (count, groups) + longs.shape[1:]
    vmem = pl.BlockSpec(memory_space=pltpu.VMEM)
    return pl.pallas_call(
        gather_kernel,
        out_shape=(
            jax.ShapeDtypeStruct(rows.shape, rows.dtype),
            jax.ShapeDtypeStruct(long_shape, longs.dtype),
        ),
        in_specs=[vmem, vmem],
        out_specs=(vmem, vmem),
        scratch_shapes=[
            pltpu.VMEM(rows.shape, rows.dtype),
            pltpu.VMEM(long_shape, longs.dtype),
            pltpu.SemaphoreType.DMA((2,)),
            pltpu.SemaphoreType.DMA((count,)),
            pltpu.SemaphoreType.DMA((count,)),
            pltpu.SemaphoreType.DMA((count * groups,)),
            pltpu.SemaphoreType.DMA((count * groups,)),
        ],
        compiler_params=pltpu.CompilerParams(collective_id=collective_id, has_side_effects=True),
    )(rows, longs)


def fused_kernel(
    grad_ref, rev_ref, in_ref, taps_ref, short_out, grad_in_out, long_out,
    hankel, toeplitz, grad_buf, rows_buf, ch_in, rows_in, local_sems,
    rows_send, rows_recv, ch_send, ch_recv,
):
    count = rows_buf.shape[0]
    chans, _, block_len = grad_ref.shape
    block_count = count
    sources, lags, _ = rev_ref.shape
    tap_count = taps_ref.shape[0]
    groups = lax.axis_size("ch")
    me = lax.axis_index("ctx")
    mine = lax.axis_index("ch")
    mesh_id = pl.DeviceIdType.MESH
    peers = [(c, 0) for c in range(1, count)] + [(0, h) for h in range(1, groups)]
    barrier = pltpu.get_barrier_semaphore()
    for step_c, step_h in peers:
        peer, other = lax.rem(me + step_c, count), lax.rem(mine + step_h, groups)
        pl.semaphore_signal(barrier, 1, device_id=(peer, other), device_id_type=mesh_id)

    def fill_hankel(lag, carry):
        col = pl.multiple_of(lag * block_len, block_len)
        for g in range(chans):
            hankel[g, :, pl.ds(col, block_len)] = grad_ref[g, pl.ds(lag, block_count), :].astype(
                hankel.dtype
            )
        return carry

    lax.fori_loop(0, lags, fill_hankel, 0, unroll=13)

    def fill_toeplitz(picked):
        def fill(lag, carry):
            row = pl.multiple_of(lag * block_len, block_len)
            for s in picked:
                line = rev_ref[s, pl.ds(lag, 1), :]
                tiled = jnp.broadcast_to(line, (block_len, 2 * block_len))
                skewed = pltpu.roll(tiled, block_len + 1, 1, stride=1, stride_axis=0)
                toeplitz[s, pl.ds(row, block_len), :] = skewed[:, :block_len].astype(
                    toeplitz.dtype
                )
            return carry

        lax.fori_loop(0, lags, fill, 0, unroll=13)

    fill_toeplitz(range(1, sources))

    acc = jnp.dot(hankel[0], toeplitz[1], preferred_element_type=jnp.float32)
    for g in range(1, chans):
        acc = acc + jnp.dot(hankel[g], toeplitz[1 + g], preferred_element_type=jnp.float32)
    ch_in[mine] = acc
    pl.semaphore_wait(barrier, len(peers))
    partials = []
    for step in range(1, groups):
        other = lax.rem(mine + step, groups)
        copy = pltpu.make_async_remote_copy(
            src_ref=ch_in.at[mine],
            dst_ref=ch_in.at[mine],
            send_sem=ch_send.at[other],
            recv_sem=ch_recv.at[mine],
            device_id=(me, other),
            device_id_type=mesh_id,
        )
        copy.start()
        partials.append(copy)
    fill_toeplitz(range(1))

    lane = lax.broadcasted_iota(jnp.int32, (block_count, block_len), 1)
    short_row = jnp.zeros((block_count, block_len), jnp.float32)
    grad_buf[...] = jnp.zeros_like(grad_buf)
    window = hankel.shape[2]
    hidden_all = jnp.dot(
        hankel[...].reshape(chans * block_count, window),
        toeplitz[0],
        preferred_element_type=jnp.float32,
    )
    for g in range(chans):
        hidden_grad = hidden_all[g * block_count : (g + 1) * block_count]
        grad_buf[g, pl.ds(0, block_count), :] = hidden_grad
        following = grad_buf[g, pl.ds(1, block_count), :]
        total = taps_ref[0, g] * hidden_grad
        for offset in range(1, tap_count):
            here = pltpu.roll(hidden_grad, block_len - offset, 1)
            there = pltpu.roll(following, block_len - offset, 1)
            total = total + taps_ref[offset, g] * jnp.where(
                lane >= block_len - offset, there, here
            )
        rows_buf[:, g, :] = total.astype(jnp.bfloat16).astype(jnp.float32)
        current = in_ref[g, pl.ds(1, block_count), :]
        previous = in_ref[g, pl.ds(0, block_count), :]
        for offset in range(tap_count):
            if offset == 0:
                delayed_in = current
            else:
                delayed_in = jnp.where(
                    lane < offset,
                    pltpu.roll(previous, offset, 1),
                    pltpu.roll(current, offset, 1),
                )
            value = jnp.sum(hidden_grad * delayed_in)
            short_row = jnp.where(lane == offset * chans + g, value, short_row)
    rows_buf[:, chans, :] = short_row

    for copy in partials:
        copy.wait_send()
    for step in range(1, groups):
        source = lax.rem(mine + step, groups)
        pltpu.make_async_remote_copy(
            src_ref=ch_in.at[source],
            dst_ref=ch_in.at[source],
            send_sem=ch_send.at[source],
            recv_sem=ch_recv.at[source],
            device_id=(me, source),
            device_id_type=mesh_id,
        ).wait_recv()
    summed = ch_in[0]
    for h in range(1, groups):
        summed = summed + ch_in[h]
    rows_buf[:, chans + 1, :] = summed

    pairs = rows_in.shape[1]

    def landing(index):
        return rows_in.at[index // pairs, lax.rem(index, pairs)]

    local_rows = pltpu.make_async_copy(rows_buf.at[me], landing(me), local_sems.at[0])
    local_rows.start()
    copies = []
    for step in range(1, count):
        peer = lax.rem(me + step, count)
        copy = pltpu.make_async_remote_copy(
            src_ref=rows_buf.at[peer],
            dst_ref=landing(me),
            send_sem=rows_send.at[peer],
            recv_sem=rows_recv.at[me],
            device_id=(peer, mine),
            device_id_type=mesh_id,
        )
        copy.start()
        copies.append(copy)
    local_rows.wait()
    for copy in copies:
        copy.wait_send()
    for step in range(1, count):
        source = lax.rem(me + step, count)
        pltpu.make_async_remote_copy(
            src_ref=rows_buf.at[source],
            dst_ref=landing(source),
            send_sem=rows_send.at[source],
            recv_sem=rows_recv.at[source],
            device_id=(source, mine),
            device_id_type=mesh_id,
        ).wait_recv()
    for pair in range(pairs):
        short_out[:, pair, :] = rows_in[:, pair, chans, :]
        for g in range(chans):
            grad_in_out[:, pair * chans + g, :] = rows_in[:, pair, g, :].astype(grad_in_out.dtype)
    total = rows_in[:, 0, chans + 1, :]
    for pair in range(1, pairs):
        total = total + rows_in[:, pair, chans + 1, :]
    long_out[...] = total


def fused(grad_seq, sources, in_seq, taps, groups, filter_count, block_len, collective_id):
    chans, total_len = grad_seq.shape
    count = sources.shape[0]
    block_count = total_len // block_len
    grad_pad = jnp.pad(
        grad_seq.astype(jnp.float32).reshape(chans, block_count, block_len),
        ((0, 0), (0, block_count), (0, 0)),
    )
    blocks = sources.reshape(count, block_count, block_len)
    padded = jnp.pad(blocks, ((0, 0), (1, 1), (0, 0)))
    pairs = jnp.concatenate([padded[:, :-1], padded[:, 1:]], axis=2)
    rev = pairs[..., ::-1].astype(jnp.float32)
    in_pad = jnp.pad(in_seq.reshape(chans, block_count, block_len), ((0, 0), (1, 0), (0, 0)))
    lags = block_count + 1
    rows_shape = (block_count, chans + 2, block_len)
    pairs = block_count // filter_count
    landed_shape = (filter_count, pairs, chans + 2, block_len)
    vmem = pl.BlockSpec(memory_space=pltpu.VMEM)
    return pl.pallas_call(
        fused_kernel,
        out_shape=(
            jax.ShapeDtypeStruct((filter_count, pairs, block_len), jnp.float32),
            jax.ShapeDtypeStruct((filter_count, pairs * chans, block_len), jnp.bfloat16),
            jax.ShapeDtypeStruct((filter_count, block_len), jnp.float32),
        ),
        in_specs=[vmem, vmem, vmem, pl.BlockSpec(memory_space=pltpu.SMEM)],
        out_specs=(vmem, vmem, vmem),
        scratch_shapes=[
            pltpu.VMEM((chans, block_count, lags * block_len), jnp.bfloat16),
            pltpu.VMEM((count, lags * block_len, block_len), jnp.bfloat16),
            pltpu.VMEM((chans, block_count + 8, block_len), jnp.float32),
            pltpu.VMEM(rows_shape, jnp.float32),
            pltpu.VMEM((groups, block_count, block_len), jnp.float32),
            pltpu.VMEM(landed_shape, jnp.float32),
            pltpu.SemaphoreType.DMA((1,)),
            pltpu.SemaphoreType.DMA((block_count,)),
            pltpu.SemaphoreType.DMA((block_count,)),
            pltpu.SemaphoreType.DMA((groups,)),
            pltpu.SemaphoreType.DMA((groups,)),
        ],
        compiler_params=pltpu.CompilerParams(
            collective_id=collective_id,
            has_side_effects=True,
            vmem_limit_bytes=48 * 1024 * 1024,
        ),
    )(grad_pad, rev, in_pad, taps)


def relay_kernel(send_ref, out_ref, middle, landed, local_sems, first_send, first_recv, second_send, second_recv):
    firsts, seconds = send_ref.shape[0], send_ref.shape[1]
    me = lax.axis_index("ctx")
    mine = lax.axis_index("ch")
    first, second = me // seconds, lax.rem(me, seconds)
    mesh_id = pl.DeviceIdType.MESH

    def place(f, s):
        return f * seconds + s

    barrier = pltpu.get_barrier_semaphore()
    for step in range(1, firsts):
        peer = place(lax.rem(first + step, firsts), second)
        pl.semaphore_signal(barrier, 1, device_id=(peer, mine), device_id_type=mesh_id)
    for step in range(1, seconds):
        peer = place(first, lax.rem(second + step, seconds))
        pl.semaphore_signal(barrier, 1, device_id=(peer, mine), device_id_type=mesh_id)
    pl.semaphore_wait(barrier, firsts - 1 + seconds - 1)
    local = pltpu.make_async_copy(send_ref.at[first], middle.at[:, first], local_sems.at[0])
    local.start()
    copies = []
    for step in range(1, firsts):
        target = lax.rem(first + step, firsts)
        copy = pltpu.make_async_remote_copy(
            src_ref=send_ref.at[target],
            dst_ref=middle.at[:, first],
            send_sem=first_send.at[target],
            recv_sem=first_recv.at[first],
            device_id=(place(target, second), mine),
            device_id_type=mesh_id,
        )
        copy.start()
        copies.append(copy)
    local.wait()
    for copy in copies:
        copy.wait_send()
    for step in range(1, firsts):
        source = lax.rem(first + step, firsts)
        pltpu.make_async_remote_copy(
            src_ref=send_ref.at[source],
            dst_ref=middle.at[:, source],
            send_sem=first_send.at[source],
            recv_sem=first_recv.at[source],
            device_id=(place(source, second), mine),
            device_id_type=mesh_id,
        ).wait_recv()
    local = pltpu.make_async_copy(middle.at[second], landed.at[second], local_sems.at[1])
    local.start()
    copies = []
    for step in range(1, seconds):
        target = lax.rem(second + step, seconds)
        copy = pltpu.make_async_remote_copy(
            src_ref=middle.at[target],
            dst_ref=landed.at[second],
            send_sem=second_send.at[target],
            recv_sem=second_recv.at[second],
            device_id=(place(first, target), mine),
            device_id_type=mesh_id,
        )
        copy.start()
        copies.append(copy)
    local.wait()
    for copy in copies:
        copy.wait_send()
    for step in range(1, seconds):
        source = lax.rem(second + step, seconds)
        pltpu.make_async_remote_copy(
            src_ref=middle.at[source],
            dst_ref=landed.at[source],
            send_sem=second_send.at[source],
            recv_sem=second_recv.at[source],
            device_id=(place(first, source), mine),
            device_id_type=mesh_id,
        ).wait_recv()
    out_ref[...] = landed[...]


def relay(chunks, inner, collective_id):
    count = chunks.shape[0]
    outer = count // inner
    rest = chunks.shape[1:]
    by_first = chunks.reshape((outer, inner) + rest)
    first_shape = (outer, inner) + rest
    second_shape = (inner, outer) + rest
    landed = pl.pallas_call(
        relay_kernel,
        out_shape=jax.ShapeDtypeStruct(second_shape, chunks.dtype),
        in_specs=[pl.BlockSpec(memory_space=pltpu.VMEM)],
        out_specs=pl.BlockSpec(memory_space=pltpu.VMEM),
        scratch_shapes=[
            pltpu.VMEM(second_shape, chunks.dtype),
            pltpu.VMEM(second_shape, chunks.dtype),
            pltpu.SemaphoreType.DMA((2,)),
            pltpu.SemaphoreType.DMA((outer,)),
            pltpu.SemaphoreType.DMA((outer,)),
            pltpu.SemaphoreType.DMA((inner,)),
            pltpu.SemaphoreType.DMA((inner,)),
        ],
        compiler_params=pltpu.CompilerParams(collective_id=collective_id, has_side_effects=True),
    )(by_first)
    return landed.swapaxes(0, 1).reshape(chunks.shape)


def per_device(inputs, short_filter, long_filter, grad_out):
    tap_count = short_filter.shape[0]
    filter_count, chan_count, shard_len = inputs.shape
    ctx_count = lax.axis_size("ctx")
    my_index = lax.axis_index("ctx")
    total_len = shard_len * ctx_count
    per_dev = filter_count * chan_count // ctx_count
    per_filter = chan_count // per_dev
    block_len = 128
    block_count = total_len // block_len

    send = jnp.concatenate(
        [
            grad_out.reshape(ctx_count, per_dev, shard_len),
            inputs.reshape(ctx_count, per_dev, shard_len),
            jnp.repeat(long_filter, per_filter, axis=0)[:, None, :],
        ],
        axis=1,
    )
    recv = relay(send, 8, 0)
    seqs = recv.transpose(1, 0, 2).reshape(2 * per_dev + 1, total_len)
    grad_seq = seqs[:per_dev]
    in_seq = seqs[per_dev : 2 * per_dev].astype(jnp.float32)
    filt_seq = seqs[2 * per_dev :]
    taps = short_filter.reshape(tap_count, ctx_count, per_dev)
    taps = lax.dynamic_index_in_dim(taps, my_index, axis=1, keepdims=False)

    hidden = sum(
        (taps[offset][:, None] * delayed(in_seq, offset, total_len) for offset in range(tap_count))
    )
    hidden = hidden.astype(jnp.bfloat16)

    groups = lax.axis_size("ch")
    short_rows, grad_in_out, grad_long_out = fused(
        grad_seq,
        jnp.concatenate([filt_seq, hidden], axis=0),
        in_seq,
        taps,
        groups,
        filter_count,
        block_len,
        1,
    )
    short_all = short_rows.reshape(ctx_count, shard_len)[:, : tap_count * per_dev]
    short_all = short_all.reshape(ctx_count, tap_count, per_dev)
    grad_short_out = short_all.transpose(1, 0, 2).reshape(tap_count, filter_count, chan_count)
    return (grad_in_out, grad_long_out, grad_short_out)


def solution(mesh):
    in_specs = (P(None, "ch", "ctx"), P(None, None, "ch"), P(None, "ctx"), P(None, "ch", "ctx"))
    out_specs = (P(None, "ch", "ctx"), P(None, "ctx"), P(None, None, "ch"))
    return jax.shard_map(
        per_device, mesh=mesh, in_specs=in_specs, out_specs=out_specs, check_vma=False
    )
```
